32 devices in a mesh: groups: 2 (over y), ctx: 4 (over z), role: 2 (over x), seq: 2 (over core).
Axes of the slice: x: 2, y: 2, z: 4, core: 2. Of those that a mesh axis runs over, the one named last changes fastest.
Arguments:
- queries: bfloat16 [32, 128, 576], P(('groups', 'role', 'seq'), 'ctx'), parts along dimension 0, may hold values from -24 to 24
- cache: bfloat16 [16, 4096, 576], P(('groups', 'role', 'seq'), 'ctx'), parts along dimension 0, may hold values from -4 to 4
- lengths: int32 [16], P(('groups', 'role', 'seq')), parts along dimension 0, may hold values from 4 to 4096, as said below
- positions: int32 [32], P(('groups', 'role', 'seq')), parts along dimension 0, may hold values from 0 to 4098, as said below
- value_up_weight: bfloat16 [128, 512, 128], P('ctx', ('role', 'seq')), may hold values from -0.25 to 0.25
- out_proj: bfloat16 [16384, 7168], P('ctx', ('role', 'seq')), may hold values from -0.046875 to 0.046875
- residual: bfloat16 [32, 7168], P('groups', ('role', 'seq')), parts along dimension 0, may hold values from -4 to 4
- norm_gain: float32 [7168], P(('role', 'seq')), may hold values from 0.5 to 1.5
- gate_weight: bfloat16 [7168, 9216], P(('role', 'seq'), 'ctx'), may hold values from -0.0625 to 0.0625
- up_weight: bfloat16 [7168, 9216], P(('role', 'seq'), 'ctx'), may hold values from -0.0625 to 0.0625
- down_weight: bfloat16 [9216, 7168], P('ctx', ('role', 'seq')), may hold values from -0.0625 to 0.0625
Outputs:
- layer_out: bfloat16 [32, 7168], P(('groups', 'ctx'), ('role', 'seq')), parts along dimension 0
The draws below stay inside these ranges and needn't reach their ends.
There are 2 independent parts, one for each index of `groups`. The reference program is written for one: setup_inputs(seed, part) draws one part's arguments, and reference() takes and returns one part's arrays. A program takes and returns all parts, laid end to end along the dimension named above; an argument that names none is the same for every part. Nothing has to cross between parts.
Inputs may be any that keep to these rules, and one draw needn't show every extreme that they name: `lengths`: every sequence has at least 4 cached positions, and in every draw some sequence has all 4096. positions[r] lies between lengths[r // 2] - 4 and lengths[r // 2] + 2.
All inputs are finite; a program needn't handle non-finite values.
Results may differ from the reference program's by a relative error of at most 0.013.
Values may be sent and summed in bfloat16 or wider, within the bound.
No kernel may reach another device: no remote copies, remote signals or barrier semaphores. Data moves between devices by JAX's collectives and lax.ppermute only.
A program may use at most 128 MiB of HBM per device.

```python
import jax
import jax.numpy as jnp
from jax import lax

D = 7168
HEADS = 128
LATENT = 512
ROPE = 64
VDIM = 128
FF = 9216
MTP = 2
CTX_DEV = 1024
SEQS = 8
ROWS = 16
CTX_LEN = 4096
N_CTX = 4


def length_table(key):
    base = jax.random.fold_in(key, 101)
    first_key, second_key = jax.random.split(base)
    spread = jax.random.randint(first_key, (SEQS,), 0, 1024)
    counts = 4 + spread * spread // 1024 * (CTX_LEN - 4) // 1024
    chosen = jax.random.randint(second_key, (), 0, SEQS)
    counts = jnp.where(jnp.arange(SEQS) == chosen, CTX_LEN, counts)
    return counts.astype(jnp.int32)


def draw_lengths(key, part):
    return length_table(key)


def draw_positions(key, part):
    counts = jnp.repeat(length_table(key), MTP)
    offsets = jax.random.randint(jax.random.fold_in(key, 102), (ROWS,), -4, 3)
    return (counts + offsets).astype(jnp.int32)


def draw_cache(key, part):
    value_vectors = jax.random.truncated_normal(jax.random.fold_in(key, 202), -4.0, 4.0, (SEQS, CTX_LEN, LATENT + ROPE), jnp.float32)
    return value_vectors.astype(jnp.bfloat16)


def draw_queries(key, part):
    value_vectors = jax.random.truncated_normal(jax.random.fold_in(key, 204), -4.0, 4.0, (ROWS, HEADS, LATENT + ROPE), jnp.float32)
    return value_vectors.astype(jnp.bfloat16)


def levels(own_key, shape, cuts, smallest, top_value):
    loudness = 1.0
    for position, blocks in cuts:
        heights = jax.random.uniform(jax.random.fold_in(jax.random.fold_in(own_key, 6), position), (blocks,), jnp.float32, smallest / len(cuts), top_value / len(cuts))
        loudness = loudness * jnp.repeat(jnp.exp(heights), shape[position] // blocks).reshape((-1,) + (1,) * (len(shape) - 1 - position))
    return loudness


def normal_values(key, dims, scale, limit, cuts=(), held_as=jnp.bfloat16):
    entries = jax.random.normal(key, dims, jnp.float32) * scale
    if len(cuts) > 0:
        entries = levels(key, dims, cuts, -0.22, 0.18) * entries
    return jnp.clip(entries, min=-limit, max=limit).astype(held_as)


def setup_inputs(seed: int = 0, part: int = 0) -> dict:
    keys = jax.random.split(jax.random.key(seed), 12)
    part_keys = jax.random.split(jax.random.fold_in(keys[11], part), 12)
    return {
        "queries": draw_queries(jax.random.fold_in(jax.random.fold_in(keys[11], part), 71), part),
        "cache": draw_cache(jax.random.fold_in(jax.random.fold_in(keys[11], part), 71), part),
        "lengths": draw_lengths(jax.random.fold_in(jax.random.fold_in(keys[11], part), 71), part),
        "positions": draw_positions(jax.random.fold_in(jax.random.fold_in(keys[11], part), 71), part),
        "value_up_weight": normal_values(keys[4], (HEADS, LATENT, VDIM), LATENT ** -0.5, 0.25, ((0, 4), (1, 4))),
        "out_proj": normal_values(keys[5], (HEADS * VDIM, D), (HEADS * VDIM) ** -0.5, 0.046875, ((0, 4), (1, 4))),
        "residual": normal_values(part_keys[6], (ROWS, D), 0.25, 4.0, ((1, 4),)),
        "norm_gain": jnp.clip(1.0 + 0.1 * jax.random.normal(keys[7], (D,), jnp.float32), 0.5, 1.5),
        "gate_weight": normal_values(keys[8], (D, FF), D ** -0.5, 0.0625, ((0, 4), (1, 4))),
        "up_weight": normal_values(keys[9], (D, FF), D ** -0.5, 0.0625, ((0, 4), (1, 4))),
        "down_weight": normal_values(keys[10], (FF, D), FF ** -0.5, 0.0625, ((0, 4), (1, 4))),
    }


softmax_scale = 0.07216878364870323
epsilon = 1e-06

def attend_single_sequence(packed):
    rows_pair, keys_all, length, spots = packed
    width = LATENT + ROPE
    flat_rows = rows_pair.reshape(MTP * HEADS, width)
    scores = jnp.dot(flat_rows, keys_all.T, preferred_element_type=jnp.float32) * softmax_scale
    places = jnp.arange(CTX_LEN, dtype=jnp.int32)
    limits = jnp.repeat(spots, HEADS)
    live = (places[None, :] < length) & (places[None, :] <= limits[:, None])
    scores = scores.reshape(MTP * HEADS, N_CTX, CTX_DEV)
    live = live.reshape(MTP * HEADS, N_CTX, CTX_DEV)
    block_max = lax.optimization_barrier(jnp.max(jnp.where(live, scores, jnp.float32(-1e+30)), axis=-1))
    probs = jnp.exp(jnp.where(live, scores - block_max[..., None], jnp.float32(-1e+30))).astype(jnp.bfloat16)
    block_weight_sum = lax.optimization_barrier(jnp.sum(probs.astype(jnp.float32), axis=-1))
    latents = keys_all[:, :LATENT].reshape(N_CTX, CTX_DEV, LATENT)
    block_out = jnp.einsum('hbj,bjd->hbd', probs.astype(jnp.float32), latents.astype(jnp.float32))
    highest = lax.optimization_barrier(jnp.max(block_max, axis=-1))
    factor = jnp.exp(block_max - highest[:, None])
    numer = lax.optimization_barrier(jnp.sum(factor[..., None] * block_out, axis=1))
    denom = lax.optimization_barrier(jnp.sum(factor * block_weight_sum, axis=1))
    return (numer / denom[:, None]).reshape(MTP, HEADS, LATENT)

def reference(queries, cache, lengths, positions, value_up_weight, out_proj, residual, norm_gain, gate_weight, up_weight, down_weight):
    grouped = queries.reshape(SEQS, MTP, HEADS, LATENT + ROPE)
    spots = positions.reshape(SEQS, MTP)
    attended_values = lax.map(attend_single_sequence, (grouped, cache, lengths, spots))
    attended_values = attended_values.reshape(ROWS, HEADS, LATENT).astype(jnp.bfloat16)
    value_vectors = jnp.einsum('nut,utc->nuc', attended_values.astype(jnp.float32), value_up_weight.astype(jnp.float32))
    value_vectors = value_vectors.astype(jnp.bfloat16).reshape(ROWS, HEADS * VDIM)
    attn_out = jnp.dot(value_vectors, out_proj, preferred_element_type=jnp.float32)
    resid = residual.astype(jnp.float32) + attn_out
    sumsq = lax.optimization_barrier(jnp.sum(resid * resid, axis=1))
    normed = (resid * lax.rsqrt(sumsq / D + epsilon)[:, None] * norm_gain[None, :]).astype(jnp.bfloat16)
    gate = jnp.dot(normed, gate_weight, preferred_element_type=jnp.float32)
    up = jnp.dot(normed, up_weight, preferred_element_type=jnp.float32)
    hidden = (jax.nn.silu(gate) * up).astype(jnp.bfloat16)
    return (resid + jnp.dot(hidden, down_weight, preferred_element_type=jnp.float32)).astype(jnp.bfloat16)
```

```python
import functools

import jax
import jax.numpy as jnp
from jax import lax
from jax.experimental import pallas as pl
from jax.experimental.pallas import tpu as pltpu
from jax.sharding import PartitionSpec as P

LATENT = 512
MTP = 2
SCALE = 0.07216878364870323
EPSILON = 1e-06
DEAD = -1e30
STAT_ROWS = 16
LANES = 128


f32, bf16 = jnp.float32, jnp.bfloat16
IN_VMEM = pl.BlockSpec(memory_space=pltpu.VMEM)
IN_SMEM = pl.BlockSpec(memory_space=pltpu.SMEM)
IN_HBM = pl.BlockSpec(memory_space=pltpu.HBM)


def xor_permute(x, axis, mask):
    size = lax.axis_size(axis)
    return lax.ppermute(x, axis, [(i, i ^ mask) for i in range(size)])


def exchange(pieces, axis):
    got = {0: pieces[0]}
    for mask in reversed(range(1, len(pieces))):
        got[mask] = xor_permute(pieces[mask], axis, mask)
    return [got[mask] for mask in range(len(pieces))]


def call(body, outs, args, specs, scratch=(), limit=8 << 20, cost=None, name=None):
    flops, moved = cost or (0, 0)
    return pl.pallas_call(
        body,
        out_shape=outs,
        in_specs=specs,
        out_specs=jax.tree.map(lambda _: IN_VMEM, outs),
        scratch_shapes=list(scratch),
        compiler_params=pltpu.CompilerParams(vmem_limit_bytes=limit),
        cost_estimate=pl.CostEstimate(flops=flops, bytes_accessed=moved, transcendentals=0),
        name=name,
    )(*args)


def in_vmem(x):
    return pltpu.with_memory_space_constraint(x, pltpu.VMEM)


def three_parts(x):
    high = x.astype(bf16)
    rest = x - high.astype(f32)
    middle = rest.astype(bf16)
    return high, middle, (rest - middle.astype(f32)).astype(bf16)


def prefetch(weights):
    count = len(weights)

    def body(*refs):
        sources, targets, done = refs[:count], refs[count : 2 * count], refs[2 * count]
        copies = [
            pltpu.make_async_copy(source, target, done.at[i])
            for i, (source, target) in enumerate(zip(sources, targets))
        ]
        for copy in copies:
            copy.start()
        for copy in copies:
            copy.wait()

    moved = sum(2 * w.size * w.dtype.itemsize for w in weights)
    return call(
        body,
        [pltpu.VMEM(w.shape, w.dtype) for w in weights],
        weights,
        [IN_HBM] * count,
        [pltpu.SemaphoreType.DMA((count,))],
        limit=1 << 20,
        cost=(0, moved),
        name="fetch",
    )


def attend(groups, cache, lengths, positions):
    count = len(groups)
    rows, heads, width = groups[0].shape
    seqs, context, _ = cache.shape
    per_seq = MTP * heads
    per_group = rows * heads

    def body(*refs):
        query_refs = refs[:count]
        cache_ref, length_ref, position_ref = refs[count : count + 3]
        out_refs = refs[count + 3 :]
        offset = lax.axis_index("ctx") * context
        total = count * per_seq
        tops, sums = [[] for _ in range(count)], [[] for _ in range(count)]
        for n in range(seqs):
            queries = jnp.concatenate(
                [q[MTP * n : MTP * (n + 1)].reshape(per_seq, width) for q in query_refs], axis=0
            )
            keys = cache_ref[n]
            scores = lax.dot_general(
                queries, keys, (((1,), (1,)), ((), ())), preferred_element_type=f32
            ) * SCALE
            row = lax.broadcasted_iota(jnp.int32, (total, 1), 0)
            which = (row // heads) % MTP
            limit = jnp.full((total, 1), 0, jnp.int32)
            for t in range(MTP):
                bound = jnp.minimum(length_ref[n], position_ref[MTP * n + t] + 1)
                limit = jnp.where(which == t, bound, limit)
            place = offset + lax.broadcasted_iota(jnp.int32, (total, context), 1)
            live = place < limit
            top = jnp.max(jnp.where(live, scores, DEAD), axis=1, keepdims=True)
            probs = jnp.exp(jnp.where(live, scores - top, DEAD)).astype(bf16)
            weight = jnp.sum(probs.astype(f32), axis=1, keepdims=True)
            out = jnp.dot(probs, cache_ref[n, :, :LATENT], preferred_element_type=f32)
            for g in range(count):
                part = slice(g * per_seq, (g + 1) * per_seq)
                out_refs[g][n * per_seq : (n + 1) * per_seq, :] = out[part].astype(bf16)
                tops[g].append(top[part])
                sums[g].append(weight[part])
        lane = lax.broadcasted_iota(jnp.int32, (LANES, LANES), 1)
        for g in range(count):
            fill = [jnp.zeros((LANES - per_group, 1), f32)] if per_group < LANES else []
            top = jnp.concatenate(tops[g] + fill, axis=0)
            weight = jnp.concatenate(sums[g] + fill, axis=0)
            table = jnp.where(lane == 0, top, jnp.where(lane == 1, weight, 0.0)).T
            for i, part in enumerate(three_parts(table[:STAT_ROWS])):
                out_refs[g][per_group:, i * LANES : (i + 1) * LANES] = part
            out_refs[g][per_group:, 3 * LANES :] = jnp.zeros((STAT_ROWS, LATENT - 3 * LANES), bf16)

    shape = jax.ShapeDtypeStruct((per_group + STAT_ROWS, LATENT), bf16)
    flops = 2 * count * rows * heads * context * (width + LATENT)
    return call(
        body,
        [shape] * count,
        [*groups, cache, lengths, positions],
        [IN_VMEM] * count + [IN_VMEM, IN_SMEM, IN_SMEM],
        limit=12 << 20,
        cost=(flops, 4 << 20),
        name="attend",
    )


def join_and_project(parts, pieces, rows, heads):
    count, slices = len(parts), len(pieces)
    per_group = rows * heads
    _, depth, vdim = pieces[0].shape

    def body(*refs):
        part_refs, piece_refs = refs[:count], refs[count : count + slices]
        value_ref, attended = refs[count + slices :]
        me = lax.axis_index(("role", "seq"))
        tops, sums = [], []
        for ref in part_refs:
            table = sum(
                ref[per_group:, i * LANES : (i + 1) * LANES].astype(f32) for i in reversed(range(3))
            )
            table = jnp.concatenate([table, jnp.zeros((LANES - STAT_ROWS, LANES), f32)], axis=0).T
            tops.append(table[:per_group, 0:1])
            sums.append(table[:per_group, 1:2])
        highest = functools.reduce(jnp.maximum, tops)
        factors = [jnp.exp(top - highest) for top in tops]
        denom = sum(f * s for f, s in zip(factors, sums))
        numer = sum(f * ref[:per_group, :].astype(f32) for f, ref in zip(factors, part_refs))
        joined = (numer / denom).astype(bf16).astype(f32)
        for k in range(slices):
            attended[k] = joined[:, k * depth : (k + 1) * depth]
        for h in range(heads):
            total = None
            for m in range(slices):
                left = attended[me ^ m, pl.ds(h, rows, stride=heads), :].astype(bf16)
                term = jnp.dot(left, piece_refs[m][h], preferred_element_type=f32)
                total = term if total is None else total + term
            value_ref[:, h * vdim : (h + 1) * vdim] = total.astype(bf16)

    return call(
        body,
        jax.ShapeDtypeStruct((rows, heads * vdim), bf16),
        [*parts, *pieces],
        [IN_VMEM] * (count + slices),
        [pltpu.VMEM((slices, per_group, depth), f32)],
        cost=(2 * rows * heads * LATENT * vdim, 4 << 20),
        name="join",
    )


def project_out(pieces, weight):
    count = len(pieces)
    rows, depth = pieces[0].shape
    width = weight.shape[1]

    def body(*refs):
        weight_ref, out_ref, placed = refs[count:]
        me = lax.axis_index(("role", "seq"))
        for m in range(count):
            placed[me ^ m] = refs[m][...].astype(f32)
        values = jnp.concatenate([placed[k] for k in range(count)], axis=0).astype(bf16)
        out_ref[...] = jnp.dot(values, weight_ref[...], preferred_element_type=f32).astype(bf16)

    return call(
        body,
        jax.ShapeDtypeStruct((count * rows, width), bf16),
        [*pieces, in_vmem(weight)],
        [IN_VMEM] * (count + 1),
        [pltpu.VMEM((count, rows, depth), f32)],
        cost=(2 * count * rows * depth * width, 4 << 20),
        name="project",
    )


def gate_and_up(pieces, residual, gain, gate_weight, up_weight):
    count = len(pieces)
    rows, width = residual.shape
    hidden = gate_weight.shape[1]
    cores = lax.axis_size("seq")
    half = hidden // cores
    own_rows = rows // count

    def body(*refs):
        residual_ref, gain_ref, gate_ref, up_ref, keep_ref, send_ref, base_ref, split, placed = refs[count:]
        resid = residual_ref[...].astype(f32) + sum(ref[...].astype(f32) for ref in refs[:count])
        for k in range(count):
            placed[k] = resid[k * own_rows : (k + 1) * own_rows]
        base_ref[...] = placed[lax.axis_index("ctx")]
        squares = jnp.sum(resid * resid, axis=1, keepdims=True)
        scaled = (resid * gain_ref[...]).astype(bf16)
        gate = jnp.dot(scaled, gate_ref[...], preferred_element_type=f32)
        up = jnp.dot(scaled, up_ref[...], preferred_element_type=f32)
        for k in range(cores):
            split[k, :, :half] = gate[:, k * half : (k + 1) * half]
            split[k, :, half:] = up[:, k * half : (k + 1) * half]
        me = lax.axis_index("seq")
        keep_ref[:, : 2 * half] = split[me]
        send_ref[:, : 2 * half] = split[me ^ 1].astype(bf16)
        keep_ref[:, 2 * half :] = jnp.broadcast_to(squares, (rows, LANES))
        lane = lax.broadcasted_iota(jnp.int32, (rows, LANES), 1)
        send_ref[:, 2 * half :] = spread(squares, lane)

    shape = (rows, 2 * half + LANES)
    return call(
        body,
        [
            jax.ShapeDtypeStruct(shape, f32),
            jax.ShapeDtypeStruct(shape, bf16),
            jax.ShapeDtypeStruct((own_rows, width), f32),
        ],
        [*pieces, residual, gain.reshape(1, width), in_vmem(gate_weight), in_vmem(up_weight)],
        [IN_VMEM] * (count + 4),
        [pltpu.VMEM((cores, rows, 2 * half), f32), pltpu.VMEM((count, own_rows, width), f32)],
        cost=(4 * rows * width * hidden, 4 << 20),
        name="gate",
    )


def spread(column, lane):
    high, middle, low = three_parts(column)
    return jnp.where(
        lane == 0,
        high.astype(f32),
        jnp.where(lane == 1, middle.astype(f32), jnp.where(lane == 2, low.astype(f32), 0.0)),
    ).astype(bf16)


def add_core(keep, got):
    rows, width = keep.shape
    body_width = width - LANES

    def body(keep_ref, got_ref, sum_ref, send_ref):
        total = keep_ref[:, :body_width] + got_ref[:, :body_width].astype(f32)
        squares = keep_ref[:, body_width : body_width + 1] + jnp.sum(
            got_ref[:, body_width:].astype(f32), axis=1, keepdims=True
        )
        sum_ref[:, :body_width] = total
        sum_ref[:, body_width:] = jnp.broadcast_to(squares, (rows, LANES))
        send_ref[:, :body_width] = total.astype(bf16)
        lane = lax.broadcasted_iota(jnp.int32, (rows, LANES), 1)
        send_ref[:, body_width:] = spread(squares, lane)

    return call(
        body,
        [jax.ShapeDtypeStruct((rows, width), f32), jax.ShapeDtypeStruct((rows, width), bf16)],
        [keep, got],
        [IN_VMEM] * 2,
        cost=(rows * width, rows * width * 8),
        name="pair",
    )


def activate(keep, pieces, features):
    rows, width = keep.shape
    body_width = width - LANES
    half = body_width // 2

    def body(*refs):
        keep_ref, out_ref = refs[0], refs[-1]
        total = keep_ref[:, :body_width] + sum(r[:, :body_width].astype(f32) for r in refs[1:-1])
        squares = keep_ref[:, body_width : body_width + 1] + sum(
            jnp.sum(r[:, body_width:].astype(f32), axis=1, keepdims=True) for r in refs[1:-1]
        )
        scale = lax.rsqrt(squares / features + EPSILON)
        gate = total[:, :half] * scale
        up = total[:, half:] * scale
        out_ref[...] = (gate / (1.0 + jnp.exp(-gate)) * up).astype(bf16)

    return call(
        body,
        jax.ShapeDtypeStruct((rows, half), bf16),
        [keep, *pieces],
        [IN_VMEM] * (1 + len(pieces)),
        cost=(rows * width, rows * width * 8),
        name="activate",
    )


def project_down(own, other, weight):
    rows, half = own.shape
    width = weight.shape[1]
    count = lax.axis_size("ctx")
    own_rows = rows // count

    def body(own_ref, other_ref, weight_ref, *refs):
        out_refs, (joined, placed) = refs[:count], refs[count:]
        core = lax.axis_index("seq")
        joined[core] = own_ref[...]
        joined[core ^ 1] = other_ref[...]
        hidden = jnp.concatenate([joined[0], joined[1]], axis=1)
        out = jnp.dot(hidden, weight_ref[...], preferred_element_type=f32)
        for k in range(count):
            placed[k] = out[k * own_rows : (k + 1) * own_rows]
        me = lax.axis_index("ctx")
        for m in range(count):
            out_refs[m][...] = placed[me ^ m].astype(bf16)

    return call(
        body,
        [jax.ShapeDtypeStruct((own_rows, width), bf16)] * count,
        [own, other, in_vmem(weight)],
        [IN_VMEM] * 3,
        [pltpu.VMEM((2, rows, half), bf16), pltpu.VMEM((count, own_rows, width), f32)],
        cost=(4 * rows * half * width, 4 << 20),
        name="down",
    )


def finish(base, pieces):
    def body(*refs):
        refs[-1][...] = (refs[0][...] + sum(r[...].astype(f32) for r in refs[1:-1])).astype(bf16)

    return call(
        body,
        jax.ShapeDtypeStruct(base.shape, bf16),
        [base, *pieces],
        [IN_VMEM] * (1 + len(pieces)),
        cost=(base.size, base.size * 8),
        name="finish",
    )


def per_device(
    queries,
    cache,
    lengths,
    positions,
    value_up_weight,
    out_proj,
    residual,
    norm_gain,
    gate_weight,
    up_weight,
    down_weight,
):
    rows, heads, _ = queries.shape
    blocks = lax.axis_size("ctx")
    roles = lax.axis_size("role")
    members = lax.axis_size(("role", "seq"))

    groups = exchange([queries] * blocks, "ctx")
    along = exchange([value_up_weight] * roles, "role")
    across = [xor_permute(piece, "seq", 1) for piece in along]
    up_pieces = [piece for pair in zip(along, across) for piece in pair]

    out_fast, gate_fast, up_fast, down_fast = prefetch([out_proj, gate_weight, up_weight, down_weight])

    partial = attend(groups, cache, lengths, positions)
    parts = exchange(partial, "ctx")
    values = join_and_project(parts, up_pieces, rows, heads)
    shared = exchange([values] * members, ("role", "seq"))
    terms = exchange([project_out(shared, out_fast)] * blocks, "ctx")
    keep, send, base = gate_and_up(terms, residual, norm_gain, gate_fast, up_fast)
    keep, send = add_core(keep, xor_permute(send, "seq", 1))
    pieces = exchange([send] * roles, "role")[1:]
    features = norm_gain.shape[0] * members
    hidden = activate(keep, pieces, features)
    last = project_down(hidden, xor_permute(hidden, "seq", 1), down_fast)
    last = exchange(last, "ctx")
    return finish(base, last)


def solution(mesh):
    placed = (
        P(("groups", "role", "seq"), "ctx", None),
        P(("groups", "role", "seq"), "ctx", None),
        P(("groups", "role", "seq")),
        P(("groups", "role", "seq")),
        P("ctx", ("role", "seq"), None),
        P("ctx", ("role", "seq")),
        P("groups", ("role", "seq")),
        P(("role", "seq")),
        P(("role", "seq"), "ctx"),
        P(("role", "seq"), "ctx"),
        P("ctx", ("role", "seq")),
    )
    return jax.shard_map(
        per_device,
        mesh=mesh,
        in_specs=placed,
        out_specs=P(("groups", "ctx"), ("role", "seq")),
        check_vma=False,
    )
```

```python
import functools

import jax
import jax.numpy as jnp
from jax import lax
from jax.experimental import pallas as pl
from jax.experimental.pallas import tpu as pltpu
from jax.sharding import PartitionSpec as P


LATENT = 512
MTP = 2
SCALE = 0.07216878364870323
EPSILON = 1e-06
DEAD = -1e30
STAT_ROWS = 16
LANES = 128
ATTEND_LIMIT = 8 << 20
KERNEL_LIMIT = 3 << 20


f32, bf16 = jnp.float32, jnp.bfloat16
IN_VMEM = pl.BlockSpec(memory_space=pltpu.VMEM)
IN_SMEM = pl.BlockSpec(memory_space=pltpu.SMEM)
IN_HBM = pl.BlockSpec(memory_space=pltpu.HBM)


def xor_permute(x, axis, mask):
    size = lax.axis_size(axis)
    return lax.ppermute(x, axis, [(i, i ^ mask) for i in range(size)])


def exchange(pieces, axis):
    got = {0: pieces[0]}
    for mask in reversed(range(1, len(pieces))):
        got[mask] = xor_permute(pieces[mask], axis, mask)
    return [got[mask] for mask in range(len(pieces))]


def call(body, outs, args, specs, scratch=(), limit=KERNEL_LIMIT, cost=None):
    flops, moved = cost or (0, 0)
    return pl.pallas_call(
        body,
        out_shape=outs,
        in_specs=specs,
        out_specs=jax.tree.map(lambda _: IN_VMEM, outs),
        scratch_shapes=list(scratch),
        compiler_params=pltpu.CompilerParams(vmem_limit_bytes=limit),
        cost_estimate=pl.CostEstimate(flops=flops, bytes_accessed=moved, transcendentals=0),
    )(*args)


def in_vmem(x):
    return pltpu.with_memory_space_constraint(x, pltpu.VMEM)


def three_parts(x):
    high = x.astype(bf16)
    rest = x - high.astype(f32)
    middle = rest.astype(bf16)
    return high, middle, (rest - middle.astype(f32)).astype(bf16)


def fetch(arrays, lengths=None, positions=None):
    count = len(arrays)
    tables = 0 if positions is None else 1
    rows = positions.shape[0] if tables else 0

    def body(*refs):
        sources, refs = refs[:count], refs[count:]
        scalars, refs = refs[: 2 * tables], refs[2 * tables :]
        targets, refs = refs[:count], refs[count:]
        done = refs[-1]
        copies = [
            pltpu.make_async_copy(source, target, done.at[i])
            for i, (source, target) in enumerate(zip(sources, targets))
        ]
        for copy in copies:
            copy.start()
        if tables:
            length_ref, position_ref = scalars
            row = lax.broadcasted_iota(jnp.int32, (rows, LANES), 0)
            seen = jnp.zeros((rows, LANES), jnp.int32)
            for r in range(rows):
                bound = jnp.minimum(length_ref[r // MTP], position_ref[r] + 1)
                seen = jnp.where(row == r, bound, seen)
            refs[0][...] = seen
        for copy in copies:
            copy.wait()

    moved = sum(2 * x.size * x.dtype.itemsize for x in arrays)
    return call(
        body,
        [pltpu.VMEM(x.shape, x.dtype) for x in arrays]
        + [pltpu.VMEM((rows, LANES), jnp.int32)] * tables,
        [pltpu.with_memory_space_constraint(x, pltpu.HBM) for x in arrays]
        + [lengths, positions] * tables,
        [IN_HBM] * count + [IN_SMEM] * (2 * tables),
        [pltpu.SemaphoreType.DMA((count,))],
        limit=1 << 20,
        cost=(0, moved),
    )


def attend(groups, cache, seen):
    count = len(groups)
    rows, heads, width = groups[0].shape
    seqs, _, context = cache.shape
    per_seq = MTP * heads
    per_group = rows * heads

    def body(*refs):
        query_refs = refs[:count]
        cache_ref, seen_ref = refs[count : count + 2]
        out_refs = refs[count + 2 :]
        offset = lax.axis_index("ctx") * context
        total = count * per_seq
        tops, sums = [[] for _ in range(count)], [[] for _ in range(count)]
        for n in range(seqs):
            queries = jnp.concatenate(
                [q[MTP * n : MTP * (n + 1)].reshape(per_seq, width) for q in query_refs], axis=0
            )
            scores = jnp.dot(queries, cache_ref[n], preferred_element_type=f32) * SCALE
            row = lax.broadcasted_iota(jnp.int32, (total, 1), 0)
            which = (row // heads) % MTP
            limit = jnp.full((total, 1), 0, jnp.int32)
            for t in range(MTP):
                r = MTP * n + t
                limit = jnp.where(which == t, seen_ref[r : r + 1, 0:1], limit)
            place = offset + lax.broadcasted_iota(jnp.int32, (total, context), 1)
            live = place < limit
            top = jnp.max(jnp.where(live, scores, DEAD), axis=1, keepdims=True)
            probs = jnp.exp(jnp.where(live, scores - top, DEAD)).astype(bf16)
            weight = jnp.sum(probs.astype(f32), axis=1, keepdims=True)
            out = lax.dot_general(
                probs, cache_ref[n, :LATENT, :], (((1,), (1,)), ((), ())), preferred_element_type=f32
            )
            for g in range(count):
                part = slice(g * per_seq, (g + 1) * per_seq)
                out_refs[g][n * per_seq : (n + 1) * per_seq, :] = out[part].astype(bf16)
                tops[g].append(top[part])
                sums[g].append(weight[part])
        lane = lax.broadcasted_iota(jnp.int32, (LANES, LANES), 1)
        for g in range(count):
            fill = [jnp.zeros((LANES - per_group, 1), f32)] if per_group < LANES else []
            top = jnp.concatenate(tops[g] + fill, axis=0)
            weight = jnp.concatenate(sums[g] + fill, axis=0)
            table = jnp.where(lane == 0, top, jnp.where(lane == 1, weight, 0.0)).T
            for i, part in enumerate(three_parts(table[:STAT_ROWS])):
                out_refs[g][per_group:, i * LANES : (i + 1) * LANES] = part
            out_refs[g][per_group:, 3 * LANES :] = jnp.zeros((STAT_ROWS, LATENT - 3 * LANES), bf16)

    shape = jax.ShapeDtypeStruct((per_group + STAT_ROWS, LATENT), bf16)
    flops = 2 * count * rows * heads * context * (width + LATENT)
    return call(
        body,
        [shape] * count,
        [*groups, in_vmem(cache), seen],
        [IN_VMEM] * (count + 2),
        limit=ATTEND_LIMIT,
        cost=(flops, 4 << 20),
    )


def join_and_project(parts, pieces, rows, heads, after):
    count, slices = len(parts), len(pieces)
    per_group = rows * heads
    _, depth, vdim = pieces[0].shape

    def body(*refs):
        part_refs, piece_refs = refs[:count], refs[count : count + slices]
        value_ref, attended = refs[count + slices + 1 :]
        me = lax.axis_index(("role", "seq"))
        tops, sums = [], []
        for ref in part_refs:
            table = sum(
                ref[per_group:, i * LANES : (i + 1) * LANES].astype(f32) for i in reversed(range(3))
            )
            table = jnp.concatenate([table, jnp.zeros((LANES - STAT_ROWS, LANES), f32)], axis=0).T
            tops.append(table[:per_group, 0:1])
            sums.append(table[:per_group, 1:2])
        highest = functools.reduce(jnp.maximum, tops)
        factors = [jnp.exp(top - highest) for top in tops]
        denom = sum(f * s for f, s in zip(factors, sums))
        numer = sum(f * ref[:per_group, :].astype(f32) for f, ref in zip(factors, part_refs))
        joined = (numer / denom).astype(bf16).astype(f32)
        for k in range(slices):
            attended[k] = joined[:, k * depth : (k + 1) * depth]
        for h in range(heads):
            total = None
            for m in range(slices):
                left = attended[me ^ m, pl.ds(h, rows, stride=heads), :].astype(bf16)
                term = jnp.dot(left, piece_refs[m][h], preferred_element_type=f32)
                total = term if total is None else total + term
            value_ref[:, h * vdim : (h + 1) * vdim] = total.astype(bf16)

    return call(
        body,
        jax.ShapeDtypeStruct((rows, heads * vdim), bf16),
        [*parts, *[in_vmem(piece) for piece in pieces], after],
        [IN_VMEM] * (count + slices + 1),
        [pltpu.VMEM((slices, per_group, depth), f32)],
        cost=(2 * rows * heads * LATENT * vdim, 4 << 20),
    )


def project_out(pieces, weight):
    count = len(pieces)
    rows, depth = pieces[0].shape
    width = weight.shape[1]

    def body(*refs):
        weight_ref, out_ref, placed = refs[count:]
        me = lax.axis_index(("role", "seq"))
        for m in range(count):
            placed[me ^ m] = refs[m][...].astype(f32)
        values = jnp.concatenate([placed[k] for k in range(count)], axis=0).astype(bf16)
        out_ref[...] = jnp.dot(values, weight_ref[...], preferred_element_type=f32).astype(bf16)

    return call(
        body,
        jax.ShapeDtypeStruct((count * rows, width), bf16),
        [*pieces, in_vmem(weight)],
        [IN_VMEM] * (count + 1),
        [pltpu.VMEM((count, rows, depth), f32)],
        cost=(2 * count * rows * depth * width, 4 << 20),
    )


def gate_and_up(pieces, residual, gain, gate_weight, up_weight):
    count = len(pieces)
    rows, width = residual.shape
    hidden = gate_weight.shape[1]
    cores = lax.axis_size("seq")
    half = hidden // cores
    own_rows = rows // count

    def body(*refs):
        residual_ref, gain_ref, gate_ref, up_ref, keep_ref, send_ref, base_ref, split, placed = refs[count:]
        resid = residual_ref[...].astype(f32) + sum(ref[...].astype(f32) for ref in refs[:count])
        for k in range(count):
            placed[k] = resid[k * own_rows : (k + 1) * own_rows]
        base_ref[...] = placed[lax.axis_index("ctx")]
        squares = jnp.sum(resid * resid, axis=1, keepdims=True)
        scaled = (resid * gain_ref[...]).astype(bf16)
        gate = jnp.dot(scaled, gate_ref[...], preferred_element_type=f32)
        up = jnp.dot(scaled, up_ref[...], preferred_element_type=f32)
        for k in range(cores):
            split[k, :, :half] = gate[:, k * half : (k + 1) * half]
            split[k, :, half:] = up[:, k * half : (k + 1) * half]
        me = lax.axis_index("seq")
        keep_ref[:, : 2 * half] = split[me]
        send_ref[:, : 2 * half] = split[me ^ 1].astype(bf16)
        keep_ref[:, 2 * half :] = jnp.broadcast_to(squares, (rows, LANES))
        lane = lax.broadcasted_iota(jnp.int32, (rows, LANES), 1)
        send_ref[:, 2 * half :] = spread(squares, lane)

    shape = (rows, 2 * half + LANES)
    return call(
        body,
        [
            jax.ShapeDtypeStruct(shape, f32),
            jax.ShapeDtypeStruct(shape, bf16),
            jax.ShapeDtypeStruct((own_rows, width), f32),
        ],
        [*pieces, residual, gain, in_vmem(gate_weight), in_vmem(up_weight)],
        [IN_VMEM] * (count + 4),
        [pltpu.VMEM((cores, rows, 2 * half), f32), pltpu.VMEM((count, own_rows, width), f32)],
        cost=(4 * rows * width * hidden, 4 << 20),
    )


def spread(column, lane):
    high, middle, low = three_parts(column)
    return jnp.where(
        lane == 0,
        high.astype(f32),
        jnp.where(lane == 1, middle.astype(f32), jnp.where(lane == 2, low.astype(f32), 0.0)),
    ).astype(bf16)


def add_core(keep, got):
    rows, width = keep.shape
    body_width = width - LANES

    def body(keep_ref, got_ref, sum_ref, send_ref):
        total = keep_ref[:, :body_width] + got_ref[:, :body_width].astype(f32)
        squares = keep_ref[:, body_width : body_width + 1] + jnp.sum(
            got_ref[:, body_width:].astype(f32), axis=1, keepdims=True
        )
        sum_ref[:, :body_width] = total
        sum_ref[:, body_width:] = jnp.broadcast_to(squares, (rows, LANES))
        send_ref[:, :body_width] = total.astype(bf16)
        lane = lax.broadcasted_iota(jnp.int32, (rows, LANES), 1)
        send_ref[:, body_width:] = spread(squares, lane)

    return call(
        body,
        [jax.ShapeDtypeStruct((rows, width), f32), jax.ShapeDtypeStruct((rows, width), bf16)],
        [keep, got],
        [IN_VMEM] * 2,
        cost=(rows * width, rows * width * 8),
    )


def activate(keep, pieces, features):
    rows, width = keep.shape
    body_width = width - LANES
    half = body_width // 2

    def body(*refs):
        keep_ref, out_ref = refs[0], refs[-1]
        total = keep_ref[:, :body_width] + sum(r[:, :body_width].astype(f32) for r in refs[1:-1])
        squares = keep_ref[:, body_width : body_width + 1] + sum(
            jnp.sum(r[:, body_width:].astype(f32), axis=1, keepdims=True) for r in refs[1:-1]
        )
        scale = lax.rsqrt(squares / features + EPSILON)
        gate = total[:, :half] * scale
        up = total[:, half:] * scale
        out_ref[...] = (gate / (1.0 + jnp.exp(-gate)) * up).astype(bf16)

    return call(
        body,
        jax.ShapeDtypeStruct((rows, half), bf16),
        [keep, *pieces],
        [IN_VMEM] * (1 + len(pieces)),
        cost=(rows * width, rows * width * 8),
    )


def project_down(own, other, weight):
    rows, half = own.shape
    width = weight.shape[1]
    count = lax.axis_size("ctx")
    own_rows = rows // count

    def body(own_ref, other_ref, weight_ref, *refs):
        out_refs, (joined, placed) = refs[:count], refs[count:]
        core = lax.axis_index("seq")
        joined[core] = own_ref[...]
        joined[core ^ 1] = other_ref[...]
        hidden = jnp.concatenate([joined[0], joined[1]], axis=1)
        out = jnp.dot(hidden, weight_ref[...], preferred_element_type=f32)
        for k in range(count):
            placed[k] = out[k * own_rows : (k + 1) * own_rows]
        me = lax.axis_index("ctx")
        for m in range(count):
            out_refs[m][...] = placed[me ^ m].astype(bf16)

    return call(
        body,
        [jax.ShapeDtypeStruct((own_rows, width), bf16)] * count,
        [own, other, in_vmem(weight)],
        [IN_VMEM] * 3,
        [pltpu.VMEM((2, rows, half), bf16), pltpu.VMEM((count, own_rows, width), f32)],
        cost=(4 * rows * half * width, 4 << 20),
    )


def finish(base, pieces):
    def body(*refs):
        refs[-1][...] = (refs[0][...] + sum(r[...].astype(f32) for r in refs[1:-1])).astype(bf16)

    return call(
        body,
        jax.ShapeDtypeStruct(base.shape, bf16),
        [base, *pieces],
        [IN_VMEM] * (1 + len(pieces)),
        cost=(base.size, base.size * 8),
    )


def per_device(
    queries,
    cache,
    lengths,
    positions,
    value_up_weight,
    out_proj,
    residual,
    norm_gain,
    gate_weight,
    up_weight,
    down_weight,
):
    rows, heads, _ = queries.shape
    blocks = lax.axis_size("ctx")
    roles = lax.axis_size("role")
    members = lax.axis_size(("role", "seq"))

    groups = exchange([queries] * blocks, "ctx")
    along = exchange([value_up_weight] * roles, "role")

    own_queries, cache_fast, up_own, out_fast, seen = fetch(
        [queries, jnp.swapaxes(cache, 1, 2), value_up_weight, out_proj], lengths, positions
    )
    partial = list(attend([own_queries, *groups[1:]], cache_fast, seen))

    gate_weight, up_weight, down_weight, partial[0] = lax.optimization_barrier(
        (gate_weight, up_weight, down_weight, partial[0])
    )
    parts = exchange(partial, "ctx")
    gate_fast, up_fast, down_fast, residual, gain = fetch(
        [gate_weight, up_weight, down_weight, residual, norm_gain.reshape(1, -1)]
    )
    *along, gain = lax.optimization_barrier((*along, gain))
    across = [xor_permute(piece, "seq", 1) for piece in along]
    up_pieces = [up_own, *[piece for pair in zip(along, across) for piece in pair][1:]]
    values = join_and_project(parts, up_pieces, rows, heads, gain)
    shared = exchange([values] * members, ("role", "seq"))
    terms = exchange([project_out(shared, out_fast)] * blocks, "ctx")
    keep, send, base = gate_and_up(terms, residual, gain, gate_fast, up_fast)
    keep, send = add_core(keep, xor_permute(send, "seq", 1))
    pieces = exchange([send] * roles, "role")[1:]
    features = norm_gain.shape[0] * members
    hidden = activate(keep, pieces, features)
    last = project_down(hidden, xor_permute(hidden, "seq", 1), down_fast)
    last = exchange(last, "ctx")
    return finish(base, last)


def solution(mesh):
    placed = (
        P(("groups", "role", "seq"), "ctx", None),
        P(("groups", "role", "seq"), "ctx", None),
        P(("groups", "role", "seq")),
        P(("groups", "role", "seq")),
        P("ctx", ("role", "seq"), None),
        P("ctx", ("role", "seq")),
        P("groups", ("role", "seq")),
        P(("role", "seq")),
        P(("role", "seq"), "ctx"),
        P(("role", "seq"), "ctx"),
        P("ctx", ("role", "seq")),
    )

    return jax.shard_map(
        per_device,
        mesh=mesh,
        in_specs=placed,
        out_specs=P(("groups", "ctx"), ("role", "seq")),
        check_vma=False,
    )
```

```python
import functools

import jax
import jax.numpy as jnp
from jax import lax
from jax.experimental import pallas as pl
from jax.experimental.pallas import tpu as pltpu
from jax.sharding import PartitionSpec as P


LATENT = 512
MTP = 2
SCALE = 0.07216878364870323
EPSILON = 1e-06
DEAD = -1e30
STAT_ROWS = 8
LANES = 128
ATTEND_LIMIT = 8 << 20
KERNEL_LIMIT = 6 << 20


f32, bf16 = jnp.float32, jnp.bfloat16
IN_VMEM = pl.BlockSpec(memory_space=pltpu.VMEM)
IN_SMEM = pl.BlockSpec(memory_space=pltpu.SMEM)
IN_HBM = pl.BlockSpec(memory_space=pltpu.HBM)


def xor_permute(x, axis, mask):
    size = lax.axis_size(axis)
    return lax.ppermute(x, axis, [(i, i ^ mask) for i in range(size)])


def exchange(pieces, axis, masks=None):
    got = {0: pieces[0]}
    for mask in masks or reversed(range(1, len(pieces))):
        got[mask] = xor_permute(pieces[mask], axis, mask)
    return got


def listed(got):
    return [got[mask] for mask in sorted(got)]


def call(body, outs, args, specs, scratch=(), limit=KERNEL_LIMIT, cost=None):
    flops, moved = cost or (0, 0)
    return pl.pallas_call(
        body,
        out_shape=outs,
        in_specs=specs,
        out_specs=jax.tree.map(lambda _: IN_VMEM, outs),
        scratch_shapes=list(scratch),
        compiler_params=pltpu.CompilerParams(vmem_limit_bytes=limit),
        cost_estimate=pl.CostEstimate(flops=flops, bytes_accessed=moved, transcendentals=0),
    )(*args)


def in_vmem(x):
    return pltpu.with_memory_space_constraint(x, pltpu.VMEM)


def three_parts(x):
    high = x.astype(bf16)
    rest = x - high.astype(f32)
    middle = rest.astype(bf16)
    return high, middle, (rest - middle.astype(f32)).astype(bf16)


def fetch(arrays, lengths=None, positions=None):
    count = len(arrays)
    tables = 0 if positions is None else 1
    rows = positions.shape[0] if tables else 0

    def body(*refs):
        sources, refs = refs[:count], refs[count:]
        scalars, refs = refs[: 2 * tables], refs[2 * tables :]
        targets, refs = refs[:count], refs[count:]
        done = refs[-1]
        copies = [
            pltpu.make_async_copy(source, target, done.at[i])
            for i, (source, target) in enumerate(zip(sources, targets))
        ]
        for copy in copies:
            copy.start()
        if tables:
            length_ref, position_ref = scalars
            row = lax.broadcasted_iota(jnp.int32, (rows, LANES), 0)
            seen = jnp.zeros((rows, LANES), jnp.int32)
            for r in range(rows):
                bound = jnp.minimum(length_ref[r // MTP], position_ref[r] + 1)
                seen = jnp.where(row == r, bound, seen)
            refs[0][...] = seen
        for copy in copies:
            copy.wait()

    moved = sum(2 * x.size * x.dtype.itemsize for x in arrays)
    return call(
        body,
        [pltpu.VMEM(x.shape, x.dtype) for x in arrays]
        + [pltpu.VMEM((rows, LANES), jnp.int32)] * tables,
        [pltpu.with_memory_space_constraint(x, pltpu.HBM) for x in arrays]
        + [lengths, positions] * tables,
        [IN_HBM] * count + [IN_SMEM] * (2 * tables),
        [pltpu.SemaphoreType.DMA((count,))],
        limit=1 << 20,
        cost=(0, moved),
    )


def attend(groups, cache, seen):
    count = len(groups)
    rows, heads, width = groups[0].shape
    seqs, _, context = cache.shape
    per_seq = MTP * heads
    per_group = rows * heads

    def body(*refs):
        query_refs = refs[:count]
        cache_ref, seen_ref = refs[count : count + 2]
        out_refs = refs[count + 2 :]
        offset = lax.axis_index("ctx") * context
        total = count * per_seq
        tops, sums = [[] for _ in range(count)], [[] for _ in range(count)]
        for n in range(seqs):
            queries = jnp.concatenate(
                [q[MTP * n : MTP * (n + 1)].reshape(per_seq, width) for q in query_refs], axis=0
            )
            scores = jnp.dot(queries, cache_ref[n], preferred_element_type=f32) * SCALE
            row = lax.broadcasted_iota(jnp.int32, (total, 1), 0)
            which = (row // heads) % MTP
            limit = jnp.full((total, 1), 0, jnp.int32)
            for t in range(MTP):
                r = MTP * n + t
                limit = jnp.where(which == t, seen_ref[r : r + 1, 0:1], limit)
            place = offset + lax.broadcasted_iota(jnp.int32, (total, context), 1)
            live = place < limit
            top = jnp.max(jnp.where(live, scores, DEAD), axis=1, keepdims=True)
            probs = jnp.exp(jnp.where(live, scores - top, DEAD)).astype(bf16)
            weight = jnp.sum(probs.astype(f32), axis=1, keepdims=True)
            out = lax.dot_general(
                probs, cache_ref[n, :LATENT, :], (((1,), (1,)), ((), ())), preferred_element_type=f32
            )
            for g in range(count):
                part = slice(g * per_seq, (g + 1) * per_seq)
                out_refs[g][n * per_seq : (n + 1) * per_seq, :] = out[part].astype(bf16)
                tops[g].append(top[part])
                sums[g].append(weight[part])
        lane = lax.broadcasted_iota(jnp.int32, (LANES, LANES), 1)
        for g in range(count):
            fill = [jnp.zeros((LANES - per_group, 1), f32)] if per_group < LANES else []
            top = jnp.concatenate(tops[g] + fill, axis=0)
            weight = jnp.concatenate(sums[g] + fill, axis=0)
            table = jnp.where(lane == 0, top, jnp.where(lane == 1, weight, 0.0)).T
            for i, part in enumerate(three_parts(table[:STAT_ROWS])):
                out_refs[g][per_group:, i * LANES : (i + 1) * LANES] = part
            out_refs[g][per_group:, 3 * LANES :] = jnp.zeros((STAT_ROWS, LATENT - 3 * LANES), bf16)

    shape = jax.ShapeDtypeStruct((per_group + STAT_ROWS, LATENT), bf16)
    flops = 2 * count * rows * heads * context * (width + LATENT)
    return call(
        body,
        [shape] * count,
        [*groups, in_vmem(cache), seen],
        [IN_VMEM] * (count + 2),
        limit=ATTEND_LIMIT,
        cost=(flops, 4 << 20),
    )


def join_and_project(parts, pieces, rows, heads, after):
    count, slices = len(parts), len(pieces)
    per_group = rows * heads
    _, depth, vdim = pieces[0].shape

    def body(*refs):
        part_refs, piece_refs = refs[:count], refs[count : count + slices]
        value_ref, attended = refs[count + slices + 1 :]
        me = lax.axis_index(("role", "seq"))
        tops, sums = [], []
        for ref in part_refs:
            table = sum(
                ref[per_group:, i * LANES : (i + 1) * LANES].astype(f32) for i in reversed(range(3))
            )
            table = jnp.concatenate([table, jnp.zeros((LANES - STAT_ROWS, LANES), f32)], axis=0).T
            tops.append(table[:per_group, 0:1])
            sums.append(table[:per_group, 1:2])
        highest = functools.reduce(jnp.maximum, tops)
        factors = [jnp.exp(top - highest) for top in tops]
        denom = sum(f * s for f, s in zip(factors, sums))
        numer = sum(f * ref[:per_group, :].astype(f32) for f, ref in zip(factors, part_refs))
        joined = (numer / denom).astype(bf16).astype(f32)
        for k in range(slices):
            attended[k] = joined[:, k * depth : (k + 1) * depth]
        for h in range(heads):
            total = None
            for m in range(slices):
                left = attended[me ^ m, pl.ds(h, rows, stride=heads), :].astype(bf16)
                term = jnp.dot(left, piece_refs[m][h], preferred_element_type=f32)
                total = term if total is None else total + term
            value_ref[:, h * vdim : (h + 1) * vdim] = total.astype(bf16)

    return call(
        body,
        jax.ShapeDtypeStruct((rows, heads * vdim), bf16),
        [*parts, *[in_vmem(piece) for piece in pieces], after],
        [IN_VMEM] * (count + slices + 1),
        [pltpu.VMEM((slices, per_group, depth), f32)],
        cost=(2 * rows * heads * LATENT * vdim, 4 << 20),
    )


def project_out(pieces, weight):
    count = len(pieces)
    rows, depth = pieces[0].shape
    width = weight.shape[1]

    def body(*refs):
        weight_ref, out_ref, placed = refs[count:]
        me = lax.axis_index(("role", "seq"))
        for m in range(count):
            placed[me ^ m] = refs[m][...].astype(f32)
        values = jnp.concatenate([placed[k] for k in range(count)], axis=0).astype(bf16)
        out_ref[...] = jnp.dot(values, weight_ref[...], preferred_element_type=f32).astype(bf16)

    return call(
        body,
        jax.ShapeDtypeStruct((count * rows, width), bf16),
        [*pieces, in_vmem(weight)],
        [IN_VMEM] * (count + 1),
        [pltpu.VMEM((count, rows, depth), f32)],
        cost=(2 * count * rows * depth * width, 4 << 20),
    )


def gate_and_up_away(pieces, residual, gain, gate_weight, up_weight):
    count = len(pieces)
    rows, width = residual.shape
    hidden = gate_weight.shape[1]
    cores = lax.axis_size("seq")
    half = hidden // cores
    own_rows = rows // count

    def body(*refs):
        residual_ref, gain_ref, gate_ref, up_ref = refs[count : count + 4]
        send_ref, scaled_ref, squares_ref, base_ref, placed = refs[count + 4 :]
        resid = residual_ref[...].astype(f32) + sum(ref[...].astype(f32) for ref in refs[:count])
        scaled = (resid * gain_ref[...]).astype(bf16)
        scaled_ref[...] = scaled
        other = lax.axis_index("seq") ^ 1
        for k in range(cores):

            @pl.when(other == k)
            def _(k=k):
                part = slice(k * half, (k + 1) * half)
                gate = jnp.dot(scaled, gate_ref[:, part], preferred_element_type=f32)
                up = jnp.dot(scaled, up_ref[:, part], preferred_element_type=f32)
                send_ref[:, :half] = gate.astype(bf16)
                send_ref[:, half : 2 * half] = up.astype(bf16)

        for k in range(count):
            placed[k] = resid[k * own_rows : (k + 1) * own_rows]
        base_ref[...] = placed[lax.axis_index("ctx")]
        squares = jnp.sum(resid * resid, axis=1, keepdims=True)
        lane = lax.broadcasted_iota(jnp.int32, (rows, LANES), 1)
        squares_ref[...] = jnp.broadcast_to(squares, (rows, LANES))
        send_ref[:, 2 * half :] = spread(squares, lane)

    return call(
        body,
        [
            jax.ShapeDtypeStruct((rows, 2 * half + LANES), bf16),
            jax.ShapeDtypeStruct((rows, width), bf16),
            jax.ShapeDtypeStruct((rows, LANES), f32),
            jax.ShapeDtypeStruct((own_rows, width), f32),
        ],
        [*pieces, residual, gain, in_vmem(gate_weight), in_vmem(up_weight)],
        [IN_VMEM] * (count + 4),
        [pltpu.VMEM((count, own_rows, width), f32)],
        cost=(2 * rows * width * hidden, 4 << 20),
    )


def gate_and_up_here(scaled, gate_weight, up_weight):
    rows, width = scaled.shape
    hidden = gate_weight.shape[1]
    cores = lax.axis_size("seq")
    half = hidden // cores

    def body(scaled_ref, gate_ref, up_ref, keep_ref):
        me = lax.axis_index("seq")
        for k in range(cores):

            @pl.when(me == k)
            def _(k=k):
                part = slice(k * half, (k + 1) * half)
                keep_ref[:, :half] = jnp.dot(scaled_ref[...], gate_ref[:, part], preferred_element_type=f32)
                keep_ref[:, half:] = jnp.dot(scaled_ref[...], up_ref[:, part], preferred_element_type=f32)

    return call(
        body,
        jax.ShapeDtypeStruct((rows, 2 * half), f32),
        [scaled, in_vmem(gate_weight), in_vmem(up_weight)],
        [IN_VMEM] * 3,
        cost=(2 * rows * width * hidden, 4 << 20),
    )


def spread(column, lane):
    high, middle, low = three_parts(column)
    return jnp.where(
        lane == 0,
        high.astype(f32),
        jnp.where(lane == 1, middle.astype(f32), jnp.where(lane == 2, low.astype(f32), 0.0)),
    ).astype(bf16)


def add_core(keep, squares, got):
    rows, width = got.shape
    body_width = width - LANES

    def body(keep_ref, squares_ref, got_ref, sum_ref, send_ref):
        total = keep_ref[...] + got_ref[:, :body_width].astype(f32)
        both = squares_ref[:, 0:1] + jnp.sum(got_ref[:, body_width:].astype(f32), axis=1, keepdims=True)
        sum_ref[:, :body_width] = total
        sum_ref[:, body_width:] = jnp.broadcast_to(both, (rows, LANES))
        send_ref[:, :body_width] = total.astype(bf16)
        lane = lax.broadcasted_iota(jnp.int32, (rows, LANES), 1)
        send_ref[:, body_width:] = spread(both, lane)

    return call(
        body,
        [jax.ShapeDtypeStruct((rows, width), f32), jax.ShapeDtypeStruct((rows, width), bf16)],
        [keep, squares, got],
        [IN_VMEM] * 3,
        cost=(rows * width, rows * width * 8),
    )


def activate(keep, pieces, features):
    rows, width = keep.shape
    body_width = width - LANES
    half = body_width // 2

    def body(*refs):
        keep_ref, out_ref = refs[0], refs[-1]
        total = keep_ref[:, :body_width] + sum(r[:, :body_width].astype(f32) for r in refs[1:-1])
        squares = keep_ref[:, body_width : body_width + 1] + sum(
            jnp.sum(r[:, body_width:].astype(f32), axis=1, keepdims=True) for r in refs[1:-1]
        )
        scale = lax.rsqrt(squares / features + EPSILON)
        gate = total[:, :half] * scale
        up = total[:, half:] * scale
        out_ref[...] = (gate / (1.0 + jnp.exp(-gate)) * up).astype(bf16)

    return call(
        body,
        jax.ShapeDtypeStruct((rows, half), bf16),
        [keep, *pieces],
        [IN_VMEM] * (1 + len(pieces)),
        cost=(rows * width, rows * width * 8),
    )


def project_down_own(own, weight):
    rows, half = own.shape
    width = weight.shape[1]

    def body(own_ref, weight_ref, out_ref):
        start = pl.multiple_of(lax.axis_index("seq") * half, 16)
        out_ref[...] = jnp.dot(own_ref[...], weight_ref[pl.ds(start, half), :], preferred_element_type=f32)

    return call(
        body,
        jax.ShapeDtypeStruct((rows, width), f32),
        [own, in_vmem(weight)],
        [IN_VMEM] * 2,
        cost=(2 * rows * half * width, 4 << 20),
    )


def project_down_other(other, weight, partial):
    rows, half = other.shape
    width = weight.shape[1]
    count = lax.axis_size("ctx")
    own_rows = rows // count

    def body(other_ref, weight_ref, partial_ref, *refs):
        out_refs, placed = refs[:count], refs[count]
        start = pl.multiple_of((lax.axis_index("seq") ^ 1) * half, 16)
        out = partial_ref[...] + jnp.dot(
            other_ref[...], weight_ref[pl.ds(start, half), :], preferred_element_type=f32
        )
        for k in range(count):
            placed[k] = out[k * own_rows : (k + 1) * own_rows]
        me = lax.axis_index("ctx")
        for m in range(count):
            out_refs[m][...] = placed[me ^ m].astype(bf16)

    return call(
        body,
        [jax.ShapeDtypeStruct((own_rows, width), bf16)] * count,
        [other, in_vmem(weight), partial],
        [IN_VMEM] * 3,
        [pltpu.VMEM((count, own_rows, width), f32)],
        cost=(2 * rows * half * width, 4 << 20),
    )


def finish(base, pieces):
    def body(*refs):
        refs[-1][...] = (refs[0][...] + sum(r[...].astype(f32) for r in refs[1:-1])).astype(bf16)

    return call(
        body,
        jax.ShapeDtypeStruct(base.shape, bf16),
        [base, *pieces],
        [IN_VMEM] * (1 + len(pieces)),
        cost=(base.size, base.size * 8),
    )


def per_device(
    queries,
    cache,
    lengths,
    positions,
    value_up_weight,
    out_proj,
    residual,
    norm_gain,
    gate_weight,
    up_weight,
    down_weight,
):
    rows, heads, _ = queries.shape
    blocks = lax.axis_size("ctx")
    roles = lax.axis_size("role")
    members = lax.axis_size(("role", "seq"))

    evens, odds = range(2, blocks, 2), range(3, blocks, 2)

    groups = exchange([queries] * blocks, "ctx", [*evens, 1])
    along = listed(exchange([value_up_weight] * roles, "role"))
    groups[0], cache_fast, up_own, out_fast, seen = fetch(
        [queries, jnp.swapaxes(cache, 1, 2), value_up_weight, out_proj], lengths, positions
    )
    relayed = {}
    for mask in evens:
        relayed[mask + 1] = xor_permute(groups[mask], "ctx", 1)

    def attend_and_answer(source, masks):
        outs = attend([source[mask] for mask in masks], cache_fast, seen)
        return dict(zip(masks, outs))

    partial = attend_and_answer(groups, evens)
    answers = exchange({0: None, **partial}, "ctx", evens)
    near = attend_and_answer(groups, [0, 1])
    answers |= exchange(near, "ctx", [1])
    far = attend_and_answer(relayed, odds)

    gate_weight, up_weight, far[odds[0]] = lax.optimization_barrier((gate_weight, up_weight, far[odds[0]]))
    answers |= exchange({0: near[0], **far}, "ctx", odds)
    gate_fast, up_fast, residual, gain = fetch(
        [gate_weight, up_weight, residual, norm_gain.reshape(1, -1)]
    )
    *along, gain = lax.optimization_barrier((*along, gain))
    across = [xor_permute(piece, "seq", 1) for piece in along]
    up_pieces = [up_own, *[piece for pair in zip(along, across) for piece in pair][1:]]

    values = join_and_project(listed(answers), up_pieces, rows, heads, gain)
    shared = listed(exchange([values] * members, ("role", "seq")))
    product = project_out(shared, out_fast)
    down_weight, product = lax.optimization_barrier((down_weight, product))
    terms = listed(exchange([product] * blocks, "ctx"))
    (down_fast,) = fetch([down_weight])

    send, scaled, squares, base = gate_and_up_away(terms, residual, gain, gate_fast, up_fast)
    got = xor_permute(send, "seq", 1)
    keep = gate_and_up_here(scaled, gate_fast, up_fast)
    keep, send = add_core(keep, squares, got)
    pieces = listed(exchange([send] * roles, "role"))[1:]
    features = norm_gain.shape[0] * members
    hidden = activate(keep, pieces, features)
    other = xor_permute(hidden, "seq", 1)
    own = project_down_own(hidden, down_fast)
    last = exchange(project_down_other(other, down_fast, own), "ctx")
    return finish(base, listed(last))


def solution(mesh):
    placed = (
        P(("groups", "role", "seq"), "ctx", None),
        P(("groups", "role", "seq"), "ctx", None),
        P(("groups", "role", "seq")),
        P(("groups", "role", "seq")),
        P("ctx", ("role", "seq"), None),
        P("ctx", ("role", "seq")),
        P("groups", ("role", "seq")),
        P(("role", "seq")),
        P(("role", "seq"), "ctx"),
        P(("role", "seq"), "ctx"),
        P("ctx", ("role", "seq")),
    )

    return jax.shard_map(
        per_device,
        mesh=mesh,
        in_specs=placed,
        out_specs=P(("groups", "ctx"), ("role", "seq")),
        check_vma=False,
    )
```

```python
import functools

import jax
import jax.numpy as jnp
from jax import lax
from jax.experimental import pallas as pl
from jax.experimental.pallas import tpu as pltpu
from jax.sharding import PartitionSpec as P


LATENT = 512
MTP = 2
SCALE = 0.07216878364870323
EPSILON = 1e-06
DEAD = -1e30
STAT_ROWS = 8
LANES = 128
ATTEND_LIMIT = 8 << 20
KERNEL_LIMIT = 6 << 20


f32, bf16 = jnp.float32, jnp.bfloat16
IN_VMEM = pl.BlockSpec(memory_space=pltpu.VMEM)
IN_SMEM = pl.BlockSpec(memory_space=pltpu.SMEM)
IN_HBM = pl.BlockSpec(memory_space=pltpu.HBM)


def xor_permute(x, axis, mask):
    size = lax.axis_size(axis)
    return lax.ppermute(x, axis, [(i, i ^ mask) for i in range(size)])


def exchange(pieces, axis, masks=None):
    got = {0: pieces[0]}
    for mask in masks or reversed(range(1, len(pieces))):
        got[mask] = xor_permute(pieces[mask], axis, mask)
    return got


def listed(got):
    return [got[mask] for mask in sorted(got)]


def call(body, outs, args, specs, scratch=(), limit=KERNEL_LIMIT, cost=None):
    flops, moved = cost or (0, 0)
    return pl.pallas_call(
        body,
        out_shape=outs,
        in_specs=specs,
        out_specs=jax.tree.map(lambda _: IN_VMEM, outs),
        scratch_shapes=list(scratch),
        compiler_params=pltpu.CompilerParams(vmem_limit_bytes=limit),
        cost_estimate=pl.CostEstimate(flops=flops, bytes_accessed=moved, transcendentals=0),
    )(*args)


def in_vmem(x):
    return pltpu.with_memory_space_constraint(x, pltpu.VMEM)


def three_parts(x):
    high = x.astype(bf16)
    rest = x - high.astype(f32)
    middle = rest.astype(bf16)
    return high, middle, (rest - middle.astype(f32)).astype(bf16)


def fetch(arrays, lengths=None, positions=None):
    count = len(arrays)
    scalars = [] if positions is None else [lengths, positions]
    rows = positions.shape[0] if scalars else 0
    copied = count + len(scalars)

    def body(*refs):
        sources, refs = refs[:copied], refs[copied:]
        targets, refs = refs[:count], refs[count:]
        done, in_smem = refs[-1], refs[-1 - len(scalars) : -1]
        copies = [
            pltpu.make_async_copy(source, target, done.at[i])
            for i, (source, target) in enumerate(zip(sources, [*targets, *in_smem]))
        ]
        for copy in reversed(copies):
            copy.start()
        for copy in copies[count:]:
            copy.wait()
        if scalars:
            length_ref, position_ref = in_smem
            row = lax.broadcasted_iota(jnp.int32, (rows, LANES), 0)
            seen = jnp.zeros((rows, LANES), jnp.int32)
            for r in range(rows):
                bound = jnp.minimum(length_ref[r // MTP], position_ref[r] + 1)
                seen = jnp.where(row == r, bound, seen)
            refs[0][...] = seen
        for copy in copies[:count]:
            copy.wait()

    moved = sum(2 * x.size * x.dtype.itemsize for x in arrays)
    return call(
        body,
        [pltpu.VMEM(x.shape, x.dtype) for x in arrays]
        + ([pltpu.VMEM((rows, LANES), jnp.int32)] if scalars else []),
        [pltpu.with_memory_space_constraint(x, pltpu.HBM) for x in [*arrays, *scalars]],
        [IN_HBM] * copied,
        [pltpu.SMEM(x.shape, x.dtype) for x in scalars] + [pltpu.SemaphoreType.DMA((copied,))],
        limit=1 << 20,
        cost=(0, moved),
    )


def attend(groups, cache, seen, weight, span):
    count = len(groups)
    rows, heads, width = groups[0].shape
    seqs, _, context = cache.shape
    per_seq = MTP * heads
    per_group = rows * heads

    def body(*refs):
        query_refs = refs[:count]
        cache_ref, seen_ref, weight_ref = refs[count : count + 3]
        out_refs = refs[count + 3 : 2 * count + 3]
        fetched, done = refs[2 * count + 3 :]
        copy = pltpu.make_async_copy(weight_ref.at[pl.ds(span[0], span[1] - span[0])], fetched, done)
        copy.start()
        offset = lax.axis_index("ctx") * context
        total = count * per_seq
        tops, sums = [[] for _ in range(count)], [[] for _ in range(count)]
        for n in range(seqs):
            queries = jnp.concatenate(
                [q[MTP * n : MTP * (n + 1)].reshape(per_seq, width) for q in query_refs], axis=0
            )
            scores = jnp.dot(queries, cache_ref[n], preferred_element_type=f32) * SCALE
            row = lax.broadcasted_iota(jnp.int32, (total, 1), 0)
            which = (row // heads) % MTP
            limit = jnp.full((total, 1), 0, jnp.int32)
            for t in range(MTP):
                r = MTP * n + t
                limit = jnp.where(which == t, seen_ref[r : r + 1, 0:1], limit)
            place = offset + lax.broadcasted_iota(jnp.int32, (total, context), 1)
            live = place < limit
            top = jnp.max(jnp.where(live, scores, DEAD), axis=1, keepdims=True)
            probs = jnp.exp(jnp.where(live, scores - top, DEAD)).astype(bf16)
            weight = jnp.sum(probs.astype(f32), axis=1, keepdims=True)
            out = lax.dot_general(
                probs, cache_ref[n, :LATENT, :], (((1,), (1,)), ((), ())), preferred_element_type=f32
            )
            for g in range(count):
                part = slice(g * per_seq, (g + 1) * per_seq)
                out_refs[g][n * per_seq : (n + 1) * per_seq, :] = out[part].astype(bf16)
                tops[g].append(top[part])
                sums[g].append(weight[part])
        lane = lax.broadcasted_iota(jnp.int32, (LANES, LANES), 1)
        for g in range(count):
            fill = [jnp.zeros((LANES - per_group, 1), f32)] if per_group < LANES else []
            top = jnp.concatenate(tops[g] + fill, axis=0)
            weight = jnp.concatenate(sums[g] + fill, axis=0)
            table = jnp.where(lane == 0, top, jnp.where(lane == 1, weight, 0.0)).T
            for i, part in enumerate(three_parts(table[:STAT_ROWS])):
                out_refs[g][per_group:, i * LANES : (i + 1) * LANES] = part
            out_refs[g][per_group:, 3 * LANES :] = jnp.zeros((STAT_ROWS, LATENT - 3 * LANES), bf16)
        copy.wait()

    shape = jax.ShapeDtypeStruct((per_group + STAT_ROWS, LATENT), bf16)
    flops = 2 * count * rows * heads * context * (width + LATENT)
    return call(
        body,
        [shape] * count + [pltpu.VMEM((span[1] - span[0], weight.shape[1]), weight.dtype)],
        [*groups, in_vmem(cache), seen, pltpu.with_memory_space_constraint(weight, pltpu.HBM)],
        [IN_VMEM] * (count + 2) + [IN_HBM],
        [pltpu.SemaphoreType.DMA],
        limit=ATTEND_LIMIT,
        cost=(flops, 4 << 20),
    )


def join_and_project(parts, pieces, rows, heads, after):
    count, slices = len(parts), len(pieces)
    per_group = rows * heads
    _, depth, vdim = pieces[0].shape

    def body(*refs):
        part_refs, piece_refs = refs[:count], refs[count : count + slices]
        value_ref, attended = refs[count + slices + 1 :]
        me = lax.axis_index(("role", "seq"))
        tops, sums = [], []
        for ref in part_refs:
            table = sum(
                ref[per_group:, i * LANES : (i + 1) * LANES].astype(f32) for i in reversed(range(3))
            )
            table = jnp.concatenate([table, jnp.zeros((LANES - STAT_ROWS, LANES), f32)], axis=0).T
            tops.append(table[:per_group, 0:1])
            sums.append(table[:per_group, 1:2])
        highest = functools.reduce(jnp.maximum, tops)
        factors = [jnp.exp(top - highest) for top in tops]
        denom = sum(f * s for f, s in zip(factors, sums))
        numer = sum(f * ref[:per_group, :].astype(f32) for f, ref in zip(factors, part_refs))
        joined = (numer / denom).astype(bf16).astype(f32)
        for k in range(slices):
            attended[k] = joined[:, k * depth : (k + 1) * depth]
        for h in range(heads):
            total = None
            for m in range(slices):
                left = attended[me ^ m, pl.ds(h, rows, stride=heads), :].astype(bf16)
                term = jnp.dot(left, piece_refs[m][h], preferred_element_type=f32)
                total = term if total is None else total + term
            value_ref[:, h * vdim : (h + 1) * vdim] = total.astype(bf16)

    return call(
        body,
        jax.ShapeDtypeStruct((rows, heads * vdim), bf16),
        [*parts, *[in_vmem(piece) for piece in pieces], after],
        [IN_VMEM] * (count + slices + 1),
        [pltpu.VMEM((slices, per_group, depth), f32)],
        cost=(2 * rows * heads * LATENT * vdim, 4 << 20),
    )


def project_out(pieces, weights):
    count, parts = len(pieces), len(weights)
    rows, depth = pieces[0].shape
    width = weights[0].shape[1]

    def body(*refs):
        weight_refs, (out_ref, placed) = refs[count : count + parts], refs[count + parts :]
        me = lax.axis_index(("role", "seq"))
        for m in range(count):
            placed[me ^ m] = refs[m][...].astype(f32)
        values = jnp.concatenate([placed[k] for k in range(count)], axis=0).astype(bf16)
        total, start = None, 0
        for ref in weight_refs:
            term = jnp.dot(values[:, start : start + ref.shape[0]], ref[...], preferred_element_type=f32)
            total = term if total is None else total + term
            start += ref.shape[0]
        out_ref[...] = total.astype(bf16)

    return call(
        body,
        jax.ShapeDtypeStruct((count * rows, width), bf16),
        [*pieces, *[in_vmem(weight) for weight in weights]],
        [IN_VMEM] * (count + parts),
        [pltpu.VMEM((count, rows, depth), f32)],
        cost=(2 * count * rows * depth * width, 4 << 20),
    )


def gate_and_up_away(pieces, residual, gain, gate_weight, up_weight):
    count = len(pieces)
    rows, width = residual.shape
    hidden = gate_weight.shape[1]
    cores = lax.axis_size("seq")
    half = hidden // cores
    own_rows = rows // count

    def body(*refs):
        residual_ref, gain_ref, gate_ref, up_ref = refs[count : count + 4]
        send_ref, scaled_ref, squares_ref, base_ref, placed = refs[count + 4 :]
        resid = residual_ref[...].astype(f32) + sum(ref[...].astype(f32) for ref in refs[:count])
        scaled = (resid * gain_ref[...][None, :]).astype(bf16)
        scaled_ref[...] = scaled
        other = lax.axis_index("seq") ^ 1
        for k in range(cores):

            @pl.when(other == k)
            def _(k=k):
                part = slice(k * half, (k + 1) * half)
                gate = jnp.dot(scaled, gate_ref[:, part], preferred_element_type=f32)
                up = jnp.dot(scaled, up_ref[:, part], preferred_element_type=f32)
                send_ref[:, :half] = gate.astype(bf16)
                send_ref[:, half : 2 * half] = up.astype(bf16)

        for k in range(count):
            placed[k] = resid[k * own_rows : (k + 1) * own_rows]
        base_ref[...] = placed[lax.axis_index("ctx")]
        squares = jnp.sum(resid * resid, axis=1, keepdims=True)
        lane = lax.broadcasted_iota(jnp.int32, (rows, LANES), 1)
        squares_ref[...] = jnp.broadcast_to(squares, (rows, LANES))
        send_ref[:, 2 * half :] = spread(squares, lane)

    return call(
        body,
        [
            jax.ShapeDtypeStruct((rows, 2 * half + LANES), bf16),
            jax.ShapeDtypeStruct((rows, width), bf16),
            jax.ShapeDtypeStruct((rows, LANES), f32),
            jax.ShapeDtypeStruct((own_rows, width), f32),
        ],
        [*pieces, residual, gain, in_vmem(gate_weight), in_vmem(up_weight)],
        [IN_VMEM] * (count + 4),
        [pltpu.VMEM((count, own_rows, width), f32)],
        cost=(2 * rows * width * hidden, 4 << 20),
    )


def gate_and_up_here(scaled, gate_weight, up_weight):
    rows, width = scaled.shape
    hidden = gate_weight.shape[1]
    cores = lax.axis_size("seq")
    half = hidden // cores

    def body(scaled_ref, gate_ref, up_ref, keep_ref):
        me = lax.axis_index("seq")
        for k in range(cores):

            @pl.when(me == k)
            def _(k=k):
                part = slice(k * half, (k + 1) * half)
                keep_ref[:, :half] = jnp.dot(scaled_ref[...], gate_ref[:, part], preferred_element_type=f32)
                keep_ref[:, half:] = jnp.dot(scaled_ref[...], up_ref[:, part], preferred_element_type=f32)

    return call(
        body,
        jax.ShapeDtypeStruct((rows, 2 * half), f32),
        [scaled, in_vmem(gate_weight), in_vmem(up_weight)],
        [IN_VMEM] * 3,
        cost=(2 * rows * width * hidden, 4 << 20),
    )


def spread(column, lane):
    high, middle, low = three_parts(column)
    return jnp.where(
        lane == 0,
        high.astype(f32),
        jnp.where(lane == 1, middle.astype(f32), jnp.where(lane == 2, low.astype(f32), 0.0)),
    ).astype(bf16)


def add_core(keep, squares, got):
    rows, width = got.shape
    body_width = width - LANES

    def body(keep_ref, squares_ref, got_ref, sum_ref, send_ref):
        total = keep_ref[...] + got_ref[:, :body_width].astype(f32)
        both = squares_ref[:, 0:1] + jnp.sum(got_ref[:, body_width:].astype(f32), axis=1, keepdims=True)
        sum_ref[:, :body_width] = total
        sum_ref[:, body_width:] = jnp.broadcast_to(both, (rows, LANES))
        send_ref[:, :body_width] = total.astype(bf16)
        lane = lax.broadcasted_iota(jnp.int32, (rows, LANES), 1)
        send_ref[:, body_width:] = spread(both, lane)

    return call(
        body,
        [jax.ShapeDtypeStruct((rows, width), f32), jax.ShapeDtypeStruct((rows, width), bf16)],
        [keep, squares, got],
        [IN_VMEM] * 3,
        cost=(rows * width, rows * width * 8),
    )


def activate(keep, pieces, features):
    rows, width = keep.shape
    body_width = width - LANES
    half = body_width // 2

    def body(*refs):
        keep_ref, out_ref = refs[0], refs[-1]
        total = keep_ref[:, :body_width] + sum(r[:, :body_width].astype(f32) for r in refs[1:-1])
        squares = keep_ref[:, body_width : body_width + 1] + sum(
            jnp.sum(r[:, body_width:].astype(f32), axis=1, keepdims=True) for r in refs[1:-1]
        )
        scale = lax.rsqrt(squares / features + EPSILON)
        gate = total[:, :half] * scale
        up = total[:, half:] * scale
        out_ref[...] = (gate / (1.0 + jnp.exp(-gate)) * up).astype(bf16)

    return call(
        body,
        jax.ShapeDtypeStruct((rows, half), bf16),
        [keep, *pieces],
        [IN_VMEM] * (1 + len(pieces)),
        cost=(rows * width, rows * width * 8),
    )


def project_down_own(own, weight):
    rows, half = own.shape
    width = weight.shape[1]

    def body(own_ref, weight_ref, out_ref):
        start = pl.multiple_of(lax.axis_index("seq") * half, 16)
        out_ref[...] = jnp.dot(own_ref[...], weight_ref[pl.ds(start, half), :], preferred_element_type=f32)

    return call(
        body,
        jax.ShapeDtypeStruct((rows, width), f32),
        [own, in_vmem(weight)],
        [IN_VMEM] * 2,
        cost=(2 * rows * half * width, 4 << 20),
    )


def project_down_other(other, weight, partial):
    rows, half = other.shape
    width = weight.shape[1]
    count = lax.axis_size("ctx")
    own_rows = rows // count

    def body(other_ref, weight_ref, partial_ref, *refs):
        out_refs, placed = refs[:count], refs[count]
        start = pl.multiple_of((lax.axis_index("seq") ^ 1) * half, 16)
        out = partial_ref[...] + jnp.dot(
            other_ref[...], weight_ref[pl.ds(start, half), :], preferred_element_type=f32
        )
        for k in range(count):
            placed[k] = out[k * own_rows : (k + 1) * own_rows]
        me = lax.axis_index("ctx")
        for m in range(count):
            out_refs[m][...] = placed[me ^ m].astype(bf16)

    return call(
        body,
        [jax.ShapeDtypeStruct((own_rows, width), bf16)] * count,
        [other, in_vmem(weight), partial],
        [IN_VMEM] * 3,
        [pltpu.VMEM((count, own_rows, width), f32)],
        cost=(2 * rows * half * width, 4 << 20),
    )


def finish(base, pieces):
    def body(*refs):
        refs[-1][...] = (refs[0][...] + sum(r[...].astype(f32) for r in refs[1:-1])).astype(bf16)

    return call(
        body,
        jax.ShapeDtypeStruct(base.shape, bf16),
        [base, *pieces],
        [IN_VMEM] * (1 + len(pieces)),
        cost=(base.size, base.size * 8),
    )


def per_device(
    queries,
    cache,
    lengths,
    positions,
    value_up_weight,
    out_proj,
    residual,
    norm_gain,
    gate_weight,
    up_weight,
    down_weight,
):
    rows, heads, _ = queries.shape
    blocks = lax.axis_size("ctx")
    roles = lax.axis_size("role")
    members = lax.axis_size(("role", "seq"))

    evens, odds = range(2, blocks, 2), range(3, blocks, 2)

    along = listed(exchange([value_up_weight] * roles, "role"))
    groups = exchange([queries] * blocks, "ctx", [*evens, 1])
    gate_fast, up_own, groups[0], cache_fast, seen = fetch(
        [gate_weight, value_up_weight, queries, jnp.swapaxes(cache, 1, 2)], lengths, positions
    )
    relayed = {}
    for mask in evens:
        relayed[mask + 1] = xor_permute(groups[mask], "ctx", 1)

    unit = out_proj.shape[0] // 16
    cuts = [0, 5 * unit, 11 * unit, 16 * unit]
    out_parts = []

    def attend_and_answer(source, masks):
        k = len(out_parts)
        *outs, part = attend(
            [source[mask] for mask in masks], cache_fast, seen, out_proj, (cuts[k], cuts[k + 1])
        )
        out_parts.append(part)
        return dict(zip(masks, outs))

    partial = attend_and_answer(groups, evens)
    answers = exchange({0: None, **partial}, "ctx", evens)
    near = attend_and_answer(groups, [0, 1])
    far = attend_and_answer(relayed, odds)
    answers |= exchange({0: near[0], **far}, "ctx", odds)
    answers |= exchange(near, "ctx", [1])

    up_weight, part = lax.optimization_barrier((up_weight, out_parts[-1]))
    out_parts[-1] = part
    up_fast, residual, gain = fetch([up_weight, residual, norm_gain])
    *far_rows, gain = lax.optimization_barrier((*along[1:], gain))
    across = [xor_permute(along[0], "seq", 1)]
    across += [xor_permute(piece, "seq", 1) for piece in far_rows]
    up_pieces = [up_own, *[piece for pair in zip([None, *far_rows], across) for piece in pair][1:]]

    values = join_and_project(listed(answers), up_pieces, rows, heads, gain)
    shared = listed(exchange([values] * members, ("role", "seq")))
    product = project_out(shared, out_parts)
    down_weight, product = lax.optimization_barrier((down_weight, product))
    terms = listed(exchange([product] * blocks, "ctx"))
    (down_fast,) = fetch([down_weight])

    send, scaled, squares, base = gate_and_up_away(terms, residual, gain, gate_fast, up_fast)
    got = xor_permute(send, "seq", 1)
    keep = gate_and_up_here(scaled, gate_fast, up_fast)
    keep, send = add_core(keep, squares, got)
    pieces = listed(exchange([send] * roles, "role"))[1:]
    features = norm_gain.shape[0] * members
    hidden = activate(keep, pieces, features)
    other = xor_permute(hidden, "seq", 1)
    own = project_down_own(hidden, down_fast)
    last = exchange(project_down_other(other, down_fast, own), "ctx")
    return finish(base, listed(last))


def solution(mesh):
    placed = (
        P(("groups", "role", "seq"), "ctx", None),
        P(("groups", "role", "seq"), "ctx", None),
        P(("groups", "role", "seq")),
        P(("groups", "role", "seq")),
        P("ctx", ("role", "seq"), None),
        P("ctx", ("role", "seq")),
        P("groups", ("role", "seq")),
        P(("role", "seq")),
        P(("role", "seq"), "ctx"),
        P(("role", "seq"), "ctx"),
        P("ctx", ("role", "seq")),
    )


    return jax.shard_map(
        per_device,
        mesh=mesh,
        in_specs=placed,
        out_specs=P(("groups", "ctx"), ("role", "seq")),
        check_vma=False,
    )
```

```python
import functools
import math

import jax
import jax.numpy as jnp
from jax import lax
from jax.experimental import pallas as pl
from jax.experimental.pallas import tpu as pltpu
from jax.sharding import PartitionSpec as P


LATENT = 512
MTP = 2
SCALE = 0.07216878364870323
EPSILON = 1e-06
DEAD = -1e30
STAT_ROWS = 8
LANES = 128
ATTEND_LIMIT = 8 << 20
KERNEL_LIMIT = 6 << 20


f32, bf16 = jnp.float32, jnp.bfloat16
IN_VMEM = pl.BlockSpec(memory_space=pltpu.VMEM)
IN_SMEM = pl.BlockSpec(memory_space=pltpu.SMEM)
IN_HBM = pl.BlockSpec(memory_space=pltpu.HBM)


def xor_permute(x, axis, mask):
    size = lax.axis_size(axis)
    return lax.ppermute(x, axis, [(i, i ^ mask) for i in range(size)])


def exchange(pieces, axis, masks=None):
    got = {0: pieces[0]}
    for mask in masks or reversed(range(1, len(pieces))):
        got[mask] = xor_permute(pieces[mask], axis, mask)
    return got


def listed(got):
    return [got[mask] for mask in sorted(got)]


def call(body, outs, args, specs, scratch=(), limit=KERNEL_LIMIT, cost=None):
    flops, moved = cost or (0, 0)
    return pl.pallas_call(
        body,
        out_shape=outs,
        in_specs=specs,
        out_specs=jax.tree.map(lambda _: IN_VMEM, outs),
        scratch_shapes=list(scratch),
        compiler_params=pltpu.CompilerParams(vmem_limit_bytes=limit),
        cost_estimate=pl.CostEstimate(flops=flops, bytes_accessed=moved, transcendentals=0),
    )(*args)


def in_vmem(x):
    return pltpu.with_memory_space_constraint(x, pltpu.VMEM)


def three_parts(x):
    high = x.astype(bf16)
    rest = x - high.astype(f32)
    middle = rest.astype(bf16)
    return high, middle, (rest - middle.astype(f32)).astype(bf16)


def fetch(arrays, lengths=None, positions=None):
    spans = [x[1] if isinstance(x, tuple) else (0, x.shape[0]) for x in arrays]
    arrays = [x[0] if isinstance(x, tuple) else x for x in arrays]
    shapes = [(last - first, *x.shape[1:]) for x, (first, last) in zip(arrays, spans)]
    count = len(arrays)
    scalars = [] if positions is None else [lengths, positions]
    rows = positions.shape[0] if scalars else 0
    copied = count + len(scalars)

    def body(*refs):
        sources, refs = refs[:copied], refs[copied:]
        targets, refs = refs[:count], refs[count:]
        sources = [
            source if i >= count or spans[i] == (0, source.shape[0]) else source.at[pl.ds(spans[i][0], shapes[i][0])]
            for i, source in enumerate(sources)
        ]
        done, in_smem = refs[-1], refs[-1 - len(scalars) : -1]
        copies = [
            pltpu.make_async_copy(source, target, done.at[i])
            for i, (source, target) in enumerate(zip(sources, [*targets, *in_smem]))
        ]
        for copy in reversed(copies):
            copy.start()
        for copy in copies[count:]:
            copy.wait()
        if scalars:
            length_ref, position_ref = in_smem
            row = lax.broadcasted_iota(jnp.int32, (rows, LANES), 0)
            seen = jnp.zeros((rows, LANES), jnp.int32)
            for r in range(rows):
                bound = jnp.minimum(length_ref[r // MTP], position_ref[r] + 1)
                seen = jnp.where(row == r, bound, seen)
            refs[0][...] = seen
        for copy in copies[:count]:
            copy.wait()

    moved = sum(2 * math.prod(shape) * x.dtype.itemsize for shape, x in zip(shapes, arrays))
    return call(
        body,
        [pltpu.VMEM(shape, x.dtype) for shape, x in zip(shapes, arrays)]
        + ([pltpu.VMEM((rows, LANES), jnp.int32)] if scalars else []),
        [pltpu.with_memory_space_constraint(x, pltpu.HBM) for x in [*arrays, *scalars]],
        [IN_HBM] * copied,
        [pltpu.SMEM(x.shape, x.dtype) for x in scalars] + [pltpu.SemaphoreType.DMA((copied,))],
        limit=1 << 20,
        cost=(0, moved),
    )


def attend(groups, cache, seen, weight, span):
    count = len(groups)
    rows, heads, width = groups[0].shape
    seqs, _, context = cache.shape
    per_seq = MTP * heads
    per_group = rows * heads

    def body(*refs):
        query_refs = refs[:count]
        cache_ref, seen_ref, weight_ref = refs[count : count + 3]
        out_refs = refs[count + 3 : 2 * count + 3]
        fetched, done = refs[2 * count + 3 :]
        copy = pltpu.make_async_copy(weight_ref.at[pl.ds(span[0], span[1] - span[0])], fetched, done)
        copy.start()
        offset = lax.axis_index("ctx") * context
        total = count * per_seq
        tops, sums = [[] for _ in range(count)], [[] for _ in range(count)]
        for n in range(seqs):
            queries = jnp.concatenate(
                [q[MTP * n : MTP * (n + 1)].reshape(per_seq, width) for q in query_refs], axis=0
            )
            scores = jnp.dot(queries, cache_ref[n], preferred_element_type=f32) * SCALE
            row = lax.broadcasted_iota(jnp.int32, (total, 1), 0)
            which = (row // heads) % MTP
            limit = jnp.full((total, 1), 0, jnp.int32)
            for t in range(MTP):
                r = MTP * n + t
                limit = jnp.where(which == t, seen_ref[r : r + 1, 0:1], limit)
            place = offset + lax.broadcasted_iota(jnp.int32, (total, context), 1)
            live = place < limit
            top = jnp.max(jnp.where(live, scores, DEAD), axis=1, keepdims=True)
            probs = jnp.exp(jnp.where(live, scores - top, DEAD)).astype(bf16)
            weight = jnp.sum(probs.astype(f32), axis=1, keepdims=True)
            out = lax.dot_general(
                probs, cache_ref[n, :LATENT, :], (((1,), (1,)), ((), ())), preferred_element_type=f32
            )
            for g in range(count):
                part = slice(g * per_seq, (g + 1) * per_seq)
                out_refs[g][n * per_seq : (n + 1) * per_seq, :] = out[part].astype(bf16)
                tops[g].append(top[part])
                sums[g].append(weight[part])
        lane = lax.broadcasted_iota(jnp.int32, (LANES, LANES), 1)
        for g in range(count):
            fill = [jnp.zeros((LANES - per_group, 1), f32)] if per_group < LANES else []
            top = jnp.concatenate(tops[g] + fill, axis=0)
            weight = jnp.concatenate(sums[g] + fill, axis=0)
            table = jnp.where(lane == 0, top, jnp.where(lane == 1, weight, 0.0)).T
            for i, part in enumerate(three_parts(table[:STAT_ROWS])):
                out_refs[g][per_group:, i * LANES : (i + 1) * LANES] = part
            out_refs[g][per_group:, 3 * LANES :] = jnp.zeros((STAT_ROWS, LATENT - 3 * LANES), bf16)
        copy.wait()

    shape = jax.ShapeDtypeStruct((per_group + STAT_ROWS, LATENT), bf16)
    flops = 2 * count * rows * heads * context * (width + LATENT)
    return call(
        body,
        [shape] * count + [pltpu.VMEM((span[1] - span[0], weight.shape[1]), weight.dtype)],
        [*groups, in_vmem(cache), seen, pltpu.with_memory_space_constraint(weight, pltpu.HBM)],
        [IN_VMEM] * (count + 2) + [IN_HBM],
        [pltpu.SemaphoreType.DMA],
        limit=ATTEND_LIMIT,
        cost=(flops, 4 << 20),
    )


def join_and_project(parts, pieces, rows, heads, after):
    count, slices = len(parts), len(pieces)
    per_group = rows * heads
    _, depth, vdim = pieces[0].shape

    def body(*refs):
        part_refs, piece_refs = refs[:count], refs[count : count + slices]
        value_ref, attended = refs[count + slices + 1 :]
        me = lax.axis_index(("role", "seq"))
        tops, sums = [], []
        for ref in part_refs:
            table = sum(
                ref[per_group:, i * LANES : (i + 1) * LANES].astype(f32) for i in reversed(range(3))
            )
            table = jnp.concatenate([table, jnp.zeros((LANES - STAT_ROWS, LANES), f32)], axis=0).T
            tops.append(table[:per_group, 0:1])
            sums.append(table[:per_group, 1:2])
        highest = functools.reduce(jnp.maximum, tops)
        factors = [jnp.exp(top - highest) for top in tops]
        denom = sum(f * s for f, s in zip(factors, sums))
        numer = sum(f * ref[:per_group, :].astype(f32) for f, ref in zip(factors, part_refs))
        joined = (numer / denom).astype(bf16).astype(f32)
        for k in range(slices):
            attended[k] = joined[:, k * depth : (k + 1) * depth]
        for h in range(heads):
            total = None
            for m in range(slices):
                left = attended[me ^ m, pl.ds(h, rows, stride=heads), :].astype(bf16)
                term = jnp.dot(left, piece_refs[m][h], preferred_element_type=f32)
                total = term if total is None else total + term
            value_ref[:, h * vdim : (h + 1) * vdim] = total.astype(bf16)

    return call(
        body,
        jax.ShapeDtypeStruct((rows, heads * vdim), bf16),
        [*parts, *[in_vmem(piece) for piece in pieces], after],
        [IN_VMEM] * (count + slices + 1),
        [pltpu.VMEM((slices, per_group, depth), f32)],
        cost=(2 * rows * heads * LATENT * vdim, 4 << 20),
    )


def project_out(pieces, weights):
    count, parts = len(pieces), len(weights)
    rows, depth = pieces[0].shape
    width = weights[0].shape[1]

    def body(*refs):
        weight_refs, (out_ref, placed) = refs[count : count + parts], refs[count + parts :]
        me = lax.axis_index(("role", "seq"))
        for m in range(count):
            placed[me ^ m] = refs[m][...].astype(f32)
        values = jnp.concatenate([placed[k] for k in range(count)], axis=0).astype(bf16)
        total, start = None, 0
        for ref in weight_refs:
            term = jnp.dot(values[:, start : start + ref.shape[0]], ref[...], preferred_element_type=f32)
            total = term if total is None else total + term
            start += ref.shape[0]
        out_ref[...] = total.astype(bf16)

    return call(
        body,
        jax.ShapeDtypeStruct((count * rows, width), bf16),
        [*pieces, *[in_vmem(weight) for weight in weights]],
        [IN_VMEM] * (count + parts),
        [pltpu.VMEM((count, rows, depth), f32)],
        cost=(2 * count * rows * depth * width, 4 << 20),
    )


def gate_and_up_away(pieces, residual, gain, gate_weight, up_weight):
    count = len(pieces)
    rows, width = residual.shape
    hidden = gate_weight.shape[1]
    cores = lax.axis_size("seq")
    half = hidden // cores
    own_rows = rows // count

    def body(*refs):
        residual_ref, gain_ref, gate_ref, up_ref = refs[count : count + 4]
        send_ref, scaled_ref, squares_ref, base_ref, placed = refs[count + 4 :]
        resid = residual_ref[...].astype(f32) + sum(ref[...].astype(f32) for ref in refs[:count])
        scaled = (resid * gain_ref[...][None, :]).astype(bf16)
        scaled_ref[...] = scaled
        other = lax.axis_index("seq") ^ 1
        for k in range(cores):

            @pl.when(other == k)
            def _(k=k):
                part = slice(k * half, (k + 1) * half)
                gate = jnp.dot(scaled, gate_ref[:, part], preferred_element_type=f32)
                up = jnp.dot(scaled, up_ref[:, part], preferred_element_type=f32)
                send_ref[:, :half] = gate.astype(bf16)
                send_ref[:, half : 2 * half] = up.astype(bf16)

        for k in range(count):
            placed[k] = resid[k * own_rows : (k + 1) * own_rows]
        base_ref[...] = placed[lax.axis_index("ctx")]
        squares = jnp.sum(resid * resid, axis=1, keepdims=True)
        lane = lax.broadcasted_iota(jnp.int32, (rows, LANES), 1)
        squares_ref[...] = jnp.broadcast_to(squares, (rows, LANES))
        send_ref[:, 2 * half :] = spread(squares, lane)

    return call(
        body,
        [
            jax.ShapeDtypeStruct((rows, 2 * half + LANES), bf16),
            jax.ShapeDtypeStruct((rows, width), bf16),
            jax.ShapeDtypeStruct((rows, LANES), f32),
            jax.ShapeDtypeStruct((own_rows, width), f32),
        ],
        [*pieces, residual, gain, in_vmem(gate_weight), in_vmem(up_weight)],
        [IN_VMEM] * (count + 4),
        [pltpu.VMEM((count, own_rows, width), f32)],
        cost=(2 * rows * width * hidden, 4 << 20),
    )


def gate_and_up_here(scaled, gate_weight, up_weight):
    rows, width = scaled.shape
    hidden = gate_weight.shape[1]
    cores = lax.axis_size("seq")
    half = hidden // cores

    def body(scaled_ref, gate_ref, up_ref, keep_ref):
        me = lax.axis_index("seq")
        for k in range(cores):

            @pl.when(me == k)
            def _(k=k):
                part = slice(k * half, (k + 1) * half)
                keep_ref[:, :half] = jnp.dot(scaled_ref[...], gate_ref[:, part], preferred_element_type=f32)
                keep_ref[:, half:] = jnp.dot(scaled_ref[...], up_ref[:, part], preferred_element_type=f32)

    return call(
        body,
        jax.ShapeDtypeStruct((rows, 2 * half), f32),
        [scaled, in_vmem(gate_weight), in_vmem(up_weight)],
        [IN_VMEM] * 3,
        cost=(2 * rows * width * hidden, 4 << 20),
    )


def spread(column, lane):
    high, middle, low = three_parts(column)
    return jnp.where(
        lane == 0,
        high.astype(f32),
        jnp.where(lane == 1, middle.astype(f32), jnp.where(lane == 2, low.astype(f32), 0.0)),
    ).astype(bf16)


def add_core(keep, squares, got):
    rows, width = got.shape
    body_width = width - LANES

    def body(keep_ref, squares_ref, got_ref, sum_ref, send_ref):
        total = keep_ref[...] + got_ref[:, :body_width].astype(f32)
        both = squares_ref[:, 0:1] + jnp.sum(got_ref[:, body_width:].astype(f32), axis=1, keepdims=True)
        sum_ref[:, :body_width] = total
        sum_ref[:, body_width:] = jnp.broadcast_to(both, (rows, LANES))
        send_ref[:, :body_width] = total.astype(bf16)
        lane = lax.broadcasted_iota(jnp.int32, (rows, LANES), 1)
        send_ref[:, body_width:] = spread(both, lane)

    return call(
        body,
        [jax.ShapeDtypeStruct((rows, width), f32), jax.ShapeDtypeStruct((rows, width), bf16)],
        [keep, squares, got],
        [IN_VMEM] * 3,
        cost=(rows * width, rows * width * 8),
    )


def activate(keep, pieces, features):
    rows, width = keep.shape
    body_width = width - LANES
    half = body_width // 2

    def body(*refs):
        keep_ref, out_ref = refs[0], refs[-1]
        total = keep_ref[:, :body_width] + sum(r[:, :body_width].astype(f32) for r in refs[1:-1])
        squares = keep_ref[:, body_width : body_width + 1] + sum(
            jnp.sum(r[:, body_width:].astype(f32), axis=1, keepdims=True) for r in refs[1:-1]
        )
        scale = lax.rsqrt(squares / features + EPSILON)
        gate = total[:, :half] * scale
        up = total[:, half:] * scale
        out_ref[...] = (gate / (1.0 + jnp.exp(-gate)) * up).astype(bf16)

    return call(
        body,
        jax.ShapeDtypeStruct((rows, half), bf16),
        [keep, *pieces],
        [IN_VMEM] * (1 + len(pieces)),
        cost=(rows * width, rows * width * 8),
    )


def project_down_own(own, weight):
    rows, half = own.shape
    width = weight.shape[1]

    def body(own_ref, weight_ref, out_ref):
        start = pl.multiple_of(lax.axis_index("seq") * half, 16)
        out_ref[...] = jnp.dot(own_ref[...], weight_ref[pl.ds(start, half), :], preferred_element_type=f32)

    return call(
        body,
        jax.ShapeDtypeStruct((rows, width), f32),
        [own, in_vmem(weight)],
        [IN_VMEM] * 2,
        cost=(2 * rows * half * width, 4 << 20),
    )


def project_down_other(other, weight, partial):
    rows, half = other.shape
    width = weight.shape[1]
    count = lax.axis_size("ctx")
    own_rows = rows // count

    def body(other_ref, weight_ref, partial_ref, *refs):
        out_refs, placed = refs[:count], refs[count]
        start = pl.multiple_of((lax.axis_index("seq") ^ 1) * half, 16)
        out = partial_ref[...] + jnp.dot(
            other_ref[...], weight_ref[pl.ds(start, half), :], preferred_element_type=f32
        )
        for k in range(count):
            placed[k] = out[k * own_rows : (k + 1) * own_rows]
        me = lax.axis_index("ctx")
        for m in range(count):
            out_refs[m][...] = placed[me ^ m].astype(bf16)

    return call(
        body,
        [jax.ShapeDtypeStruct((own_rows, width), bf16)] * count,
        [other, in_vmem(weight), partial],
        [IN_VMEM] * 3,
        [pltpu.VMEM((count, own_rows, width), f32)],
        cost=(2 * rows * half * width, 4 << 20),
    )


def finish(base, pieces):
    def body(*refs):
        refs[-1][...] = (refs[0][...] + sum(r[...].astype(f32) for r in refs[1:-1])).astype(bf16)

    return call(
        body,
        jax.ShapeDtypeStruct(base.shape, bf16),
        [base, *pieces],
        [IN_VMEM] * (1 + len(pieces)),
        cost=(base.size, base.size * 8),
    )


def per_device(
    queries,
    cache,
    lengths,
    positions,
    value_up_weight,
    out_proj,
    residual,
    norm_gain,
    gate_weight,
    up_weight,
    down_weight,
):
    rows, heads, _ = queries.shape
    blocks = lax.axis_size("ctx")
    roles = lax.axis_size("role")
    members = lax.axis_size(("role", "seq"))

    evens, odds = range(2, blocks, 2), range(3, blocks, 2)

    along = listed(exchange([value_up_weight] * roles, "role"))
    groups = exchange([queries] * blocks, "ctx", [*evens, 1])
    unit = out_proj.shape[0] // 16
    own_span, early_span, even_span, odd_span, late_span = [
        (unit * first, unit * last) for first, last in ((0, 2), (2, 9), (9, 11), (11, 13), (13, 16))
    ]
    groups[0], cache_fast, seen = fetch([queries, jnp.swapaxes(cache, 1, 2)], lengths, positions)

    def attend_some(source, span):
        *outs, part = attend(list(source.values()), cache_fast, seen, out_proj, span)
        return dict(zip(source, outs)), part

    answers, own_part = attend_some({0: groups[0]}, own_span)
    (early_part,) = fetch([(out_proj, early_span)])
    relayed = {}
    for mask in evens:
        relayed[mask + 1] = xor_permute(groups[mask], "ctx", 1)
    even, even_part = attend_some({mask: groups[mask] for mask in evens}, even_span)
    answers |= exchange({0: answers[0], **even}, "ctx", evens)
    far, odd_part = attend_some({**relayed, 1: groups[1]}, odd_span)
    answers |= exchange({0: answers[0], **far}, "ctx", odds)
    answers |= exchange({0: answers[0], **far}, "ctx", [1])

    late_part, gate_fast, up_own, residual, gain = fetch(
        [(out_proj, late_span), gate_weight, value_up_weight, residual, norm_gain]
    )
    *far_rows, gain = lax.optimization_barrier((*along[1:], gain))
    across = [xor_permute(along[0], "seq", 1)]
    across += [xor_permute(piece, "seq", 1) for piece in far_rows]
    up_pieces = [up_own, *[piece for pair in zip([None, *far_rows], across) for piece in pair][1:]]
    out_parts = [own_part, early_part, even_part, odd_part, late_part]

    values = join_and_project(listed(answers), up_pieces, rows, heads, gain)
    shared = listed(exchange([values] * members, ("role", "seq")))
    product = project_out(shared, out_parts)
    up_weight, product = lax.optimization_barrier((up_weight, product))
    terms = listed(exchange([product] * blocks, "ctx"))
    (up_fast,) = fetch([up_weight])

    send, scaled, squares, base = gate_and_up_away(terms, residual, gain, gate_fast, up_fast)
    got = xor_permute(send, "seq", 1)
    keep = gate_and_up_here(scaled, gate_fast, up_fast)
    keep, send = add_core(keep, squares, got)
    down_weight, send = lax.optimization_barrier((down_weight, send))
    (down_fast,) = fetch([down_weight])
    pieces = listed(exchange([send] * roles, "role"))[1:]
    features = norm_gain.shape[0] * members
    hidden = activate(keep, pieces, features)
    other = xor_permute(hidden, "seq", 1)
    own = project_down_own(hidden, down_fast)
    last = exchange(project_down_other(other, down_fast, own), "ctx")
    return finish(base, listed(last))


def solution(mesh):
    placed = (
        P(("groups", "role", "seq"), "ctx", None),
        P(("groups", "role", "seq"), "ctx", None),
        P(("groups", "role", "seq")),
        P(("groups", "role", "seq")),
        P("ctx", ("role", "seq"), None),
        P("ctx", ("role", "seq")),
        P("groups", ("role", "seq")),
        P(("role", "seq")),
        P(("role", "seq"), "ctx"),
        P(("role", "seq"), "ctx"),
        P("ctx", ("role", "seq")),
    )


    return jax.shard_map(
        per_device,
        mesh=mesh,
        in_specs=placed,
        out_specs=P(("groups", "ctx"), ("role", "seq")),
        check_vma=False,
    )
```

```python
import functools
import math

import jax
import jax.numpy as jnp
from jax import lax
from jax.experimental import pallas as pl
from jax.experimental.pallas import tpu as pltpu
from jax.sharding import PartitionSpec as P


LATENT = 512
MTP = 2
SCALE = 0.07216878364870323
EPSILON = 1e-06
DEAD = -1e30
STAT_ROWS = 8
LANES = 128
ATTEND_LIMIT = 8 << 20
KERNEL_LIMIT = 6 << 20


f32, bf16 = jnp.float32, jnp.bfloat16
IN_VMEM = pl.BlockSpec(memory_space=pltpu.VMEM)
IN_SMEM = pl.BlockSpec(memory_space=pltpu.SMEM)
IN_HBM = pl.BlockSpec(memory_space=pltpu.HBM)


def xor_permute(x, axis, mask):
    size = lax.axis_size(axis)
    return lax.ppermute(x, axis, [(i, i ^ mask) for i in range(size)])


def exchange(pieces, axis, masks=None):
    got = {0: pieces[0]}
    for mask in masks or reversed(range(1, len(pieces))):
        got[mask] = xor_permute(pieces[mask], axis, mask)
    return got


def listed(got):
    return [got[mask] for mask in sorted(got)]


def call(body, outs, args, specs, scratch=(), limit=KERNEL_LIMIT, cost=None):
    flops, moved = cost or (0, 0)
    return pl.pallas_call(
        body,
        out_shape=outs,
        in_specs=specs,
        out_specs=jax.tree.map(lambda _: IN_VMEM, outs),
        scratch_shapes=list(scratch),
        compiler_params=pltpu.CompilerParams(vmem_limit_bytes=limit),
        cost_estimate=pl.CostEstimate(flops=flops, bytes_accessed=moved, transcendentals=0),
    )(*args)


def in_vmem(x):
    return pltpu.with_memory_space_constraint(x, pltpu.VMEM)


def three_parts(x):
    high = x.astype(bf16)
    rest = x - high.astype(f32)
    middle = rest.astype(bf16)
    return high, middle, (rest - middle.astype(f32)).astype(bf16)


def fetch(arrays, lengths=None, positions=None):
    spans = [x[1] if isinstance(x, tuple) else (0, x.shape[0]) for x in arrays]
    arrays = [x[0] if isinstance(x, tuple) else x for x in arrays]
    shapes = [(last - first, *x.shape[1:]) for x, (first, last) in zip(arrays, spans)]
    count = len(arrays)
    scalars = [] if positions is None else [lengths, positions]
    rows = positions.shape[0] if scalars else 0
    copied = count + len(scalars)

    def body(*refs):
        sources, refs = refs[:copied], refs[copied:]
        targets, refs = refs[:count], refs[count:]
        sources = [
            source if i >= count or spans[i] == (0, source.shape[0]) else source.at[pl.ds(spans[i][0], shapes[i][0])]
            for i, source in enumerate(sources)
        ]
        done, in_smem = refs[-1], refs[-1 - len(scalars) : -1]
        copies = [
            pltpu.make_async_copy(source, target, done.at[i])
            for i, (source, target) in enumerate(zip(sources, [*targets, *in_smem]))
        ]
        for copy in reversed(copies):
            copy.start()
        for copy in copies[count:]:
            copy.wait()
        if scalars:
            length_ref, position_ref = in_smem
            row = lax.broadcasted_iota(jnp.int32, (rows, LANES), 0)
            seen = jnp.zeros((rows, LANES), jnp.int32)
            for r in range(rows):
                bound = jnp.minimum(length_ref[r // MTP], position_ref[r] + 1)
                seen = jnp.where(row == r, bound, seen)
            refs[0][...] = seen
        for copy in copies[:count]:
            copy.wait()

    moved = sum(2 * math.prod(shape) * x.dtype.itemsize for shape, x in zip(shapes, arrays))
    return call(
        body,
        [pltpu.VMEM(shape, x.dtype) for shape, x in zip(shapes, arrays)]
        + ([pltpu.VMEM((rows, LANES), jnp.int32)] if scalars else []),
        [pltpu.with_memory_space_constraint(x, pltpu.HBM) for x in [*arrays, *scalars]],
        [IN_HBM] * copied,
        [pltpu.SMEM(x.shape, x.dtype) for x in scalars] + [pltpu.SemaphoreType.DMA((copied,))],
        limit=1 << 20,
        cost=(0, moved),
    )


def attend(groups, cache, seen, weight, span):
    count = len(groups)
    rows, heads, width = groups[0].shape
    seqs, _, context = cache.shape
    per_seq = MTP * heads
    per_group = rows * heads

    def body(*refs):
        query_refs = refs[:count]
        cache_ref, seen_ref, weight_ref = refs[count : count + 3]
        out_refs = refs[count + 3 : 2 * count + 3]
        fetched, done = refs[2 * count + 3 :]
        copy = pltpu.make_async_copy(weight_ref.at[pl.ds(span[0], span[1] - span[0])], fetched, done)
        copy.start()
        offset = lax.axis_index("ctx") * context
        total = count * per_seq
        tops, sums = [[] for _ in range(count)], [[] for _ in range(count)]
        for n in range(seqs):
            queries = jnp.concatenate(
                [q[MTP * n : MTP * (n + 1)].reshape(per_seq, width) for q in query_refs], axis=0
            )
            scores = jnp.dot(queries, cache_ref[n], preferred_element_type=f32) * SCALE
            row = lax.broadcasted_iota(jnp.int32, (total, 1), 0)
            which = (row // heads) % MTP
            limit = jnp.full((total, 1), 0, jnp.int32)
            for t in range(MTP):
                r = MTP * n + t
                limit = jnp.where(which == t, seen_ref[r : r + 1, 0:1], limit)
            place = offset + lax.broadcasted_iota(jnp.int32, (total, context), 1)
            live = place < limit
            top = jnp.max(jnp.where(live, scores, DEAD), axis=1, keepdims=True)
            probs = jnp.exp(jnp.where(live, scores - top, DEAD)).astype(bf16)
            weight = jnp.sum(probs.astype(f32), axis=1, keepdims=True)
            out = lax.dot_general(
                probs, cache_ref[n, :LATENT, :], (((1,), (1,)), ((), ())), preferred_element_type=f32
            )
            for g in range(count):
                part = slice(g * per_seq, (g + 1) * per_seq)
                out_refs[g][n * per_seq : (n + 1) * per_seq, :] = out[part].astype(bf16)
                tops[g].append(top[part])
                sums[g].append(weight[part])
        lane = lax.broadcasted_iota(jnp.int32, (LANES, LANES), 1)
        for g in range(count):
            fill = [jnp.zeros((LANES - per_group, 1), f32)] if per_group < LANES else []
            top = jnp.concatenate(tops[g] + fill, axis=0)
            weight = jnp.concatenate(sums[g] + fill, axis=0)
            table = jnp.where(lane == 0, top, jnp.where(lane == 1, weight, 0.0)).T
            for i, part in enumerate(three_parts(table[:STAT_ROWS])):
                out_refs[g][per_group:, i * LANES : (i + 1) * LANES] = part
            out_refs[g][per_group:, 3 * LANES :] = jnp.zeros((STAT_ROWS, LATENT - 3 * LANES), bf16)
        copy.wait()

    shape = jax.ShapeDtypeStruct((per_group + STAT_ROWS, LATENT), bf16)
    flops = 2 * count * rows * heads * context * (width + LATENT)
    return call(
        body,
        [shape] * count + [pltpu.VMEM((span[1] - span[0], weight.shape[1]), weight.dtype)],
        [*groups, in_vmem(cache), seen, pltpu.with_memory_space_constraint(weight, pltpu.HBM)],
        [IN_VMEM] * (count + 2) + [IN_HBM],
        [pltpu.SemaphoreType.DMA],
        limit=ATTEND_LIMIT,
        cost=(flops, 4 << 20),
    )


def join_and_project(parts, pieces, rows, heads, after):
    count, slices = len(parts), len(pieces)
    per_group = rows * heads
    _, depth, vdim = pieces[0].shape

    def body(*refs):
        part_refs, piece_refs = refs[:count], refs[count : count + slices]
        value_ref, attended = refs[count + slices + 1 :]
        me = lax.axis_index(("role", "seq"))
        tops, sums = [], []
        for ref in part_refs:
            table = sum(
                ref[per_group:, i * LANES : (i + 1) * LANES].astype(f32) for i in reversed(range(3))
            )
            table = jnp.concatenate([table, jnp.zeros((LANES - STAT_ROWS, LANES), f32)], axis=0).T
            tops.append(table[:per_group, 0:1])
            sums.append(table[:per_group, 1:2])
        highest = functools.reduce(jnp.maximum, tops)
        factors = [jnp.exp(top - highest) for top in tops]
        denom = sum(f * s for f, s in zip(factors, sums))
        numer = sum(f * ref[:per_group, :].astype(f32) for f, ref in zip(factors, part_refs))
        joined = (numer / denom).astype(bf16).astype(f32)
        for k in range(slices):
            attended[k] = joined[:, k * depth : (k + 1) * depth]
        for h in range(heads):
            total = None
            for m in range(slices):
                left = attended[me ^ m, pl.ds(h, rows, stride=heads), :].astype(bf16)
                term = jnp.dot(left, piece_refs[m][h], preferred_element_type=f32)
                total = term if total is None else total + term
            value_ref[:, h * vdim : (h + 1) * vdim] = total.astype(bf16)

    return call(
        body,
        jax.ShapeDtypeStruct((rows, heads * vdim), bf16),
        [*parts, *[in_vmem(piece) for piece in pieces], after],
        [IN_VMEM] * (count + slices + 1),
        [pltpu.VMEM((slices, per_group, depth), f32)],
        cost=(2 * rows * heads * LATENT * vdim, 4 << 20),
    )


def project_out(pieces, weights):
    count, parts = len(pieces), len(weights)
    rows, depth = pieces[0].shape
    width = weights[0].shape[1]

    def body(*refs):
        weight_refs, (out_ref, placed) = refs[count : count + parts], refs[count + parts :]
        me = lax.axis_index(("role", "seq"))
        for m in range(count):
            placed[me ^ m] = refs[m][...].astype(f32)
        values = jnp.concatenate([placed[k] for k in range(count)], axis=0).astype(bf16)
        total, start = None, 0
        for ref in weight_refs:
            term = jnp.dot(values[:, start : start + ref.shape[0]], ref[...], preferred_element_type=f32)
            total = term if total is None else total + term
            start += ref.shape[0]
        out_ref[...] = total.astype(bf16)

    return call(
        body,
        jax.ShapeDtypeStruct((count * rows, width), bf16),
        [*pieces, *[in_vmem(weight) for weight in weights]],
        [IN_VMEM] * (count + parts),
        [pltpu.VMEM((count, rows, depth), f32)],
        cost=(2 * count * rows * depth * width, 4 << 20),
    )


def gate_and_up_away(pieces, residual, gain, gate_weight, up_weight):
    count = len(pieces)
    rows, width = residual.shape
    hidden = gate_weight.shape[1]
    cores = lax.axis_size("seq")
    half = hidden // cores
    own_rows = rows // count

    def body(*refs):
        residual_ref, gain_ref, gate_ref, up_ref = refs[count : count + 4]
        send_ref, scaled_ref, squares_ref, base_ref, placed = refs[count + 4 :]
        resid = residual_ref[...].astype(f32) + sum(ref[...].astype(f32) for ref in refs[:count])
        scaled = (resid * gain_ref[...][None, :]).astype(bf16)
        scaled_ref[...] = scaled
        other = lax.axis_index("seq") ^ 1
        for k in range(cores):

            @pl.when(other == k)
            def _(k=k):
                part = slice(k * half, (k + 1) * half)
                gate = jnp.dot(scaled, gate_ref[:, part], preferred_element_type=f32)
                up = jnp.dot(scaled, up_ref[:, part], preferred_element_type=f32)
                send_ref[:, :half] = gate.astype(bf16)
                send_ref[:, half : 2 * half] = up.astype(bf16)

        for k in range(count):
            placed[k] = resid[k * own_rows : (k + 1) * own_rows]
        base_ref[...] = placed[lax.axis_index("ctx")]
        squares = jnp.sum(resid * resid, axis=1, keepdims=True)
        lane = lax.broadcasted_iota(jnp.int32, (rows, LANES), 1)
        squares_ref[...] = jnp.broadcast_to(squares, (rows, LANES))
        send_ref[:, 2 * half :] = spread(squares, lane)

    return call(
        body,
        [
            jax.ShapeDtypeStruct((rows, 2 * half + LANES), bf16),
            jax.ShapeDtypeStruct((rows, width), bf16),
            jax.ShapeDtypeStruct((rows, LANES), f32),
            jax.ShapeDtypeStruct((own_rows, width), f32),
        ],
        [*pieces, residual, gain, in_vmem(gate_weight), in_vmem(up_weight)],
        [IN_VMEM] * (count + 4),
        [pltpu.VMEM((count, own_rows, width), f32)],
        cost=(2 * rows * width * hidden, 4 << 20),
    )


def gate_and_up_here(scaled, gate_weight, up_weight):
    rows, width = scaled.shape
    hidden = gate_weight.shape[1]
    cores = lax.axis_size("seq")
    half = hidden // cores

    def body(scaled_ref, gate_ref, up_ref, keep_ref):
        me = lax.axis_index("seq")
        for k in range(cores):

            @pl.when(me == k)
            def _(k=k):
                part = slice(k * half, (k + 1) * half)
                keep_ref[:, :half] = jnp.dot(scaled_ref[...], gate_ref[:, part], preferred_element_type=f32)
                keep_ref[:, half:] = jnp.dot(scaled_ref[...], up_ref[:, part], preferred_element_type=f32)

    return call(
        body,
        jax.ShapeDtypeStruct((rows, 2 * half), f32),
        [scaled, in_vmem(gate_weight), in_vmem(up_weight)],
        [IN_VMEM] * 3,
        cost=(2 * rows * width * hidden, 4 << 20),
    )


def spread(column, lane):
    high, middle, low = three_parts(column)
    return jnp.where(
        lane == 0,
        high.astype(f32),
        jnp.where(lane == 1, middle.astype(f32), jnp.where(lane == 2, low.astype(f32), 0.0)),
    ).astype(bf16)


def add_core(keep, squares, got):
    rows, width = got.shape
    body_width = width - LANES

    def body(keep_ref, squares_ref, got_ref, sum_ref, send_ref):
        total = keep_ref[...] + got_ref[:, :body_width].astype(f32)
        both = squares_ref[:, 0:1] + jnp.sum(got_ref[:, body_width:].astype(f32), axis=1, keepdims=True)
        sum_ref[:, :body_width] = total
        sum_ref[:, body_width:] = jnp.broadcast_to(both, (rows, LANES))
        send_ref[:, :body_width] = total.astype(bf16)
        lane = lax.broadcasted_iota(jnp.int32, (rows, LANES), 1)
        send_ref[:, body_width:] = spread(both, lane)

    return call(
        body,
        [jax.ShapeDtypeStruct((rows, width), f32), jax.ShapeDtypeStruct((rows, width), bf16)],
        [keep, squares, got],
        [IN_VMEM] * 3,
        cost=(rows * width, rows * width * 8),
    )


def activate(keep, pieces, features):
    rows, width = keep.shape
    body_width = width - LANES
    half = body_width // 2

    def body(*refs):
        keep_ref, out_ref = refs[0], refs[-1]
        total = keep_ref[:, :body_width] + sum(r[:, :body_width].astype(f32) for r in refs[1:-1])
        squares = keep_ref[:, body_width : body_width + 1] + sum(
            jnp.sum(r[:, body_width:].astype(f32), axis=1, keepdims=True) for r in refs[1:-1]
        )
        scale = lax.rsqrt(squares / features + EPSILON)
        gate = total[:, :half] * scale
        up = total[:, half:] * scale
        out_ref[...] = (gate / (1.0 + jnp.exp(-gate)) * up).astype(bf16)

    return call(
        body,
        jax.ShapeDtypeStruct((rows, half), bf16),
        [keep, *pieces],
        [IN_VMEM] * (1 + len(pieces)),
        cost=(rows * width, rows * width * 8),
    )


def project_down_own(own, weight):
    rows, half = own.shape
    width = weight.shape[1]

    def body(own_ref, weight_ref, out_ref):
        start = pl.multiple_of(lax.axis_index("seq") * half, 16)
        out_ref[...] = jnp.dot(own_ref[...], weight_ref[pl.ds(start, half), :], preferred_element_type=f32)

    return call(
        body,
        jax.ShapeDtypeStruct((rows, width), f32),
        [own, in_vmem(weight)],
        [IN_VMEM] * 2,
        cost=(2 * rows * half * width, 4 << 20),
    )


def project_down_other(other, weight, partial):
    rows, half = other.shape
    width = weight.shape[1]
    count = lax.axis_size("ctx")
    own_rows = rows // count

    def body(other_ref, weight_ref, partial_ref, *refs):
        out_refs, placed = refs[:count], refs[count]
        start = pl.multiple_of((lax.axis_index("seq") ^ 1) * half, 16)
        out = partial_ref[...] + jnp.dot(
            other_ref[...], weight_ref[pl.ds(start, half), :], preferred_element_type=f32
        )
        for k in range(count):
            placed[k] = out[k * own_rows : (k + 1) * own_rows]
        me = lax.axis_index("ctx")
        for m in range(count):
            out_refs[m][...] = placed[me ^ m].astype(bf16)

    return call(
        body,
        [jax.ShapeDtypeStruct((own_rows, width), bf16)] * count,
        [other, in_vmem(weight), partial],
        [IN_VMEM] * 3,
        [pltpu.VMEM((count, own_rows, width), f32)],
        cost=(2 * rows * half * width, 4 << 20),
    )


def finish(base, pieces):
    def body(*refs):
        refs[-1][...] = (refs[0][...] + sum(r[...].astype(f32) for r in refs[1:-1])).astype(bf16)

    return call(
        body,
        jax.ShapeDtypeStruct(base.shape, bf16),
        [base, *pieces],
        [IN_VMEM] * (1 + len(pieces)),
        cost=(base.size, base.size * 8),
    )


def per_device(
    queries,
    cache,
    lengths,
    positions,
    value_up_weight,
    out_proj,
    residual,
    norm_gain,
    gate_weight,
    up_weight,
    down_weight,
):
    rows, heads, _ = queries.shape
    blocks = lax.axis_size("ctx")
    roles = lax.axis_size("role")
    members = lax.axis_size(("role", "seq"))

    evens, odds = range(2, blocks, 2), range(3, blocks, 2)

    along = listed(exchange([value_up_weight] * roles, "role"))
    groups = exchange([queries] * blocks, "ctx", [*evens, 1])
    unit = out_proj.shape[0] // 16
    cuts = [unit * k for k in (0, 2, 6, 8, 10, 13, 16)]
    own_span, early_span, even_span, odd_span, late_span, last_span = zip(cuts, cuts[1:])
    groups[0], cache_fast, seen = fetch([queries, jnp.swapaxes(cache, 1, 2)], lengths, positions)

    def attend_some(source, span):
        *outs, part = attend(list(source.values()), cache_fast, seen, out_proj, span)
        return dict(zip(source, outs)), part

    answers, own_part = attend_some({0: groups[0]}, own_span)
    (early_part,) = fetch([(out_proj, early_span)])
    relayed = {}
    for mask in evens:
        relayed[mask + 1] = xor_permute(groups[mask], "ctx", 1)
    even, even_part = attend_some({mask: groups[mask] for mask in evens}, even_span)
    answers |= exchange({0: answers[0], **even}, "ctx", evens)
    far, odd_part = attend_some({**relayed, 1: groups[1]}, odd_span)
    answers |= exchange({0: answers[0], **far}, "ctx", odds)
    answers |= exchange({0: answers[0], **far}, "ctx", [1])

    gate_fast, up_own, residual, gain = fetch([gate_weight, value_up_weight, residual, norm_gain])
    *far_rows, gain = lax.optimization_barrier((*along[1:], gain))
    across = [xor_permute(along[0], "seq", 1)]
    across += [xor_permute(piece, "seq", 1) for piece in far_rows]
    up_pieces = [up_own, *[piece for pair in zip([None, *far_rows], across) for piece in pair][1:]]
    (late_part,) = fetch([(out_proj, late_span)])

    values = join_and_project(listed(answers), up_pieces, rows, heads, gain)
    last_out, values = lax.optimization_barrier((out_proj, values))
    shared = listed(exchange([values] * members, ("role", "seq")))
    (last_part,) = fetch([(last_out, last_span)])
    product = project_out(shared, [own_part, early_part, even_part, odd_part, late_part, last_part])
    up_weight, product = lax.optimization_barrier((up_weight, product))
    terms = listed(exchange([product] * blocks, "ctx"))
    (up_fast,) = fetch([up_weight])

    send, scaled, squares, base = gate_and_up_away(terms, residual, gain, gate_fast, up_fast)
    got = xor_permute(send, "seq", 1)
    keep = gate_and_up_here(scaled, gate_fast, up_fast)
    keep, send = add_core(keep, squares, got)
    down_weight, send = lax.optimization_barrier((down_weight, send))
    (down_fast,) = fetch([down_weight])
    pieces = listed(exchange([send] * roles, "role"))[1:]
    features = norm_gain.shape[0] * members
    hidden = activate(keep, pieces, features)
    other = xor_permute(hidden, "seq", 1)
    own = project_down_own(hidden, down_fast)
    last = exchange(project_down_other(other, down_fast, own), "ctx")
    return finish(base, listed(last))


def solution(mesh):
    placed = (
        P(("groups", "role", "seq"), "ctx", None),
        P(("groups", "role", "seq"), "ctx", None),
        P(("groups", "role", "seq")),
        P(("groups", "role", "seq")),
        P("ctx", ("role", "seq"), None),
        P("ctx", ("role", "seq")),
        P("groups", ("role", "seq")),
        P(("role", "seq")),
        P(("role", "seq"), "ctx"),
        P(("role", "seq"), "ctx"),
        P("ctx", ("role", "seq")),
    )


    return jax.shard_map(
        per_device,
        mesh=mesh,
        in_specs=placed,
        out_specs=P(("groups", "ctx"), ("role", "seq")),
        check_vma=False,
    )
```

```python
import functools

import jax
import jax.numpy as jnp
from jax import lax
from jax.experimental import pallas as pl
from jax.experimental.pallas import tpu as pltpu
from jax.sharding import PartitionSpec as P


LATENT = 512
MTP = 2
SCALE = 0.07216878364870323
EPSILON = 1e-06
DEAD = -1e30
STAT_ROWS = 8
LANES = 128
ATTEND_LIMIT = 8 << 20
KERNEL_LIMIT = 6 << 20


f32, bf16 = jnp.float32, jnp.bfloat16
IN_VMEM = pl.BlockSpec(memory_space=pltpu.VMEM)
IN_SMEM = pl.BlockSpec(memory_space=pltpu.SMEM)
IN_HBM = pl.BlockSpec(memory_space=pltpu.HBM)


def xor_permute(x, axis, mask):
    size = lax.axis_size(axis)
    return lax.ppermute(x, axis, [(i, i ^ mask) for i in range(size)])


def exchange(pieces, axis, masks=None):
    got = {0: pieces[0]}
    for mask in masks or reversed(range(1, len(pieces))):
        got[mask] = xor_permute(pieces[mask], axis, mask)
    return got


def listed(got):
    return [got[mask] for mask in sorted(got)]


def call(body, outs, args, specs, scratch=(), limit=KERNEL_LIMIT, cost=None):
    flops, moved = cost or (0, 0)
    return pl.pallas_call(
        body,
        out_shape=outs,
        in_specs=specs,
        out_specs=jax.tree.map(lambda _: IN_VMEM, outs),
        scratch_shapes=list(scratch),
        compiler_params=pltpu.CompilerParams(vmem_limit_bytes=limit),
        cost_estimate=pl.CostEstimate(flops=flops, bytes_accessed=moved, transcendentals=0),
    )(*args)


def in_vmem(x):
    return pltpu.with_memory_space_constraint(x, pltpu.VMEM)


def three_parts(x):
    high = x.astype(bf16)
    rest = x - high.astype(f32)
    middle = rest.astype(bf16)
    return high, middle, (rest - middle.astype(f32)).astype(bf16)


def fetch_rows(array, first, last):
    def body(source, target, done):
        copy = pltpu.make_async_copy(source.at[pl.ds(first, last - first)], target, done)
        copy.start()
        copy.wait()

    shape = (last - first, *array.shape[1:])
    return call(
        body,
        pltpu.VMEM(shape, array.dtype),
        [pltpu.with_memory_space_constraint(array, pltpu.HBM)],
        [IN_HBM],
        [pltpu.SemaphoreType.DMA],
        limit=1 << 20,
        cost=(0, 4 * shape[0] * array.shape[1]),
    )


def fetch(arrays, lengths, positions):
    count = len(arrays)
    scalars = [lengths, positions]
    rows = positions.shape[0]
    copied = count + len(scalars)

    def body(*refs):
        sources, refs = refs[:copied], refs[copied:]
        targets, refs = refs[:count], refs[count:]
        done, in_smem = refs[-1], refs[-1 - len(scalars) : -1]
        copies = [
            pltpu.make_async_copy(source, target, done.at[i])
            for i, (source, target) in enumerate(zip(sources, [*targets, *in_smem]))
        ]
        for copy in reversed(copies):
            copy.start()
        for copy in copies[count:]:
            copy.wait()
        length_ref, position_ref = in_smem
        row = lax.broadcasted_iota(jnp.int32, (rows, LANES), 0)
        seen = jnp.zeros((rows, LANES), jnp.int32)
        for r in range(rows):
            bound = jnp.minimum(length_ref[r // MTP], position_ref[r] + 1)
            seen = jnp.where(row == r, bound, seen)
        refs[0][...] = seen
        for copy in copies[:count]:
            copy.wait()

    moved = sum(2 * x.size * x.dtype.itemsize for x in arrays)
    return call(
        body,
        [pltpu.VMEM(x.shape, x.dtype) for x in arrays]
        + [pltpu.VMEM((rows, LANES), jnp.int32)],
        [pltpu.with_memory_space_constraint(x, pltpu.HBM) for x in [*arrays, *scalars]],
        [IN_HBM] * copied,
        [pltpu.SMEM(x.shape, x.dtype) for x in scalars] + [pltpu.SemaphoreType.DMA((copied,))],
        limit=1 << 20,
        cost=(0, moved),
    )


def attend(groups, cache, seen):
    count = len(groups)
    rows, heads, width = groups[0].shape
    seqs, _, context = cache.shape
    per_seq = MTP * heads
    per_group = rows * heads

    def body(*refs):
        query_refs = refs[:count]
        cache_ref, seen_ref = refs[count : count + 2]
        out_refs = refs[count + 2 :]
        offset = lax.axis_index("ctx") * context
        total = count * per_seq
        tops, sums = [[] for _ in range(count)], [[] for _ in range(count)]
        for n in range(seqs):
            queries = jnp.concatenate(
                [q[MTP * n : MTP * (n + 1)].reshape(per_seq, width) for q in query_refs], axis=0
            )
            scores = jnp.dot(queries, cache_ref[n], preferred_element_type=f32) * SCALE
            row = lax.broadcasted_iota(jnp.int32, (total, 1), 0)
            which = (row // heads) % MTP
            limit = jnp.full((total, 1), 0, jnp.int32)
            for t in range(MTP):
                r = MTP * n + t
                limit = jnp.where(which == t, seen_ref[r : r + 1, 0:1], limit)
            place = offset + lax.broadcasted_iota(jnp.int32, (total, context), 1)
            live = place < limit
            top = jnp.max(jnp.where(live, scores, DEAD), axis=1, keepdims=True)
            probs = jnp.exp(jnp.where(live, scores - top, DEAD)).astype(bf16)
            weight = jnp.sum(probs.astype(f32), axis=1, keepdims=True)
            out = lax.dot_general(
                probs, cache_ref[n, :LATENT, :], (((1,), (1,)), ((), ())), preferred_element_type=f32
            )
            for g in range(count):
                part = slice(g * per_seq, (g + 1) * per_seq)
                out_refs[g][n * per_seq : (n + 1) * per_seq, :] = out[part].astype(bf16)
                tops[g].append(top[part])
                sums[g].append(weight[part])
        lane = lax.broadcasted_iota(jnp.int32, (LANES, LANES), 1)
        for g in range(count):
            fill = [jnp.zeros((LANES - per_group, 1), f32)] if per_group < LANES else []
            top = jnp.concatenate(tops[g] + fill, axis=0)
            weight = jnp.concatenate(sums[g] + fill, axis=0)
            table = jnp.where(lane == 0, top, jnp.where(lane == 1, weight, 0.0)).T
            for i, part in enumerate(three_parts(table[:STAT_ROWS])):
                out_refs[g][per_group:, i * LANES : (i + 1) * LANES] = part
            out_refs[g][per_group:, 3 * LANES :] = jnp.zeros((STAT_ROWS, LATENT - 3 * LANES), bf16)

    shape = jax.ShapeDtypeStruct((per_group + STAT_ROWS, LATENT), bf16)
    flops = 2 * count * rows * heads * context * (width + LATENT)
    return call(
        body,
        [shape] * count,
        [*groups, in_vmem(cache), seen],
        [IN_VMEM] * (count + 2),
        limit=ATTEND_LIMIT,
        cost=(flops, 4 << 20),
    )


def join_and_project(parts, pieces, rows, heads):
    count, slices = len(parts), len(pieces)
    per_group = rows * heads
    _, depth, vdim = pieces[0].shape

    def body(*refs):
        part_refs, piece_refs = refs[:count], refs[count : count + slices]
        value_ref, attended = refs[count + slices :]
        me = lax.axis_index(("role", "seq"))
        tops, sums = [], []
        for ref in part_refs:
            table = sum(
                ref[per_group:, i * LANES : (i + 1) * LANES].astype(f32) for i in reversed(range(3))
            )
            table = jnp.concatenate([table, jnp.zeros((LANES - STAT_ROWS, LANES), f32)], axis=0).T
            tops.append(table[:per_group, 0:1])
            sums.append(table[:per_group, 1:2])
        highest = functools.reduce(jnp.maximum, tops)
        factors = [jnp.exp(top - highest) for top in tops]
        denom = sum(f * s for f, s in zip(factors, sums))
        numer = sum(f * ref[:per_group, :].astype(f32) for f, ref in zip(factors, part_refs))
        joined = (numer / denom).astype(bf16).astype(f32)
        for k in range(slices):
            attended[k] = joined[:, k * depth : (k + 1) * depth]
        for h in range(heads):
            total = None
            for m in range(slices):
                left = attended[me ^ m, pl.ds(h, rows, stride=heads), :].astype(bf16)
                term = jnp.dot(left, piece_refs[m][h], preferred_element_type=f32)
                total = term if total is None else total + term
            value_ref[:, h * vdim : (h + 1) * vdim] = total.astype(bf16)

    return call(
        body,
        jax.ShapeDtypeStruct((rows, heads * vdim), bf16),
        [*parts, *[in_vmem(piece) for piece in pieces]],
        [IN_VMEM] * (count + slices),
        [pltpu.VMEM((slices, per_group, depth), f32)],
        cost=(2 * rows * heads * LATENT * vdim, 4 << 20),
    )


def project_out(pieces, weights):
    count, parts = len(pieces), len(weights)
    rows, depth = pieces[0].shape
    width = weights[0].shape[1]

    def body(*refs):
        weight_refs, (out_ref, placed) = refs[count : count + parts], refs[count + parts :]
        me = lax.axis_index(("role", "seq"))
        for m in range(count):
            placed[me ^ m] = refs[m][...].astype(f32)
        values = jnp.concatenate([placed[k] for k in range(count)], axis=0).astype(bf16)
        total, start = None, 0
        for ref in weight_refs:
            term = jnp.dot(values[:, start : start + ref.shape[0]], ref[...], preferred_element_type=f32)
            total = term if total is None else total + term
            start += ref.shape[0]
        out_ref[...] = total.astype(bf16)

    return call(
        body,
        jax.ShapeDtypeStruct((count * rows, width), bf16),
        [*pieces, *[in_vmem(weight) for weight in weights]],
        [IN_VMEM] * (count + parts),
        [pltpu.VMEM((count, rows, depth), f32)],
        cost=(2 * count * rows * depth * width, 4 << 20),
    )


def gate_and_up_away(pieces, residual, gain, gate_weight, up_weight):
    count = len(pieces)
    rows, width = residual.shape
    hidden = gate_weight.shape[1]
    cores = lax.axis_size("seq")
    half = hidden // cores
    own_rows = rows // count

    def body(*refs):
        residual_ref, gain_ref, gate_ref, up_ref = refs[count : count + 4]
        send_ref, scaled_ref, squares_ref, base_ref, placed = refs[count + 4 :]
        resid = residual_ref[...].astype(f32) + sum(ref[...].astype(f32) for ref in refs[:count])
        scaled = (resid * gain_ref[...][None, :]).astype(bf16)
        scaled_ref[...] = scaled
        other = lax.axis_index("seq") ^ 1
        for k in range(cores):

            @pl.when(other == k)
            def _(k=k):
                part = slice(k * half, (k + 1) * half)
                gate = jnp.dot(scaled, gate_ref[:, part], preferred_element_type=f32)
                up = jnp.dot(scaled, up_ref[:, part], preferred_element_type=f32)
                send_ref[:, :half] = gate.astype(bf16)
                send_ref[:, half : 2 * half] = up.astype(bf16)

        for k in range(count):
            placed[k] = resid[k * own_rows : (k + 1) * own_rows]
        base_ref[...] = placed[lax.axis_index("ctx")]
        squares = jnp.sum(resid * resid, axis=1, keepdims=True)
        lane = lax.broadcasted_iota(jnp.int32, (rows, LANES), 1)
        squares_ref[...] = jnp.broadcast_to(squares, (rows, LANES))
        send_ref[:, 2 * half :] = spread(squares, lane)

    return call(
        body,
        [
            jax.ShapeDtypeStruct((rows, 2 * half + LANES), bf16),
            jax.ShapeDtypeStruct((rows, width), bf16),
            jax.ShapeDtypeStruct((rows, LANES), f32),
            jax.ShapeDtypeStruct((own_rows, width), f32),
        ],
        [*pieces, residual, gain, in_vmem(gate_weight), in_vmem(up_weight)],
        [IN_VMEM] * (count + 4),
        [pltpu.VMEM((count, own_rows, width), f32)],
        cost=(2 * rows * width * hidden, 4 << 20),
    )


def gate_and_up_here(scaled, gate_weight, up_weight):
    rows, width = scaled.shape
    hidden = gate_weight.shape[1]
    cores = lax.axis_size("seq")
    half = hidden // cores

    def body(scaled_ref, gate_ref, up_ref, keep_ref):
        me = lax.axis_index("seq")
        for k in range(cores):

            @pl.when(me == k)
            def _(k=k):
                part = slice(k * half, (k + 1) * half)
                keep_ref[:, :half] = jnp.dot(scaled_ref[...], gate_ref[:, part], preferred_element_type=f32)
                keep_ref[:, half:] = jnp.dot(scaled_ref[...], up_ref[:, part], preferred_element_type=f32)

    return call(
        body,
        jax.ShapeDtypeStruct((rows, 2 * half), f32),
        [scaled, in_vmem(gate_weight), in_vmem(up_weight)],
        [IN_VMEM] * 3,
        cost=(2 * rows * width * hidden, 4 << 20),
    )


def spread(column, lane):
    high, middle, low = three_parts(column)
    return jnp.where(
        lane == 0,
        high.astype(f32),
        jnp.where(lane == 1, middle.astype(f32), jnp.where(lane == 2, low.astype(f32), 0.0)),
    ).astype(bf16)


def add_core(keep, squares, got):
    rows, width = got.shape
    body_width = width - LANES

    def body(keep_ref, squares_ref, got_ref, sum_ref, send_ref):
        total = keep_ref[...] + got_ref[:, :body_width].astype(f32)
        both = squares_ref[:, 0:1] + jnp.sum(got_ref[:, body_width:].astype(f32), axis=1, keepdims=True)
        sum_ref[:, :body_width] = total
        sum_ref[:, body_width:] = jnp.broadcast_to(both, (rows, LANES))
        send_ref[:, :body_width] = total.astype(bf16)
        lane = lax.broadcasted_iota(jnp.int32, (rows, LANES), 1)
        send_ref[:, body_width:] = spread(both, lane)

    return call(
        body,
        [jax.ShapeDtypeStruct((rows, width), f32), jax.ShapeDtypeStruct((rows, width), bf16)],
        [keep, squares, got],
        [IN_VMEM] * 3,
        cost=(rows * width, rows * width * 8),
    )


def activate(keep, pieces, features):
    rows, width = keep.shape
    body_width = width - LANES
    half = body_width // 2

    def body(*refs):
        keep_ref, out_ref = refs[0], refs[-1]
        total = keep_ref[:, :body_width] + sum(r[:, :body_width].astype(f32) for r in refs[1:-1])
        squares = keep_ref[:, body_width : body_width + 1] + sum(
            jnp.sum(r[:, body_width:].astype(f32), axis=1, keepdims=True) for r in refs[1:-1]
        )
        scale = lax.rsqrt(squares / features + EPSILON)
        gate = total[:, :half] * scale
        up = total[:, half:] * scale
        out_ref[...] = (gate / (1.0 + jnp.exp(-gate)) * up).astype(bf16)

    return call(
        body,
        jax.ShapeDtypeStruct((rows, half), bf16),
        [keep, *pieces],
        [IN_VMEM] * (1 + len(pieces)),
        cost=(rows * width, rows * width * 8),
    )


def project_down_own(own, weight):
    rows, half = own.shape
    width = weight.shape[1]

    def body(own_ref, weight_ref, out_ref):
        start = pl.multiple_of(lax.axis_index("seq") * half, 16)
        out_ref[...] = jnp.dot(own_ref[...], weight_ref[pl.ds(start, half), :], preferred_element_type=f32)

    return call(
        body,
        jax.ShapeDtypeStruct((rows, width), f32),
        [own, in_vmem(weight)],
        [IN_VMEM] * 2,
        cost=(2 * rows * half * width, 4 << 20),
    )


def project_down_other(other, weight, partial):
    rows, half = other.shape
    width = weight.shape[1]
    count = lax.axis_size("ctx")
    own_rows = rows // count

    def body(other_ref, weight_ref, partial_ref, *refs):
        out_refs, placed = refs[:count], refs[count]
        start = pl.multiple_of((lax.axis_index("seq") ^ 1) * half, 16)
        out = partial_ref[...] + jnp.dot(
            other_ref[...], weight_ref[pl.ds(start, half), :], preferred_element_type=f32
        )
        for k in range(count):
            placed[k] = out[k * own_rows : (k + 1) * own_rows]
        me = lax.axis_index("ctx")
        for m in range(count):
            out_refs[m][...] = placed[me ^ m].astype(bf16)

    return call(
        body,
        [jax.ShapeDtypeStruct((own_rows, width), bf16)] * count,
        [other, in_vmem(weight), partial],
        [IN_VMEM] * 3,
        [pltpu.VMEM((count, own_rows, width), f32)],
        cost=(2 * rows * half * width, 4 << 20),
    )


def finish(base, pieces):
    def body(*refs):
        refs[-1][...] = (refs[0][...] + sum(r[...].astype(f32) for r in refs[1:-1])).astype(bf16)

    return call(
        body,
        jax.ShapeDtypeStruct(base.shape, bf16),
        [base, *pieces],
        [IN_VMEM] * (1 + len(pieces)),
        cost=(base.size, base.size * 8),
    )


def per_device(
    queries,
    cache,
    lengths,
    positions,
    value_up_weight,
    out_proj,
    residual,
    norm_gain,
    gate_weight,
    up_weight,
    down_weight,
):
    rows, heads, _ = queries.shape
    blocks = lax.axis_size("ctx")
    roles = lax.axis_size("role")
    members = lax.axis_size(("role", "seq"))

    evens, odds = range(2, blocks, 2), range(3, blocks, 2)

    along = listed(exchange([value_up_weight] * roles, "role"))
    groups = exchange([queries] * blocks, "ctx", [*evens, 1])
    groups[0], cache_fast, seen = fetch([queries, jnp.swapaxes(cache, 1, 2)], lengths, positions)

    def attend_some(source):
        return dict(zip(source, attend(list(source.values()), cache_fast, seen)))

    answers = attend_some({0: groups[0]})
    relayed = {}
    for mask in evens:
        relayed[mask + 1] = xor_permute(groups[mask], "ctx", 1)
    even = attend_some({mask: groups[mask] for mask in evens})
    answers |= exchange({0: answers[0], **even}, "ctx", evens)
    far = attend_some({**relayed, 1: groups[1]})
    answers |= exchange({0: answers[0], **far}, "ctx", odds)
    answers |= exchange({0: answers[0], **far}, "ctx", [1])

    cut = out_proj.shape[0] // 8 * 5
    out_a = fetch_rows(out_proj, 0, cut)
    *along, out_a = lax.optimization_barrier((*along, out_a))
    across = [xor_permute(piece, "seq", 1) for piece in along]
    out_b = fetch_rows(out_proj, cut, out_proj.shape[0])
    up_pieces = [piece for pair in zip(along, across) for piece in pair]

    values = join_and_project(listed(answers), up_pieces, rows, heads)
    shared = listed(exchange([values] * members, ("role", "seq")))
    terms = listed(exchange([project_out(shared, [out_a, out_b])] * blocks, "ctx"))
    send, scaled, squares, base = gate_and_up_away(terms, residual, norm_gain, gate_weight, up_weight)
    got = xor_permute(send, "seq", 1)
    keep = gate_and_up_here(scaled, gate_weight, up_weight)
    keep, send = add_core(keep, squares, got)
    pieces = listed(exchange([send] * roles, "role"))[1:]
    features = norm_gain.shape[0] * members
    hidden = activate(keep, pieces, features)
    other = xor_permute(hidden, "seq", 1)
    own = project_down_own(hidden, down_weight)
    last = exchange(project_down_other(other, down_weight, own), "ctx")
    return finish(base, listed(last))


def solution(mesh):
    placed = (
        P(("groups", "role", "seq"), "ctx", None),
        P(("groups", "role", "seq"), "ctx", None),
        P(("groups", "role", "seq")),
        P(("groups", "role", "seq")),
        P("ctx", ("role", "seq"), None),
        P("ctx", ("role", "seq")),
        P("groups", ("role", "seq")),
        P(("role", "seq")),
        P(("role", "seq"), "ctx"),
        P(("role", "seq"), "ctx"),
        P("ctx", ("role", "seq")),
    )


    return jax.shard_map(
        per_device,
        mesh=mesh,
        in_specs=placed,
        out_specs=P(("groups", "ctx"), ("role", "seq")),
        check_vma=False,
    )
```

```python
import functools
import math

import jax
import jax.numpy as jnp
from jax import lax
from jax.experimental import pallas as pl
from jax.experimental.pallas import tpu as pltpu
from jax.sharding import PartitionSpec as P


LATENT = 512
MTP = 2
SCALE = 0.07216878364870323
EPSILON = 1e-06
DEAD = -1e30
STAT_ROWS = 8
LANES = 128
ATTEND_LIMIT = 8 << 20
KERNEL_LIMIT = 6 << 20


f32, bf16 = jnp.float32, jnp.bfloat16
IN_VMEM = pl.BlockSpec(memory_space=pltpu.VMEM)
IN_SMEM = pl.BlockSpec(memory_space=pltpu.SMEM)
IN_HBM = pl.BlockSpec(memory_space=pltpu.HBM)


def xor_permute(x, axis, mask):
    size = lax.axis_size(axis)
    return lax.ppermute(x, axis, [(i, i ^ mask) for i in range(size)])


def exchange(pieces, axis, masks=None):
    got = {0: pieces[0]}
    for mask in masks or reversed(range(1, len(pieces))):
        got[mask] = xor_permute(pieces[mask], axis, mask)
    return got


def listed(got):
    return [got[mask] for mask in sorted(got)]


def call(body, outs, args, specs, scratch=(), limit=KERNEL_LIMIT, cost=None):
    flops, moved = cost or (0, 0)
    return pl.pallas_call(
        body,
        out_shape=outs,
        in_specs=specs,
        out_specs=jax.tree.map(lambda _: IN_VMEM, outs),
        scratch_shapes=list(scratch),
        compiler_params=pltpu.CompilerParams(vmem_limit_bytes=limit),
        cost_estimate=pl.CostEstimate(flops=flops, bytes_accessed=moved, transcendentals=0),
    )(*args)


def in_vmem(x):
    return pltpu.with_memory_space_constraint(x, pltpu.VMEM)


def three_parts(x):
    high = x.astype(bf16)
    rest = x - high.astype(f32)
    middle = rest.astype(bf16)
    return high, middle, (rest - middle.astype(f32)).astype(bf16)


def fetch(arrays, lengths=None, positions=None):
    spans = [x[1] if isinstance(x, tuple) else (0, x.shape[0]) for x in arrays]
    arrays = [x[0] if isinstance(x, tuple) else x for x in arrays]
    shapes = [(last - first, *x.shape[1:]) for x, (first, last) in zip(arrays, spans)]
    count = len(arrays)
    scalars = [] if positions is None else [lengths, positions]
    rows = positions.shape[0] if scalars else 0
    copied = count + len(scalars)

    def body(*refs):
        sources, refs = refs[:copied], refs[copied:]
        targets, refs = refs[:count], refs[count:]
        sources = [
            source if i >= count or spans[i] == (0, source.shape[0]) else source.at[pl.ds(spans[i][0], shapes[i][0])]
            for i, source in enumerate(sources)
        ]
        done, in_smem = refs[-1], refs[-1 - len(scalars) : -1]
        copies = [
            pltpu.make_async_copy(source, target, done.at[i])
            for i, (source, target) in enumerate(zip(sources, [*targets, *in_smem]))
        ]
        for copy in reversed(copies):
            copy.start()
        for copy in copies[count:]:
            copy.wait()
        if scalars:
            length_ref, position_ref = in_smem
            row = lax.broadcasted_iota(jnp.int32, (rows, LANES), 0)
            seen = jnp.zeros((rows, LANES), jnp.int32)
            for r in range(rows):
                bound = jnp.minimum(length_ref[r // MTP], position_ref[r] + 1)
                seen = jnp.where(row == r, bound, seen)
            refs[0][...] = seen
        for copy in copies[:count]:
            copy.wait()

    moved = sum(2 * math.prod(shape) * x.dtype.itemsize for shape, x in zip(shapes, arrays))
    return call(
        body,
        [pltpu.VMEM(shape, x.dtype) for shape, x in zip(shapes, arrays)]
        + ([pltpu.VMEM((rows, LANES), jnp.int32)] if scalars else []),
        [pltpu.with_memory_space_constraint(x, pltpu.HBM) for x in [*arrays, *scalars]],
        [IN_HBM] * copied,
        [pltpu.SMEM(x.shape, x.dtype) for x in scalars] + [pltpu.SemaphoreType.DMA((copied,))],
        limit=1 << 20,
        cost=(0, moved),
    )


def attend(groups, cache, seen, weight, span):
    count = len(groups)
    rows, heads, width = groups[0].shape
    seqs, _, context = cache.shape
    per_seq = MTP * heads
    per_group = rows * heads

    def body(*refs):
        query_refs = refs[:count]
        cache_ref, seen_ref, weight_ref = refs[count : count + 3]
        out_refs = refs[count + 3 : 2 * count + 3]
        fetched, done = refs[2 * count + 3 :]
        copy = pltpu.make_async_copy(weight_ref.at[pl.ds(span[0], span[1] - span[0])], fetched, done)
        copy.start()
        offset = lax.axis_index("ctx") * context
        total = count * per_seq
        tops, sums = [[] for _ in range(count)], [[] for _ in range(count)]
        for n in range(seqs):
            queries = jnp.concatenate(
                [q[MTP * n : MTP * (n + 1)].reshape(per_seq, width) for q in query_refs], axis=0
            )
            scores = jnp.dot(queries, cache_ref[n], preferred_element_type=f32) * SCALE
            row = lax.broadcasted_iota(jnp.int32, (total, 1), 0)
            which = (row // heads) % MTP
            limit = jnp.full((total, 1), 0, jnp.int32)
            for t in range(MTP):
                r = MTP * n + t
                limit = jnp.where(which == t, seen_ref[r : r + 1, 0:1], limit)
            place = offset + lax.broadcasted_iota(jnp.int32, (total, context), 1)
            live = place < limit
            top = jnp.max(jnp.where(live, scores, DEAD), axis=1, keepdims=True)
            probs = jnp.exp(jnp.where(live, scores - top, DEAD)).astype(bf16)
            weight = jnp.sum(probs.astype(f32), axis=1, keepdims=True)
            out = lax.dot_general(
                probs, cache_ref[n, :LATENT, :], (((1,), (1,)), ((), ())), preferred_element_type=f32
            )
            for g in range(count):
                part = slice(g * per_seq, (g + 1) * per_seq)
                out_refs[g][n * per_seq : (n + 1) * per_seq, :] = out[part].astype(bf16)
                tops[g].append(top[part])
                sums[g].append(weight[part])
        lane = lax.broadcasted_iota(jnp.int32, (LANES, LANES), 1)
        for g in range(count):
            fill = [jnp.zeros((LANES - per_group, 1), f32)] if per_group < LANES else []
            top = jnp.concatenate(tops[g] + fill, axis=0)
            weight = jnp.concatenate(sums[g] + fill, axis=0)
            table = jnp.where(lane == 0, top, jnp.where(lane == 1, weight, 0.0)).T
            for i, part in enumerate(three_parts(table[:STAT_ROWS])):
                out_refs[g][per_group:, i * LANES : (i + 1) * LANES] = part
            out_refs[g][per_group:, 3 * LANES :] = jnp.zeros((STAT_ROWS, LATENT - 3 * LANES), bf16)
        copy.wait()

    shape = jax.ShapeDtypeStruct((per_group + STAT_ROWS, LATENT), bf16)
    flops = 2 * count * rows * heads * context * (width + LATENT)
    return call(
        body,
        [shape] * count + [pltpu.VMEM((span[1] - span[0], weight.shape[1]), weight.dtype)],
        [*groups, in_vmem(cache), seen, pltpu.with_memory_space_constraint(weight, pltpu.HBM)],
        [IN_VMEM] * (count + 2) + [IN_HBM],
        [pltpu.SemaphoreType.DMA],
        limit=ATTEND_LIMIT,
        cost=(flops, 4 << 20),
    )


def join_blocks(parts, pieces, rows, heads, slices):
    count, near = len(parts), len(pieces)
    per_group = rows * heads
    _, depth, vdim = pieces[0].shape

    def body(*refs):
        part_refs, piece_refs = refs[:count], refs[count : count + near]
        attended, sum_ref = refs[count + near :]
        me = lax.axis_index(("role", "seq"))
        tops, sums = [], []
        for ref in part_refs:
            table = sum(
                ref[per_group:, i * LANES : (i + 1) * LANES].astype(f32) for i in reversed(range(3))
            )
            table = jnp.concatenate([table, jnp.zeros((LANES - STAT_ROWS, LANES), f32)], axis=0).T
            tops.append(table[:per_group, 0:1])
            sums.append(table[:per_group, 1:2])
        highest = functools.reduce(jnp.maximum, tops)
        factors = [jnp.exp(top - highest) for top in tops]
        denom = sum(f * s for f, s in zip(factors, sums))
        numer = sum(f * ref[:per_group, :].astype(f32) for f, ref in zip(factors, part_refs))
        joined = (numer / denom).astype(bf16).astype(f32)
        for k in range(slices):
            attended[k] = joined[:, k * depth : (k + 1) * depth]
        project_values(attended, piece_refs, range(near), me, rows, heads, sum_ref, None)

    return call(
        body,
        [
            jax.ShapeDtypeStruct((slices, per_group, depth), f32),
            jax.ShapeDtypeStruct((rows, heads * vdim), f32),
        ],
        [*parts, *[in_vmem(piece) for piece in pieces]],
        [IN_VMEM] * (count + near),
        cost=(rows * heads * LATENT * vdim, 4 << 20),
    )


def project_values(attended, piece_refs, masks, me, rows, heads, out_ref, sum_ref):
    vdim = piece_refs[0].shape[2]
    for h in range(heads):
        part = slice(h * vdim, (h + 1) * vdim)
        total = None if sum_ref is None else sum_ref[:, part]
        for ref, m in zip(piece_refs, masks):
            left = attended[me ^ m, pl.ds(h, rows, stride=heads), :].astype(bf16)
            term = jnp.dot(left, ref[h], preferred_element_type=f32)
            total = term if total is None else total + term
        out_ref[:, part] = total.astype(out_ref.dtype)


def add_values(attended, sums, pieces, masks, heads):
    far = len(pieces)
    rows = sums.shape[0]

    def body(attended_ref, sum_ref, *refs):
        me = lax.axis_index(("role", "seq"))
        project_values(attended_ref, refs[:far], masks, me, rows, heads, refs[far], sum_ref)

    return call(
        body,
        jax.ShapeDtypeStruct(sums.shape, bf16),
        [attended, sums, *[in_vmem(piece) for piece in pieces]],
        [IN_VMEM] * (far + 2),
        cost=(rows * LATENT * sums.shape[1], 4 << 20),
    )


def project_out(pieces, weights):
    count, parts = len(pieces), len(weights)
    rows, depth = pieces[0].shape
    width = weights[0].shape[1]

    def body(*refs):
        weight_refs, (out_ref, placed) = refs[count : count + parts], refs[count + parts :]
        me = lax.axis_index(("role", "seq"))
        for m in range(count):
            placed[me ^ m] = refs[m][...].astype(f32)
        values = jnp.concatenate([placed[k] for k in range(count)], axis=0).astype(bf16)
        total, start = None, 0
        for ref in weight_refs:
            term = jnp.dot(values[:, start : start + ref.shape[0]], ref[...], preferred_element_type=f32)
            total = term if total is None else total + term
            start += ref.shape[0]
        out_ref[...] = total.astype(bf16)

    return call(
        body,
        jax.ShapeDtypeStruct((count * rows, width), bf16),
        [*pieces, *[in_vmem(weight) for weight in weights]],
        [IN_VMEM] * (count + parts),
        [pltpu.VMEM((count, rows, depth), f32)],
        cost=(2 * count * rows * depth * width, 4 << 20),
    )


def gate_and_up_away(pieces, residual, gain, gate_weight, up_weight):
    count = len(pieces)
    rows, width = residual.shape
    hidden = gate_weight.shape[1]
    cores = lax.axis_size("seq")
    half = hidden // cores
    own_rows = rows // count

    def body(*refs):
        residual_ref, gain_ref, gate_ref, up_ref = refs[count : count + 4]
        send_ref, scaled_ref, squares_ref, base_ref, placed = refs[count + 4 :]
        resid = residual_ref[...].astype(f32) + sum(ref[...].astype(f32) for ref in refs[:count])
        scaled = (resid * gain_ref[...][None, :]).astype(bf16)
        scaled_ref[...] = scaled
        other = lax.axis_index("seq") ^ 1
        for k in range(cores):

            @pl.when(other == k)
            def _(k=k):
                part = slice(k * half, (k + 1) * half)
                gate = jnp.dot(scaled, gate_ref[:, part], preferred_element_type=f32)
                up = jnp.dot(scaled, up_ref[:, part], preferred_element_type=f32)
                send_ref[:, :half] = gate.astype(bf16)
                send_ref[:, half : 2 * half] = up.astype(bf16)

        for k in range(count):
            placed[k] = resid[k * own_rows : (k + 1) * own_rows]
        base_ref[...] = placed[lax.axis_index("ctx")]
        squares = jnp.sum(resid * resid, axis=1, keepdims=True)
        lane = lax.broadcasted_iota(jnp.int32, (rows, LANES), 1)
        squares_ref[...] = jnp.broadcast_to(squares, (rows, LANES))
        send_ref[:, 2 * half :] = spread(squares, lane)

    return call(
        body,
        [
            jax.ShapeDtypeStruct((rows, 2 * half + LANES), bf16),
            jax.ShapeDtypeStruct((rows, width), bf16),
            jax.ShapeDtypeStruct((rows, LANES), f32),
            jax.ShapeDtypeStruct((own_rows, width), f32),
        ],
        [*pieces, residual, gain, in_vmem(gate_weight), in_vmem(up_weight)],
        [IN_VMEM] * (count + 4),
        [pltpu.VMEM((count, own_rows, width), f32)],
        cost=(2 * rows * width * hidden, 4 << 20),
    )


def gate_and_up_here(scaled, gate_weight, up_weight):
    rows, width = scaled.shape
    hidden = gate_weight.shape[1]
    cores = lax.axis_size("seq")
    half = hidden // cores

    def body(scaled_ref, gate_ref, up_ref, keep_ref):
        me = lax.axis_index("seq")
        for k in range(cores):

            @pl.when(me == k)
            def _(k=k):
                part = slice(k * half, (k + 1) * half)
                keep_ref[:, :half] = jnp.dot(scaled_ref[...], gate_ref[:, part], preferred_element_type=f32)
                keep_ref[:, half:] = jnp.dot(scaled_ref[...], up_ref[:, part], preferred_element_type=f32)

    return call(
        body,
        jax.ShapeDtypeStruct((rows, 2 * half), f32),
        [scaled, in_vmem(gate_weight), in_vmem(up_weight)],
        [IN_VMEM] * 3,
        cost=(2 * rows * width * hidden, 4 << 20),
    )


def spread(column, lane):
    high, middle, low = three_parts(column)
    return jnp.where(
        lane == 0,
        high.astype(f32),
        jnp.where(lane == 1, middle.astype(f32), jnp.where(lane == 2, low.astype(f32), 0.0)),
    ).astype(bf16)


def add_core(keep, squares, got):
    rows, width = got.shape
    body_width = width - LANES

    def body(keep_ref, squares_ref, got_ref, sum_ref, send_ref):
        total = keep_ref[...] + got_ref[:, :body_width].astype(f32)
        both = squares_ref[:, 0:1] + jnp.sum(got_ref[:, body_width:].astype(f32), axis=1, keepdims=True)
        sum_ref[:, :body_width] = total
        sum_ref[:, body_width:] = jnp.broadcast_to(both, (rows, LANES))
        send_ref[:, :body_width] = total.astype(bf16)
        lane = lax.broadcasted_iota(jnp.int32, (rows, LANES), 1)
        send_ref[:, body_width:] = spread(both, lane)

    return call(
        body,
        [jax.ShapeDtypeStruct((rows, width), f32), jax.ShapeDtypeStruct((rows, width), bf16)],
        [keep, squares, got],
        [IN_VMEM] * 3,
        cost=(rows * width, rows * width * 8),
    )


def activate(keep, pieces, features):
    rows, width = keep.shape
    body_width = width - LANES
    half = body_width // 2

    def body(*refs):
        keep_ref, out_ref = refs[0], refs[-1]
        total = keep_ref[:, :body_width] + sum(r[:, :body_width].astype(f32) for r in refs[1:-1])
        squares = keep_ref[:, body_width : body_width + 1] + sum(
            jnp.sum(r[:, body_width:].astype(f32), axis=1, keepdims=True) for r in refs[1:-1]
        )
        scale = lax.rsqrt(squares / features + EPSILON)
        gate = total[:, :half] * scale
        up = total[:, half:] * scale
        out_ref[...] = (gate / (1.0 + jnp.exp(-gate)) * up).astype(bf16)

    return call(
        body,
        jax.ShapeDtypeStruct((rows, half), bf16),
        [keep, *pieces],
        [IN_VMEM] * (1 + len(pieces)),
        cost=(rows * width, rows * width * 8),
    )


def project_down_own(own, weight):
    rows, half = own.shape
    width = weight.shape[1]

    def body(own_ref, weight_ref, out_ref):
        start = pl.multiple_of(lax.axis_index("seq") * half, 16)
        out_ref[...] = jnp.dot(own_ref[...], weight_ref[pl.ds(start, half), :], preferred_element_type=f32)

    return call(
        body,
        jax.ShapeDtypeStruct((rows, width), f32),
        [own, in_vmem(weight)],
        [IN_VMEM] * 2,
        cost=(2 * rows * half * width, 4 << 20),
    )


def project_down_other(other, weight, partial):
    rows, half = other.shape
    width = weight.shape[1]
    count = lax.axis_size("ctx")
    own_rows = rows // count

    def body(other_ref, weight_ref, partial_ref, *refs):
        out_refs, placed = refs[:count], refs[count]
        start = pl.multiple_of((lax.axis_index("seq") ^ 1) * half, 16)
        out = partial_ref[...] + jnp.dot(
            other_ref[...], weight_ref[pl.ds(start, half), :], preferred_element_type=f32
        )
        for k in range(count):
            placed[k] = out[k * own_rows : (k + 1) * own_rows]
        me = lax.axis_index("ctx")
        for m in range(count):
            out_refs[m][...] = placed[me ^ m].astype(bf16)

    return call(
        body,
        [jax.ShapeDtypeStruct((own_rows, width), bf16)] * count,
        [other, in_vmem(weight), partial],
        [IN_VMEM] * 3,
        [pltpu.VMEM((count, own_rows, width), f32)],
        cost=(2 * rows * half * width, 4 << 20),
    )


def finish(base, pieces):
    def body(*refs):
        refs[-1][...] = (refs[0][...] + sum(r[...].astype(f32) for r in refs[1:-1])).astype(bf16)

    return call(
        body,
        jax.ShapeDtypeStruct(base.shape, bf16),
        [base, *pieces],
        [IN_VMEM] * (1 + len(pieces)),
        cost=(base.size, base.size * 8),
    )


def per_device(
    queries,
    cache,
    lengths,
    positions,
    value_up_weight,
    out_proj,
    residual,
    norm_gain,
    gate_weight,
    up_weight,
    down_weight,
):
    rows, heads, _ = queries.shape
    blocks = lax.axis_size("ctx")
    roles = lax.axis_size("role")
    members = lax.axis_size(("role", "seq"))

    evens, odds = range(2, blocks, 2), range(3, blocks, 2)

    along = listed(exchange([value_up_weight] * roles, "role"))
    groups = exchange([queries] * blocks, "ctx", [*evens, 1])
    unit = out_proj.shape[0] // 16
    cuts = [unit * k for k in (0, 2, 6, 8, 10, 13, 16)]
    own_span, early_span, even_span, odd_span, late_span, last_span = zip(cuts, cuts[1:])
    groups[0], cache_fast, seen = fetch([queries, jnp.swapaxes(cache, 1, 2)], lengths, positions)

    def attend_some(source, span):
        *outs, part = attend(list(source.values()), cache_fast, seen, out_proj, span)
        return dict(zip(source, outs)), part

    answers, own_part = attend_some({0: groups[0]}, own_span)
    (early_part,) = fetch([(out_proj, early_span)])
    relayed = {}
    for mask in evens:
        relayed[mask + 1] = xor_permute(groups[mask], "ctx", 1)
    even, even_part = attend_some({mask: groups[mask] for mask in [*evens, 1]}, even_span)
    answers |= exchange({0: answers[0], **even}, "ctx", evens)
    far, odd_part = attend_some(relayed, odd_span)
    answers |= exchange({0: answers[0], **far}, "ctx", odds)
    answers |= exchange({0: answers[0], **even}, "ctx", [1])

    gate_fast, up_own, residual, gain = fetch([gate_weight, value_up_weight, residual, norm_gain])
    *far_rows, gain = lax.optimization_barrier((*along[1:], gain))
    near_rows = [up_own, xor_permute(along[0], "seq", 1)]
    far_rows = [part for piece in far_rows for part in (piece, xor_permute(piece, "seq", 1))]
    (late_part,) = fetch([(out_proj, late_span)])

    attended, sums = join_blocks(listed(answers), near_rows, rows, heads, members)
    values = add_values(attended, sums, far_rows, range(2, members), heads)
    last_out, values = lax.optimization_barrier((out_proj, values))
    shared = listed(exchange([values] * members, ("role", "seq")))
    (last_part,) = fetch([(last_out, last_span)])
    product = project_out(shared, [own_part, early_part, even_part, odd_part, late_part, last_part])
    up_weight, product = lax.optimization_barrier((up_weight, product))
    terms = listed(exchange([product] * blocks, "ctx"))
    (up_fast,) = fetch([up_weight])

    send, scaled, squares, base = gate_and_up_away(terms, residual, gain, gate_fast, up_fast)
    got = xor_permute(send, "seq", 1)
    keep = gate_and_up_here(scaled, gate_fast, up_fast)
    keep, send = add_core(keep, squares, got)
    down_weight, send = lax.optimization_barrier((down_weight, send))
    (down_fast,) = fetch([down_weight])
    pieces = listed(exchange([send] * roles, "role"))[1:]
    features = norm_gain.shape[0] * members
    hidden = activate(keep, pieces, features)
    other = xor_permute(hidden, "seq", 1)
    own = project_down_own(hidden, down_fast)
    last = exchange(project_down_other(other, down_fast, own), "ctx")
    return finish(base, listed(last))


def solution(mesh):
    placed = (
        P(("groups", "role", "seq"), "ctx", None),
        P(("groups", "role", "seq"), "ctx", None),
        P(("groups", "role", "seq")),
        P(("groups", "role", "seq")),
        P("ctx", ("role", "seq"), None),
        P("ctx", ("role", "seq")),
        P("groups", ("role", "seq")),
        P(("role", "seq")),
        P(("role", "seq"), "ctx"),
        P(("role", "seq"), "ctx"),
        P("ctx", ("role", "seq")),
    )


    return jax.shard_map(
        per_device,
        mesh=mesh,
        in_specs=placed,
        out_specs=P(("groups", "ctx"), ("role", "seq")),
        check_vma=False,
    )
```

```python
import functools
import math

import jax
import jax.numpy as jnp
from jax import lax
from jax.experimental import pallas as pl
from jax.experimental.pallas import tpu as pltpu
from jax.sharding import PartitionSpec as P


LATENT = 512
MTP = 2
SCALE = 0.07216878364870323
EPSILON = 1e-06
DEAD = -1e30
STAT_ROWS = 8
LANES = 128
ATTEND_LIMIT = 8 << 20
KERNEL_LIMIT = 6 << 20


f32, bf16 = jnp.float32, jnp.bfloat16
IN_VMEM = pl.BlockSpec(memory_space=pltpu.VMEM)
IN_SMEM = pl.BlockSpec(memory_space=pltpu.SMEM)
IN_HBM = pl.BlockSpec(memory_space=pltpu.HBM)


def xor_permute(x, axis, mask):
    size = lax.axis_size(axis)
    return lax.ppermute(x, axis, [(i, i ^ mask) for i in range(size)])


def exchange(pieces, axis, masks=None):
    got = {0: pieces[0]}
    for mask in masks or reversed(range(1, len(pieces))):
        got[mask] = xor_permute(pieces[mask], axis, mask)
    return got


def listed(got):
    return [got[mask] for mask in sorted(got)]


def call(body, outs, args, specs, scratch=(), limit=KERNEL_LIMIT, cost=None):
    flops, moved = cost or (0, 0)
    return pl.pallas_call(
        body,
        out_shape=outs,
        in_specs=specs,
        out_specs=jax.tree.map(lambda _: IN_VMEM, outs),
        scratch_shapes=list(scratch),
        compiler_params=pltpu.CompilerParams(vmem_limit_bytes=limit),
        cost_estimate=pl.CostEstimate(flops=flops, bytes_accessed=moved, transcendentals=0),
    )(*args)


def in_vmem(x):
    return pltpu.with_memory_space_constraint(x, pltpu.VMEM)


def three_parts(x):
    high = x.astype(bf16)
    rest = x - high.astype(f32)
    middle = rest.astype(bf16)
    return high, middle, (rest - middle.astype(f32)).astype(bf16)


def fetch(arrays, lengths=None, positions=None):
    spans = [x[1] if isinstance(x, tuple) else (0, x.shape[0]) for x in arrays]
    arrays = [x[0] if isinstance(x, tuple) else x for x in arrays]
    shapes = [(last - first, *x.shape[1:]) for x, (first, last) in zip(arrays, spans)]
    count = len(arrays)
    scalars = [] if positions is None else [lengths, positions]
    rows = positions.shape[0] if scalars else 0
    copied = count + len(scalars)

    def body(*refs):
        sources, refs = refs[:copied], refs[copied:]
        targets, refs = refs[:count], refs[count:]
        sources = [
            source if i >= count or spans[i] == (0, source.shape[0]) else source.at[pl.ds(spans[i][0], shapes[i][0])]
            for i, source in enumerate(sources)
        ]
        done, in_smem = refs[-1], refs[-1 - len(scalars) : -1]
        copies = [
            pltpu.make_async_copy(source, target, done.at[i])
            for i, (source, target) in enumerate(zip(sources, [*targets, *in_smem]))
        ]
        for copy in reversed(copies):
            copy.start()
        for copy in copies[count:]:
            copy.wait()
        if scalars:
            length_ref, position_ref = in_smem
            row = lax.broadcasted_iota(jnp.int32, (rows, LANES), 0)
            seen = jnp.zeros((rows, LANES), jnp.int32)
            for r in range(rows):
                bound = jnp.minimum(length_ref[r // MTP], position_ref[r] + 1)
                seen = jnp.where(row == r, bound, seen)
            refs[0][...] = seen
        for copy in copies[:count]:
            copy.wait()

    moved = sum(2 * math.prod(shape) * x.dtype.itemsize for shape, x in zip(shapes, arrays))
    return call(
        body,
        [pltpu.VMEM(shape, x.dtype) for shape, x in zip(shapes, arrays)]
        + ([pltpu.VMEM((rows, LANES), jnp.int32)] if scalars else []),
        [pltpu.with_memory_space_constraint(x, pltpu.HBM) for x in [*arrays, *scalars]],
        [IN_HBM] * copied,
        [pltpu.SMEM(x.shape, x.dtype) for x in scalars] + [pltpu.SemaphoreType.DMA((copied,))],
        limit=1 << 20,
        cost=(0, moved),
    )


def attend(groups, cache, seen, weight, span):
    count = len(groups)
    rows, heads, width = groups[0].shape
    seqs, _, context = cache.shape
    per_seq = MTP * heads
    per_group = rows * heads

    def body(*refs):
        query_refs = refs[:count]
        cache_ref, seen_ref, weight_ref = refs[count : count + 3]
        out_refs = refs[count + 3 : 2 * count + 3]
        fetched, done = refs[2 * count + 3 :]
        copy = pltpu.make_async_copy(weight_ref.at[pl.ds(span[0], span[1] - span[0])], fetched, done)
        copy.start()
        offset = lax.axis_index("ctx") * context
        total = count * per_seq
        tops, sums = [[] for _ in range(count)], [[] for _ in range(count)]
        for n in range(seqs):
            queries = jnp.concatenate(
                [q[MTP * n : MTP * (n + 1)].reshape(per_seq, width) for q in query_refs], axis=0
            )
            scores = jnp.dot(queries, cache_ref[n], preferred_element_type=f32) * SCALE
            row = lax.broadcasted_iota(jnp.int32, (total, 1), 0)
            which = (row // heads) % MTP
            limit = jnp.full((total, 1), 0, jnp.int32)
            for t in range(MTP):
                r = MTP * n + t
                limit = jnp.where(which == t, seen_ref[r : r + 1, 0:1], limit)
            place = offset + lax.broadcasted_iota(jnp.int32, (total, context), 1)
            live = place < limit
            top = jnp.max(jnp.where(live, scores, DEAD), axis=1, keepdims=True)
            probs = jnp.exp(jnp.where(live, scores - top, DEAD)).astype(bf16)
            weight = jnp.sum(probs.astype(f32), axis=1, keepdims=True)
            out = lax.dot_general(
                probs, cache_ref[n, :LATENT, :], (((1,), (1,)), ((), ())), preferred_element_type=f32
            )
            for g in range(count):
                part = slice(g * per_seq, (g + 1) * per_seq)
                out_refs[g][n * per_seq : (n + 1) * per_seq, :] = out[part].astype(bf16)
                tops[g].append(top[part])
                sums[g].append(weight[part])
        lane = lax.broadcasted_iota(jnp.int32, (LANES, LANES), 1)
        for g in range(count):
            fill = [jnp.zeros((LANES - per_group, 1), f32)] if per_group < LANES else []
            top = jnp.concatenate(tops[g] + fill, axis=0)
            weight = jnp.concatenate(sums[g] + fill, axis=0)
            table = jnp.where(lane == 0, top, jnp.where(lane == 1, weight, 0.0)).T
            for i, part in enumerate(three_parts(table[:STAT_ROWS])):
                out_refs[g][per_group:, i * LANES : (i + 1) * LANES] = part
            out_refs[g][per_group:, 3 * LANES :] = jnp.zeros((STAT_ROWS, LATENT - 3 * LANES), bf16)
        copy.wait()

    shape = jax.ShapeDtypeStruct((per_group + STAT_ROWS, LATENT), bf16)
    flops = 2 * count * rows * heads * context * (width + LATENT)
    return call(
        body,
        [shape] * count + [pltpu.VMEM((span[1] - span[0], weight.shape[1]), weight.dtype)],
        [*groups, in_vmem(cache), seen, pltpu.with_memory_space_constraint(weight, pltpu.HBM)],
        [IN_VMEM] * (count + 2) + [IN_HBM],
        [pltpu.SemaphoreType.DMA],
        limit=ATTEND_LIMIT,
        cost=(flops, 4 << 20),
    )


def join_blocks(parts, pieces, rows, heads, slices):
    count, near = len(parts), len(pieces)
    per_group = rows * heads
    _, depth, vdim = pieces[0].shape

    def body(*refs):
        part_refs, piece_refs = refs[:count], refs[count : count + near]
        attended, sum_ref = refs[count + near :]
        me = lax.axis_index(("role", "seq"))
        tops, sums = [], []
        for ref in part_refs:
            table = sum(
                ref[per_group:, i * LANES : (i + 1) * LANES].astype(f32) for i in reversed(range(3))
            )
            table = jnp.concatenate([table, jnp.zeros((LANES - STAT_ROWS, LANES), f32)], axis=0).T
            tops.append(table[:per_group, 0:1])
            sums.append(table[:per_group, 1:2])
        highest = functools.reduce(jnp.maximum, tops)
        factors = [jnp.exp(top - highest) for top in tops]
        denom = sum(f * s for f, s in zip(factors, sums))
        numer = sum(f * ref[:per_group, :].astype(f32) for f, ref in zip(factors, part_refs))
        joined = (numer / denom).astype(bf16).astype(f32)
        for k in range(slices):
            attended[k] = joined[:, k * depth : (k + 1) * depth]
        project_values(attended, piece_refs, range(near), me, rows, heads, sum_ref, None)

    return call(
        body,
        [
            jax.ShapeDtypeStruct((slices, per_group, depth), f32),
            jax.ShapeDtypeStruct((rows, heads * vdim), f32),
        ],
        [*parts, *[in_vmem(piece) for piece in pieces]],
        [IN_VMEM] * (count + near),
        cost=(rows * heads * LATENT * vdim, 4 << 20),
    )


def project_values(attended, piece_refs, masks, me, rows, heads, out_ref, sum_ref):
    vdim = piece_refs[0].shape[2]
    for h in range(heads):
        part = slice(h * vdim, (h + 1) * vdim)
        total = None if sum_ref is None else sum_ref[:, part]
        for ref, m in zip(piece_refs, masks):
            left = attended[me ^ m, pl.ds(h, rows, stride=heads), :].astype(bf16)
            term = jnp.dot(left, ref[h], preferred_element_type=f32)
            total = term if total is None else total + term
        out_ref[:, part] = total.astype(out_ref.dtype)


def add_values(attended, sums, pieces, masks, heads):
    far = len(pieces)
    rows = sums.shape[0]

    def body(attended_ref, sum_ref, *refs):
        me = lax.axis_index(("role", "seq"))
        project_values(attended_ref, refs[:far], masks, me, rows, heads, refs[far], sum_ref)

    return call(
        body,
        jax.ShapeDtypeStruct(sums.shape, bf16),
        [attended, sums, *[in_vmem(piece) for piece in pieces]],
        [IN_VMEM] * (far + 2),
        cost=(rows * LATENT * sums.shape[1], 4 << 20),
    )


def project_out(pieces, weights):
    count, parts = len(pieces), len(weights)
    rows, depth = pieces[0].shape
    width = weights[0].shape[1]

    def body(*refs):
        weight_refs, (out_ref, placed) = refs[count : count + parts], refs[count + parts :]
        me = lax.axis_index(("role", "seq"))
        for m in range(count):
            placed[me ^ m] = refs[m][...].astype(f32)
        values = jnp.concatenate([placed[k] for k in range(count)], axis=0).astype(bf16)
        total, start = None, 0
        for ref in weight_refs:
            term = jnp.dot(values[:, start : start + ref.shape[0]], ref[...], preferred_element_type=f32)
            total = term if total is None else total + term
            start += ref.shape[0]
        out_ref[...] = total.astype(bf16)

    return call(
        body,
        jax.ShapeDtypeStruct((count * rows, width), bf16),
        [*pieces, *[in_vmem(weight) for weight in weights]],
        [IN_VMEM] * (count + parts),
        [pltpu.VMEM((count, rows, depth), f32)],
        cost=(2 * count * rows * depth * width, 4 << 20),
    )


def gate_and_up_away(pieces, residual, gain, gate_weight, up_weight):
    count = len(pieces)
    rows, width = residual.shape
    hidden = gate_weight.shape[1]
    cores = lax.axis_size("seq")
    half = hidden // cores
    own_rows = rows // count

    def body(*refs):
        residual_ref, gain_ref, gate_ref, up_ref = refs[count : count + 4]
        send_ref, scaled_ref, squares_ref, base_ref, placed = refs[count + 4 :]
        resid = residual_ref[...].astype(f32) + sum(ref[...].astype(f32) for ref in refs[:count])
        scaled = (resid * gain_ref[...][None, :]).astype(bf16)
        scaled_ref[...] = scaled
        other = lax.axis_index("seq") ^ 1
        for k in range(cores):

            @pl.when(other == k)
            def _(k=k):
                part = slice(k * half, (k + 1) * half)
                gate = jnp.dot(scaled, gate_ref[:, part], preferred_element_type=f32)
                up = jnp.dot(scaled, up_ref[:, part], preferred_element_type=f32)
                send_ref[:, :half] = gate.astype(bf16)
                send_ref[:, half : 2 * half] = up.astype(bf16)

        for k in range(count):
            placed[k] = resid[k * own_rows : (k + 1) * own_rows]
        base_ref[...] = placed[lax.axis_index("ctx")]
        squares = jnp.sum(resid * resid, axis=1, keepdims=True)
        lane = lax.broadcasted_iota(jnp.int32, (rows, LANES), 1)
        squares_ref[...] = jnp.broadcast_to(squares, (rows, LANES))
        send_ref[:, 2 * half :] = spread(squares, lane)

    return call(
        body,
        [
            jax.ShapeDtypeStruct((rows, 2 * half + LANES), bf16),
            jax.ShapeDtypeStruct((rows, width), bf16),
            jax.ShapeDtypeStruct((rows, LANES), f32),
            jax.ShapeDtypeStruct((own_rows, width), f32),
        ],
        [*pieces, residual, gain, in_vmem(gate_weight), in_vmem(up_weight)],
        [IN_VMEM] * (count + 4),
        [pltpu.VMEM((count, own_rows, width), f32)],
        cost=(2 * rows * width * hidden, 4 << 20),
    )


def gate_and_up_here(scaled, gate_weight, up_weight):
    rows, width = scaled.shape
    hidden = gate_weight.shape[1]
    cores = lax.axis_size("seq")
    half = hidden // cores

    def body(scaled_ref, gate_ref, up_ref, keep_ref):
        me = lax.axis_index("seq")
        for k in range(cores):

            @pl.when(me == k)
            def _(k=k):
                part = slice(k * half, (k + 1) * half)
                keep_ref[:, :half] = jnp.dot(scaled_ref[...], gate_ref[:, part], preferred_element_type=f32)
                keep_ref[:, half:] = jnp.dot(scaled_ref[...], up_ref[:, part], preferred_element_type=f32)

    return call(
        body,
        jax.ShapeDtypeStruct((rows, 2 * half), f32),
        [scaled, in_vmem(gate_weight), in_vmem(up_weight)],
        [IN_VMEM] * 3,
        cost=(2 * rows * width * hidden, 4 << 20),
    )


def spread(column, lane):
    high, middle, low = three_parts(column)
    return jnp.where(
        lane == 0,
        high.astype(f32),
        jnp.where(lane == 1, middle.astype(f32), jnp.where(lane == 2, low.astype(f32), 0.0)),
    ).astype(bf16)


def add_core(keep, squares, got):
    rows, width = got.shape
    body_width = width - LANES

    def body(keep_ref, squares_ref, got_ref, sum_ref, send_ref):
        total = keep_ref[...] + got_ref[:, :body_width].astype(f32)
        both = squares_ref[:, 0:1] + jnp.sum(got_ref[:, body_width:].astype(f32), axis=1, keepdims=True)
        sum_ref[:, :body_width] = total
        sum_ref[:, body_width:] = jnp.broadcast_to(both, (rows, LANES))
        send_ref[:, :body_width] = total.astype(bf16)
        lane = lax.broadcasted_iota(jnp.int32, (rows, LANES), 1)
        send_ref[:, body_width:] = spread(both, lane)

    return call(
        body,
        [jax.ShapeDtypeStruct((rows, width), f32), jax.ShapeDtypeStruct((rows, width), bf16)],
        [keep, squares, got],
        [IN_VMEM] * 3,
        cost=(rows * width, rows * width * 8),
    )


def activate(keep, pieces, features):
    rows, width = keep.shape
    body_width = width - LANES
    half = body_width // 2

    def body(*refs):
        keep_ref, out_ref = refs[0], refs[-1]
        total = keep_ref[:, :body_width] + sum(r[:, :body_width].astype(f32) for r in refs[1:-1])
        squares = keep_ref[:, body_width : body_width + 1] + sum(
            jnp.sum(r[:, body_width:].astype(f32), axis=1, keepdims=True) for r in refs[1:-1]
        )
        scale = lax.rsqrt(squares / features + EPSILON)
        gate = total[:, :half] * scale
        up = total[:, half:] * scale
        out_ref[...] = (gate / (1.0 + jnp.exp(-gate)) * up).astype(bf16)

    return call(
        body,
        jax.ShapeDtypeStruct((rows, half), bf16),
        [keep, *pieces],
        [IN_VMEM] * (1 + len(pieces)),
        cost=(rows * width, rows * width * 8),
    )


def project_down_own(own, weight):
    rows, half = own.shape
    width = weight.shape[1]

    def body(own_ref, weight_ref, out_ref):
        start = pl.multiple_of(lax.axis_index("seq") * half, 16)
        out_ref[...] = jnp.dot(own_ref[...], weight_ref[pl.ds(start, half), :], preferred_element_type=f32)

    return call(
        body,
        jax.ShapeDtypeStruct((rows, width), f32),
        [own, in_vmem(weight)],
        [IN_VMEM] * 2,
        cost=(2 * rows * half * width, 4 << 20),
    )


def project_down_other(other, weight, partial):
    rows, half = other.shape
    width = weight.shape[1]
    count = lax.axis_size("ctx")
    own_rows = rows // count

    def body(other_ref, weight_ref, partial_ref, *refs):
        out_refs, placed = refs[:count], refs[count]
        start = pl.multiple_of((lax.axis_index("seq") ^ 1) * half, 16)
        out = partial_ref[...] + jnp.dot(
            other_ref[...], weight_ref[pl.ds(start, half), :], preferred_element_type=f32
        )
        for k in range(count):
            placed[k] = out[k * own_rows : (k + 1) * own_rows]
        me = lax.axis_index("ctx")
        for m in range(count):
            out_refs[m][...] = placed[me ^ m].astype(bf16)

    return call(
        body,
        [jax.ShapeDtypeStruct((own_rows, width), bf16)] * count,
        [other, in_vmem(weight), partial],
        [IN_VMEM] * 3,
        [pltpu.VMEM((count, own_rows, width), f32)],
        cost=(2 * rows * half * width, 4 << 20),
    )


def finish(base, pieces):
    def body(*refs):
        refs[-1][...] = (refs[0][...] + sum(r[...].astype(f32) for r in refs[1:-1])).astype(bf16)

    return call(
        body,
        jax.ShapeDtypeStruct(base.shape, bf16),
        [base, *pieces],
        [IN_VMEM] * (1 + len(pieces)),
        cost=(base.size, base.size * 8),
    )


def per_device(
    queries,
    cache,
    lengths,
    positions,
    value_up_weight,
    out_proj,
    residual,
    norm_gain,
    gate_weight,
    up_weight,
    down_weight,
):
    rows, heads, _ = queries.shape
    blocks = lax.axis_size("ctx")
    roles = lax.axis_size("role")
    members = lax.axis_size(("role", "seq"))

    evens, odds = range(2, blocks, 2), range(3, blocks, 2)

    along = listed(exchange([value_up_weight] * roles, "role"))
    groups = exchange([queries] * blocks, "ctx", [*evens, 1])
    unit = out_proj.shape[0] // 16
    cuts = [unit * k for k in (0, 2, 6, 8, 10, 16)]
    own_span, early_span, even_span, odd_span, last_span = zip(cuts, cuts[1:])
    groups[0], cache_fast, seen = fetch([queries, jnp.swapaxes(cache, 1, 2)], lengths, positions)

    def attend_some(source, span):
        *outs, part = attend(list(source.values()), cache_fast, seen, out_proj, span)
        return dict(zip(source, outs)), part

    answers, own_part = attend_some({0: groups[0]}, own_span)
    (early_part,) = fetch([(out_proj, early_span)])
    relayed = {}
    for mask in evens:
        relayed[mask + 1] = xor_permute(groups[mask], "ctx", 1)
    even, even_part = attend_some({mask: groups[mask] for mask in [*evens, 1]}, even_span)
    answers |= exchange({0: answers[0], **even}, "ctx", evens)
    answers |= exchange({0: answers[0], **even}, "ctx", [1])
    far, odd_part = attend_some(relayed, odd_span)
    answers |= exchange({0: answers[0], **far}, "ctx", odds)

    gate_fast, up_own, residual, gain = fetch([gate_weight, value_up_weight, residual, norm_gain])
    *far_rows, gain = lax.optimization_barrier((*along[1:], gain))
    near_rows = [up_own, xor_permute(along[0], "seq", 1)]
    far_rows = [part for piece in far_rows for part in (piece, xor_permute(piece, "seq", 1))]
    attended, sums = join_blocks(listed(answers), near_rows, rows, heads, members)
    values = add_values(attended, sums, far_rows, range(2, members), heads)
    last_out, values = lax.optimization_barrier((out_proj, values))
    shared = listed(exchange([values] * members, ("role", "seq")))
    (last_part,) = fetch([(last_out, last_span)])
    product = project_out(shared, [own_part, early_part, even_part, odd_part, last_part])
    up_weight, product = lax.optimization_barrier((up_weight, product))
    terms = listed(exchange([product] * blocks, "ctx"))
    up_fast = up_weight

    send, scaled, squares, base = gate_and_up_away(terms, residual, gain, gate_fast, up_fast)
    got = xor_permute(send, "seq", 1)
    keep = gate_and_up_here(scaled, gate_fast, up_fast)
    keep, send = add_core(keep, squares, got)
    down_fast = down_weight
    pieces = listed(exchange([send] * roles, "role"))[1:]
    features = norm_gain.shape[0] * members
    hidden = activate(keep, pieces, features)
    other = xor_permute(hidden, "seq", 1)
    own = project_down_own(hidden, down_fast)
    last = exchange(project_down_other(other, down_fast, own), "ctx")
    return finish(base, listed(last))


def solution(mesh):
    placed = (
        P(("groups", "role", "seq"), "ctx", None),
        P(("groups", "role", "seq"), "ctx", None),
        P(("groups", "role", "seq")),
        P(("groups", "role", "seq")),
        P("ctx", ("role", "seq"), None),
        P("ctx", ("role", "seq")),
        P("groups", ("role", "seq")),
        P(("role", "seq")),
        P(("role", "seq"), "ctx"),
        P(("role", "seq"), "ctx"),
        P("ctx", ("role", "seq")),
    )


    return jax.shard_map(
        per_device,
        mesh=mesh,
        in_specs=placed,
        out_specs=P(("groups", "ctx"), ("role", "seq")),
        check_vma=False,
    )
```

```python
import functools
import math

import jax
import jax.numpy as jnp
from jax import lax
from jax.experimental import pallas as pl
from jax.experimental.pallas import tpu as pltpu
from jax.sharding import PartitionSpec as P


LATENT = 512
MTP = 2
SCALE = 0.07216878364870323
EPSILON = 1e-06
DEAD = -1e30
STAT_ROWS = 8
LANES = 128
ATTEND_LIMIT = 8 << 20
KERNEL_LIMIT = 6 << 20


f32, bf16 = jnp.float32, jnp.bfloat16
IN_VMEM = pl.BlockSpec(memory_space=pltpu.VMEM)
IN_SMEM = pl.BlockSpec(memory_space=pltpu.SMEM)
IN_HBM = pl.BlockSpec(memory_space=pltpu.HBM)


def xor_permute(x, axis, mask):
    size = lax.axis_size(axis)
    return lax.ppermute(x, axis, [(i, i ^ mask) for i in range(size)])


def exchange(pieces, axis, masks=None):
    got = {0: pieces[0]}
    for mask in masks or reversed(range(1, len(pieces))):
        got[mask] = xor_permute(pieces[mask], axis, mask)
    return got


def listed(got):
    return [got[mask] for mask in sorted(got)]


def call(body, outs, args, specs, scratch=(), limit=KERNEL_LIMIT, cost=None):
    flops, moved = cost or (0, 0)
    return pl.pallas_call(
        body,
        out_shape=outs,
        in_specs=specs,
        out_specs=jax.tree.map(lambda _: IN_VMEM, outs),
        scratch_shapes=list(scratch),
        compiler_params=pltpu.CompilerParams(vmem_limit_bytes=limit),
        cost_estimate=pl.CostEstimate(flops=flops, bytes_accessed=moved, transcendentals=0),
    )(*args)


def in_vmem(x):
    return pltpu.with_memory_space_constraint(x, pltpu.VMEM)


def three_parts(x):
    high = x.astype(bf16)
    rest = x - high.astype(f32)
    middle = rest.astype(bf16)
    return high, middle, (rest - middle.astype(f32)).astype(bf16)


def fetch(arrays, lengths=None, positions=None):
    spans = [x[1] if isinstance(x, tuple) else (0, x.shape[0]) for x in arrays]
    arrays = [x[0] if isinstance(x, tuple) else x for x in arrays]
    shapes = [(last - first, *x.shape[1:]) for x, (first, last) in zip(arrays, spans)]
    count = len(arrays)
    scalars = [] if positions is None else [lengths, positions]
    rows = positions.shape[0] if scalars else 0
    copied = count + len(scalars)

    def body(*refs):
        sources, refs = refs[:copied], refs[copied:]
        targets, refs = refs[:count], refs[count:]
        sources = [
            source if i >= count or spans[i] == (0, source.shape[0]) else source.at[pl.ds(spans[i][0], shapes[i][0])]
            for i, source in enumerate(sources)
        ]
        done, in_smem = refs[-1], refs[-1 - len(scalars) : -1]
        copies = [
            pltpu.make_async_copy(source, target, done.at[i])
            for i, (source, target) in enumerate(zip(sources, [*targets, *in_smem]))
        ]
        for copy in reversed(copies):
            copy.start()
        for copy in copies[count:]:
            copy.wait()
        if scalars:
            length_ref, position_ref = in_smem
            row = lax.broadcasted_iota(jnp.int32, (rows, LANES), 0)
            seen = jnp.zeros((rows, LANES), jnp.int32)
            for r in range(rows):
                bound = jnp.minimum(length_ref[r // MTP], position_ref[r] + 1)
                seen = jnp.where(row == r, bound, seen)
            refs[0][...] = seen
        for copy in copies[:count]:
            copy.wait()

    moved = sum(2 * math.prod(shape) * x.dtype.itemsize for shape, x in zip(shapes, arrays))
    return call(
        body,
        [pltpu.VMEM(shape, x.dtype) for shape, x in zip(shapes, arrays)]
        + ([pltpu.VMEM((rows, LANES), jnp.int32)] if scalars else []),
        [pltpu.with_memory_space_constraint(x, pltpu.HBM) for x in [*arrays, *scalars]],
        [IN_HBM] * copied,
        [pltpu.SMEM(x.shape, x.dtype) for x in scalars] + [pltpu.SemaphoreType.DMA((copied,))],
        limit=1 << 20,
        cost=(0, moved),
    )


def attend(groups, cache, seen, weight, span):
    count = len(groups)
    rows, heads, width = groups[0].shape
    seqs, _, context = cache.shape
    per_seq = MTP * heads
    per_group = rows * heads

    def body(*refs):
        query_refs = refs[:count]
        cache_ref, seen_ref, weight_ref = refs[count : count + 3]
        out_refs = refs[count + 3 : 2 * count + 3]
        fetched, done = refs[2 * count + 3 :]
        copy = pltpu.make_async_copy(weight_ref.at[pl.ds(span[0], span[1] - span[0])], fetched, done)
        copy.start()
        offset = lax.axis_index("ctx") * context
        total = count * per_seq
        tops, sums = [[] for _ in range(count)], [[] for _ in range(count)]
        for n in range(seqs):
            queries = jnp.concatenate(
                [q[MTP * n : MTP * (n + 1)].reshape(per_seq, width) for q in query_refs], axis=0
            )
            scores = jnp.dot(queries, cache_ref[n], preferred_element_type=f32) * SCALE
            row = lax.broadcasted_iota(jnp.int32, (total, 1), 0)
            which = (row // heads) % MTP
            limit = jnp.full((total, 1), 0, jnp.int32)
            for t in range(MTP):
                r = MTP * n + t
                limit = jnp.where(which == t, seen_ref[r : r + 1, 0:1], limit)
            place = offset + lax.broadcasted_iota(jnp.int32, (total, context), 1)
            live = place < limit
            top = jnp.max(jnp.where(live, scores, DEAD), axis=1, keepdims=True)
            probs = jnp.exp(jnp.where(live, scores - top, DEAD)).astype(bf16)
            weight = jnp.sum(probs.astype(f32), axis=1, keepdims=True)
            out = lax.dot_general(
                probs, cache_ref[n, :LATENT, :], (((1,), (1,)), ((), ())), preferred_element_type=f32
            )
            for g in range(count):
                part = slice(g * per_seq, (g + 1) * per_seq)
                out_refs[g][n * per_seq : (n + 1) * per_seq, :] = out[part].astype(bf16)
                tops[g].append(top[part])
                sums[g].append(weight[part])
        lane = lax.broadcasted_iota(jnp.int32, (LANES, LANES), 1)
        for g in range(count):
            fill = [jnp.zeros((LANES - per_group, 1), f32)] if per_group < LANES else []
            top = jnp.concatenate(tops[g] + fill, axis=0)
            weight = jnp.concatenate(sums[g] + fill, axis=0)
            table = jnp.where(lane == 0, top, jnp.where(lane == 1, weight, 0.0)).T
            for i, part in enumerate(three_parts(table[:STAT_ROWS])):
                out_refs[g][per_group:, i * LANES : (i + 1) * LANES] = part
            out_refs[g][per_group:, 3 * LANES :] = jnp.zeros((STAT_ROWS, LATENT - 3 * LANES), bf16)
        copy.wait()

    shape = jax.ShapeDtypeStruct((per_group + STAT_ROWS, LATENT), bf16)
    flops = 2 * count * rows * heads * context * (width + LATENT)
    return call(
        body,
        [shape] * count + [pltpu.VMEM((span[1] - span[0], weight.shape[1]), weight.dtype)],
        [*groups, in_vmem(cache), seen, pltpu.with_memory_space_constraint(weight, pltpu.HBM)],
        [IN_VMEM] * (count + 2) + [IN_HBM],
        [pltpu.SemaphoreType.DMA],
        limit=ATTEND_LIMIT,
        cost=(flops, 4 << 20),
    )


def join_blocks(parts, pieces, rows, heads, slices):
    count, near = len(parts), len(pieces)
    per_group = rows * heads
    _, depth, vdim = pieces[0].shape

    def body(*refs):
        part_refs, piece_refs = refs[:count], refs[count : count + near]
        attended, sum_ref = refs[count + near :]
        me = lax.axis_index(("role", "seq"))
        tops, sums = [], []
        for ref in part_refs:
            table = sum(
                ref[per_group:, i * LANES : (i + 1) * LANES].astype(f32) for i in reversed(range(3))
            )
            table = jnp.concatenate([table, jnp.zeros((LANES - STAT_ROWS, LANES), f32)], axis=0).T
            tops.append(table[:per_group, 0:1])
            sums.append(table[:per_group, 1:2])
        highest = functools.reduce(jnp.maximum, tops)
        factors = [jnp.exp(top - highest) for top in tops]
        denom = sum(f * s for f, s in zip(factors, sums))
        numer = sum(f * ref[:per_group, :].astype(f32) for f, ref in zip(factors, part_refs))
        joined = (numer / denom).astype(bf16).astype(f32)
        for k in range(slices):
            attended[k] = joined[:, k * depth : (k + 1) * depth]
        project_values(attended, piece_refs, range(near), me, rows, heads, sum_ref, None)

    return call(
        body,
        [
            jax.ShapeDtypeStruct((slices, per_group, depth), f32),
            jax.ShapeDtypeStruct((rows, heads * vdim), f32),
        ],
        [*parts, *[in_vmem(piece) for piece in pieces]],
        [IN_VMEM] * (count + near),
        cost=(rows * heads * LATENT * vdim, 4 << 20),
    )


def project_values(attended, piece_refs, masks, me, rows, heads, out_ref, sum_ref):
    vdim = piece_refs[0].shape[2]
    for h in range(heads):
        part = slice(h * vdim, (h + 1) * vdim)
        total = None if sum_ref is None else sum_ref[:, part]
        for ref, m in zip(piece_refs, masks):
            left = attended[me ^ m, pl.ds(h, rows, stride=heads), :].astype(bf16)
            term = jnp.dot(left, ref[h], preferred_element_type=f32)
            total = term if total is None else total + term
        out_ref[:, part] = total.astype(out_ref.dtype)


def add_values(attended, sums, pieces, masks, heads):
    far = len(pieces)
    rows = sums.shape[0]

    def body(attended_ref, sum_ref, *refs):
        me = lax.axis_index(("role", "seq"))
        project_values(attended_ref, refs[:far], masks, me, rows, heads, refs[far], sum_ref)

    return call(
        body,
        jax.ShapeDtypeStruct(sums.shape, bf16),
        [attended, sums, *[in_vmem(piece) for piece in pieces]],
        [IN_VMEM] * (far + 2),
        cost=(rows * LATENT * sums.shape[1], 4 << 20),
    )


def project_out(pieces, weights):
    count, parts = len(pieces), len(weights)
    rows, depth = pieces[0].shape
    width = weights[0].shape[1]

    def body(*refs):
        weight_refs, (out_ref, placed) = refs[count : count + parts], refs[count + parts :]
        me = lax.axis_index(("role", "seq"))
        for m in range(count):
            placed[me ^ m] = refs[m][...].astype(f32)
        values = jnp.concatenate([placed[k] for k in range(count)], axis=0).astype(bf16)
        total, start = None, 0
        for ref in weight_refs:
            term = jnp.dot(values[:, start : start + ref.shape[0]], ref[...], preferred_element_type=f32)
            total = term if total is None else total + term
            start += ref.shape[0]
        out_ref[...] = total.astype(bf16)

    return call(
        body,
        jax.ShapeDtypeStruct((count * rows, width), bf16),
        [*pieces, *[in_vmem(weight) for weight in weights]],
        [IN_VMEM] * (count + parts),
        [pltpu.VMEM((count, rows, depth), f32)],
        cost=(2 * count * rows * depth * width, 4 << 20),
    )


def gate_and_up_away(pieces, residual, gain, gate_weight, up_weight):
    count = len(pieces)
    rows, width = residual.shape
    hidden = gate_weight.shape[1]
    cores = lax.axis_size("seq")
    half = hidden // cores
    own_rows = rows // count

    def body(*refs):
        residual_ref, gain_ref, gate_ref, up_ref = refs[count : count + 4]
        send_ref, scaled_ref, squares_ref, base_ref, placed = refs[count + 4 :]
        resid = residual_ref[...].astype(f32) + sum(ref[...].astype(f32) for ref in refs[:count])
        scaled = (resid * gain_ref[...][None, :]).astype(bf16)
        scaled_ref[...] = scaled
        other = lax.axis_index("seq") ^ 1
        for k in range(cores):

            @pl.when(other == k)
            def _(k=k):
                part = slice(k * half, (k + 1) * half)
                gate = jnp.dot(scaled, gate_ref[:, part], preferred_element_type=f32)
                up = jnp.dot(scaled, up_ref[:, part], preferred_element_type=f32)
                send_ref[:, :half] = gate.astype(bf16)
                send_ref[:, half : 2 * half] = up.astype(bf16)

        for k in range(count):
            placed[k] = resid[k * own_rows : (k + 1) * own_rows]
        base_ref[...] = placed[lax.axis_index("ctx")]
        squares = jnp.sum(resid * resid, axis=1, keepdims=True)
        lane = lax.broadcasted_iota(jnp.int32, (rows, LANES), 1)
        squares_ref[...] = jnp.broadcast_to(squares, (rows, LANES))
        send_ref[:, 2 * half :] = spread(squares, lane)

    return call(
        body,
        [
            jax.ShapeDtypeStruct((rows, 2 * half + LANES), bf16),
            jax.ShapeDtypeStruct((rows, width), bf16),
            jax.ShapeDtypeStruct((rows, LANES), f32),
            jax.ShapeDtypeStruct((own_rows, width), f32),
        ],
        [*pieces, residual, gain, in_vmem(gate_weight), in_vmem(up_weight)],
        [IN_VMEM] * (count + 4),
        [pltpu.VMEM((count, own_rows, width), f32)],
        cost=(2 * rows * width * hidden, 4 << 20),
    )


def gate_and_up_here(scaled, gate_weight, up_weight):
    rows, width = scaled.shape
    hidden = gate_weight.shape[1]
    cores = lax.axis_size("seq")
    half = hidden // cores

    def body(scaled_ref, gate_ref, up_ref, keep_ref):
        me = lax.axis_index("seq")
        for k in range(cores):

            @pl.when(me == k)
            def _(k=k):
                part = slice(k * half, (k + 1) * half)
                keep_ref[:, :half] = jnp.dot(scaled_ref[...], gate_ref[:, part], preferred_element_type=f32)
                keep_ref[:, half:] = jnp.dot(scaled_ref[...], up_ref[:, part], preferred_element_type=f32)

    return call(
        body,
        jax.ShapeDtypeStruct((rows, 2 * half), f32),
        [scaled, in_vmem(gate_weight), in_vmem(up_weight)],
        [IN_VMEM] * 3,
        cost=(2 * rows * width * hidden, 4 << 20),
    )


def spread(column, lane):
    high, middle, low = three_parts(column)
    return jnp.where(
        lane == 0,
        high.astype(f32),
        jnp.where(lane == 1, middle.astype(f32), jnp.where(lane == 2, low.astype(f32), 0.0)),
    ).astype(bf16)


def add_core(keep, squares, got):
    rows, width = got.shape
    body_width = width - LANES

    def body(keep_ref, squares_ref, got_ref, sum_ref, send_ref):
        total = keep_ref[...] + got_ref[:, :body_width].astype(f32)
        both = squares_ref[:, 0:1] + jnp.sum(got_ref[:, body_width:].astype(f32), axis=1, keepdims=True)
        sum_ref[:, :body_width] = total
        sum_ref[:, body_width:] = jnp.broadcast_to(both, (rows, LANES))
        send_ref[:, :body_width] = total.astype(bf16)
        lane = lax.broadcasted_iota(jnp.int32, (rows, LANES), 1)
        send_ref[:, body_width:] = spread(both, lane)

    return call(
        body,
        [jax.ShapeDtypeStruct((rows, width), f32), jax.ShapeDtypeStruct((rows, width), bf16)],
        [keep, squares, got],
        [IN_VMEM] * 3,
        cost=(rows * width, rows * width * 8),
    )


def activate(keep, pieces, features):
    rows, width = keep.shape
    body_width = width - LANES
    half = body_width // 2

    def body(*refs):
        keep_ref, out_ref = refs[0], refs[-1]
        total = keep_ref[:, :body_width] + sum(r[:, :body_width].astype(f32) for r in refs[1:-1])
        squares = keep_ref[:, body_width : body_width + 1] + sum(
            jnp.sum(r[:, body_width:].astype(f32), axis=1, keepdims=True) for r in refs[1:-1]
        )
        scale = lax.rsqrt(squares / features + EPSILON)
        gate = total[:, :half] * scale
        up = total[:, half:] * scale
        out_ref[...] = (gate / (1.0 + jnp.exp(-gate)) * up).astype(bf16)

    return call(
        body,
        jax.ShapeDtypeStruct((rows, half), bf16),
        [keep, *pieces],
        [IN_VMEM] * (1 + len(pieces)),
        cost=(rows * width, rows * width * 8),
    )


def project_down_own(own, weight):
    rows, half = own.shape
    width = weight.shape[1]

    def body(own_ref, weight_ref, out_ref):
        start = pl.multiple_of(lax.axis_index("seq") * half, 16)
        out_ref[...] = jnp.dot(own_ref[...], weight_ref[pl.ds(start, half), :], preferred_element_type=f32)

    return call(
        body,
        jax.ShapeDtypeStruct((rows, width), f32),
        [own, in_vmem(weight)],
        [IN_VMEM] * 2,
        cost=(2 * rows * half * width, 4 << 20),
    )


def project_down_other(other, weight, partial):
    rows, half = other.shape
    width = weight.shape[1]
    count = lax.axis_size("ctx")
    own_rows = rows // count

    def body(other_ref, weight_ref, partial_ref, *refs):
        out_refs, placed = refs[:count], refs[count]
        start = pl.multiple_of((lax.axis_index("seq") ^ 1) * half, 16)
        out = partial_ref[...] + jnp.dot(
            other_ref[...], weight_ref[pl.ds(start, half), :], preferred_element_type=f32
        )
        for k in range(count):
            placed[k] = out[k * own_rows : (k + 1) * own_rows]
        me = lax.axis_index("ctx")
        for m in range(count):
            out_refs[m][...] = placed[me ^ m].astype(bf16)

    return call(
        body,
        [jax.ShapeDtypeStruct((own_rows, width), bf16)] * count,
        [other, in_vmem(weight), partial],
        [IN_VMEM] * 3,
        [pltpu.VMEM((count, own_rows, width), f32)],
        cost=(2 * rows * half * width, 4 << 20),
    )


def finish(base, pieces):
    def body(*refs):
        refs[-1][...] = (refs[0][...] + sum(r[...].astype(f32) for r in refs[1:-1])).astype(bf16)

    return call(
        body,
        jax.ShapeDtypeStruct(base.shape, bf16),
        [base, *pieces],
        [IN_VMEM] * (1 + len(pieces)),
        cost=(base.size, base.size * 8),
    )


def per_device(
    queries,
    cache,
    lengths,
    positions,
    value_up_weight,
    out_proj,
    residual,
    norm_gain,
    gate_weight,
    up_weight,
    down_weight,
):
    rows, heads, _ = queries.shape
    blocks = lax.axis_size("ctx")
    roles = lax.axis_size("role")
    members = lax.axis_size(("role", "seq"))

    evens, odds = range(2, blocks, 2), range(3, blocks, 2)

    along = listed(exchange([value_up_weight] * roles, "role"))
    groups = exchange([queries] * blocks, "ctx", [*evens, 1])
    unit = out_proj.shape[0] // 16
    cuts = [unit * k for k in (0, 2, 6, 8, 10, 16)]
    own_span, early_span, even_span, odd_span, last_span = zip(cuts, cuts[1:])
    groups[0], cache_fast, seen = fetch([queries, jnp.swapaxes(cache, 1, 2)], lengths, positions)

    def attend_some(source, span):
        *outs, part = attend(list(source.values()), cache_fast, seen, out_proj, span)
        return dict(zip(source, outs)), part

    answers, own_part = attend_some({0: groups[0]}, own_span)
    (early_part,) = fetch([(out_proj, early_span)])
    relayed = {}
    for mask in evens:
        relayed[mask + 1] = xor_permute(groups[mask], "ctx", 1)
    even, even_part = attend_some({mask: groups[mask] for mask in [*evens, 1]}, even_span)
    answers |= exchange({0: answers[0], **even}, "ctx", evens)
    answers |= exchange({0: answers[0], **even}, "ctx", [1])
    far, odd_part = attend_some(relayed, odd_span)
    answers |= exchange({0: answers[0], **far}, "ctx", odds)

    gate_fast, up_own, residual, gain = fetch([gate_weight, value_up_weight, residual, norm_gain])
    *far_rows, gain = lax.optimization_barrier((*along[1:], gain))
    near_rows = [up_own, xor_permute(along[0], "seq", 1)]
    far_rows = [part for piece in far_rows for part in (piece, xor_permute(piece, "seq", 1))]
    attended, sums = join_blocks(listed(answers), near_rows, rows, heads, members)
    values = add_values(attended, sums, far_rows, range(2, members), heads)
    last_out, values = lax.optimization_barrier((out_proj, values))
    shared = listed(exchange([values] * members, ("role", "seq")))
    (last_part,) = fetch([(last_out, last_span)])
    product = project_out(shared, [own_part, early_part, even_part, odd_part, last_part])
    up_weight, product = lax.optimization_barrier((up_weight, product))
    terms = listed(exchange([product] * blocks, "ctx"))
    (up_fast,) = fetch([up_weight])

    send, scaled, squares, base = gate_and_up_away(terms, residual, gain, gate_fast, up_fast)
    got = xor_permute(send, "seq", 1)
    keep = gate_and_up_here(scaled, gate_fast, up_fast)
    keep, send = add_core(keep, squares, got)
    down_weight, send = lax.optimization_barrier((down_weight, send))
    (down_fast,) = fetch([down_weight])
    pieces = listed(exchange([send] * roles, "role"))[1:]
    features = norm_gain.shape[0] * members
    hidden = activate(keep, pieces, features)
    other = xor_permute(hidden, "seq", 1)
    own = project_down_own(hidden, down_fast)
    last = exchange(project_down_other(other, down_fast, own), "ctx")
    return finish(base, listed(last))


def solution(mesh):
    placed = (
        P(("groups", "role", "seq"), "ctx", None),
        P(("groups", "role", "seq"), "ctx", None),
        P(("groups", "role", "seq")),
        P(("groups", "role", "seq")),
        P("ctx", ("role", "seq"), None),
        P("ctx", ("role", "seq")),
        P("groups", ("role", "seq")),
        P(("role", "seq")),
        P(("role", "seq"), "ctx"),
        P(("role", "seq"), "ctx"),
        P("ctx", ("role", "seq")),
    )


    return jax.shard_map(
        per_device,
        mesh=mesh,
        in_specs=placed,
        out_specs=P(("groups", "ctx"), ("role", "seq")),
        check_vma=False,
    )
```
